32 devices in a mesh: dp: 8 (over z, y), seq: 4 (over x, core).
Axes of the slice: x: 2, y: 2, z: 4, core: 2. Of those that a mesh axis runs over, the one named last changes fastest.
Arguments:
- token_ids: int32 [24, 1536], P('dp', 'seq'), may hold values from 0 to 4106
- mask_rows: int32 [24, 228], P('dp', 'seq'), may hold values from 0 to 383, as said below
- mask_labels: int32 [24, 228], P('dp', 'seq'), may hold values from 0 to 4106
- mask_counts: int32 [24, 4], P('dp', 'seq'), may hold values from 28 to 57, as said below
- step_count: int32 [1], replicated, may hold values from 1 to 20
- vocab_tables: float32 [2, 1024, 4107], P(None, ('dp', 'seq')), may hold values from -0.1875 to 0.1875
- attention: float32 [1024, 4096], P(('dp', 'seq'))
- feed_in: float32 [1024, 8192], P(('dp', 'seq')), may hold values from -0.1875 to 0.1875
- feed_out: float32 [4096, 1024], P(('dp', 'seq')), may hold values from -0.09375 to 0.09375
- norm_params: float32 [1024, 6], P(('dp', 'seq'))
- first_tables: float32 [2, 1024, 4107], P(None, ('dp', 'seq')), may hold values from -1.9073486e-06 to 1.9073486e-06
- first_attention: float32 [1024, 4096], P(('dp', 'seq')), may hold values from -1.9073486e-06 to 1.9073486e-06
- first_feed_in: float32 [1024, 8192], P(('dp', 'seq')), may hold values from -1.9073486e-06 to 1.9073486e-06
- first_feed_out: float32 [4096, 1024], P(('dp', 'seq')), may hold values from -1.9073486e-06 to 1.9073486e-06
- first_norms: float32 [1024, 6], P(('dp', 'seq')), may hold values from -1.9073486e-06 to 1.9073486e-06
- second_tables: float32 [2, 1024, 4107], P(None, ('dp', 'seq')), may hold values from 3.6267554e-15 to 5.8028086e-14
- second_attention: float32 [1024, 4096], P(('dp', 'seq')), may hold values from 3.6267554e-15 to 5.8028086e-14
- second_feed_in: float32 [1024, 8192], P(('dp', 'seq')), may hold values from 3.6267554e-15 to 5.8028086e-14
- second_feed_out: float32 [4096, 1024], P(('dp', 'seq')), may hold values from 3.6267554e-15 to 5.8028086e-14
- second_norms: float32 [1024, 6], P(('dp', 'seq')), may hold values from 3.6267554e-15 to 5.8028086e-14
- ema_tables: float32 [2, 1024, 4107], P(None, ('dp', 'seq')), may hold values from -0.1875 to 0.1875
- ema_attention: float32 [1024, 4096], P(('dp', 'seq'))
- ema_feed_in: float32 [1024, 8192], P(('dp', 'seq')), may hold values from -0.1875 to 0.1875
- ema_feed_out: float32 [4096, 1024], P(('dp', 'seq')), may hold values from -0.09375 to 0.09375
- ema_norms: float32 [1024, 6], P(('dp', 'seq'))
Outputs:
- masked_loss: float32 [], replicated
- total_norm: float32 [], replicated
- new_tables: float32 [2, 1024, 4107], P(None, ('dp', 'seq'))
- new_attention: float32 [1024, 4096], P(('dp', 'seq'))
- new_feed_in: float32 [1024, 8192], P(('dp', 'seq'))
- new_feed_out: float32 [4096, 1024], P(('dp', 'seq'))
- new_norms: float32 [1024, 6], P(('dp', 'seq'))
- new_first_tables: float32 [2, 1024, 4107], P(None, ('dp', 'seq'))
- new_first_attention: float32 [1024, 4096], P(('dp', 'seq'))
- new_first_feed_in: float32 [1024, 8192], P(('dp', 'seq'))
- new_first_feed_out: float32 [4096, 1024], P(('dp', 'seq'))
- new_first_norms: float32 [1024, 6], P(('dp', 'seq'))
- new_second_tables: float32 [2, 1024, 4107], P(None, ('dp', 'seq'))
- new_second_attention: float32 [1024, 4096], P(('dp', 'seq'))
- new_second_feed_in: float32 [1024, 8192], P(('dp', 'seq'))
- new_second_feed_out: float32 [4096, 1024], P(('dp', 'seq'))
- new_second_norms: float32 [1024, 6], P(('dp', 'seq'))
- new_ema_tables: float32 [2, 1024, 4107], P(None, ('dp', 'seq'))
- new_ema_attention: float32 [1024, 4096], P(('dp', 'seq'))
- new_ema_feed_in: float32 [1024, 8192], P(('dp', 'seq'))
- new_ema_feed_out: float32 [4096, 1024], P(('dp', 'seq'))
- new_ema_norms: float32 [1024, 6], P(('dp', 'seq'))
The draws below stay inside these ranges and needn't reach their ends.
Inputs may be any that keep to these rules, and one draw needn't show every extreme that they name: `mask_rows`: the 57 slots of a window on one shard name distinct positions. `mask_counts`: the live slots of a shard are its first ones; 57 is reached in every draw.
All inputs are finite; a program needn't handle non-finite values.
Results may differ from the reference program's by a relative error of at most 0.012.
The reference program's roundings to bfloat16 on the way (of `mixture` and `hidden`) count: a program that leaves them out, or rounds other values in their place, can miss the bound.
Values may be sent and summed in bfloat16 or wider, within the bound.
A program may use at most 384 MiB of HBM per device.

```python
import math
import jax
import jax.numpy as jnp
from jax import lax

D = 1024
HEADS = 16
HEAD_DIM = 64
FF = 4096
V = 4107
SEQ_LEN = 1536
S_DEV = 384
CAP = 57
SLOTS = 228
WINDOWS = 24
PARAMS = 25194496


def attention_like(key):
    base = jax.random.normal(key, (D, 4 * D), jnp.float32)
    column = jnp.arange(4 * D)[None, :]
    return base * jnp.where(column < 3 * D, D ** (-0.5), (32.0 / D) ** 0.5)


def draw_attention(key, part):
    return attention_like(jax.random.fold_in(key, 11))


def draw_ema_attention(key, part):
    return attention_like(jax.random.fold_in(key, 12))


def norms_like(key):
    base = jax.random.normal(key, (D, 6), jnp.float32)
    column = jnp.arange(6)[None, :]
    return jnp.where(column % 2 == 0, 1.0 + 0.15 * base, 0.3 * base)


def draw_norm_params(key, part):
    return norms_like(jax.random.fold_in(key, 13))


def draw_ema_norms(key, part):
    return norms_like(jax.random.fold_in(key, 14))


def draw_mask_rows(key, part):
    shards = SLOTS // CAP
    scores = jax.random.randint(jax.random.fold_in(key, 21), (WINDOWS, shards, S_DEV), 0, 2 ** 19)
    scores = scores * S_DEV + jnp.arange(S_DEV, dtype=jnp.int32)[None, None, :]
    order = jnp.argsort(scores, axis=-1)
    return order[:, :, :CAP].reshape(WINDOWS, SLOTS).astype(jnp.int32)


def draw_mask_counts(key, part):
    shards = SLOTS // CAP
    counts = jax.random.randint(jax.random.fold_in(key, 22), (WINDOWS, shards), max(1, CAP // 2), CAP + 1)
    return counts.at[0, 0].set(CAP).astype(jnp.int32)


def place_ends(array, rng, least, largest):
    dims = array.shape
    place = [jax.random.randint(jax.random.fold_in(rng, axis), (), 0, dims[axis]) for axis in range(len(dims))]
    array = array.at[tuple(place)].set(least)
    longest = dims.index(max(dims))
    place[longest] = (place[longest] + 1) % dims[longest]
    return array.at[tuple(place)].set(largest)


def steps_of(rng, dims, cuts, least, top_value):
    factor_of, own = 1.0, jax.random.fold_in(rng, 6)
    for dim, shards_of in cuts:
        steps = jnp.exp(jax.random.uniform(jax.random.fold_in(own, dim), (shards_of,), jnp.float32, least / len(cuts), top_value / len(cuts)))
        factor_of = factor_of * jnp.repeat(steps, dims[dim] // shards_of).reshape([-1 if axis == dim else 1 for axis in range(len(dims))])
    return factor_of


def scatter_about(stream_key, shape, scale, most, pieces=(), kind=jnp.bfloat16):
    level = steps_of(stream_key, shape, pieces, -0.22, 0.18) if pieces else 1.0
    result = jax.random.normal(stream_key, shape, jnp.float32) * scale * level
    return jnp.minimum(jnp.maximum(result, -most), most).astype(kind)


def setup_inputs(seed: int = 0) -> dict:
    splits = jax.random.split(jax.random.key(seed), 26)
    return {
        "token_ids": place_ends(jax.random.randint(splits[0], (WINDOWS, SEQ_LEN), 0, V), jax.random.fold_in(splits[0], 1), 0, V - 1).astype(jnp.int32),
        "mask_rows": draw_mask_rows(jax.random.fold_in(splits[25], 71), 0),
        "mask_labels": place_ends(jax.random.randint(splits[2], (WINDOWS, SLOTS), 0, V), jax.random.fold_in(splits[2], 1), 0, V - 1).astype(jnp.int32),
        "mask_counts": draw_mask_counts(jax.random.fold_in(splits[25], 71), 0),
        "step_count": jax.random.randint(splits[4], (1,), 1, 21).astype(jnp.int32),
        "vocab_tables": scatter_about(splits[5], (2, D, V), D ** -0.5, 0.1875, ((1, 32),), jnp.float32),
        "attention": draw_attention(jax.random.fold_in(splits[25], 71), 0),
        "feed_in": scatter_about(splits[7], (D, 2 * FF), D ** -0.5, 0.1875, ((0, 32),), jnp.float32),
        "feed_out": scatter_about(splits[8], (FF, D), FF ** -0.5, 0.09375, ((0, 32),), jnp.float32),
        "norm_params": draw_norm_params(jax.random.fold_in(splits[25], 71), 0),
        "first_tables": scatter_about(splits[10], (2, D, V), (0.111 * (SLOTS * WINDOWS * PARAMS) ** -0.5), 1.9073486328125e-06, ((1, 32),), jnp.float32),
        "first_attention": scatter_about(splits[11], (D, 4 * D), (0.111 * (SLOTS * WINDOWS * PARAMS) ** -0.5), 1.9073486328125e-06, ((0, 32),), jnp.float32),
        "first_feed_in": scatter_about(splits[12], (D, 2 * FF), (0.111 * (SLOTS * WINDOWS * PARAMS) ** -0.5), 1.9073486328125e-06, ((0, 32),), jnp.float32),
        "first_feed_out": scatter_about(splits[13], (FF, D), (0.111 * (SLOTS * WINDOWS * PARAMS) ** -0.5), 1.9073486328125e-06, ((0, 32),), jnp.float32),
        "first_norms": scatter_about(splits[14], (D, 6), (0.111 * (SLOTS * WINDOWS * PARAMS) ** -0.5), 1.9073486328125e-06, ((0, 32),), jnp.float32),
        "second_tables": jnp.clip(jnp.exp(math.log(5.802808591710146e-14) - 2.7725887 * jax.random.uniform(splits[15], (2, D, V), jnp.float32) ** steps_of(splits[15], (2, D, V), ((1, 32),), -0.2, 0.2)), 3.626755369818841e-15, 5.802808591710146e-14),
        "second_attention": jnp.clip(jnp.exp(math.log(5.802808591710146e-14) - 2.7725887 * jax.random.uniform(splits[16], (D, 4 * D), jnp.float32) ** steps_of(splits[16], (D, 4 * D), ((0, 32),), -0.2, 0.2)), 3.626755369818841e-15, 5.802808591710146e-14),
        "second_feed_in": jnp.clip(jnp.exp(math.log(5.802808591710146e-14) - 2.7725887 * jax.random.uniform(splits[17], (D, 2 * FF), jnp.float32) ** steps_of(splits[17], (D, 2 * FF), ((0, 32),), -0.2, 0.2)), 3.626755369818841e-15, 5.802808591710146e-14),
        "second_feed_out": jnp.clip(jnp.exp(math.log(5.802808591710146e-14) - 2.7725887 * jax.random.uniform(splits[18], (FF, D), jnp.float32) ** steps_of(splits[18], (FF, D), ((0, 32),), -0.2, 0.2)), 3.626755369818841e-15, 5.802808591710146e-14),
        "second_norms": jnp.clip(jnp.exp(math.log(5.802808591710146e-14) - 2.7725887 * jax.random.uniform(splits[19], (D, 6), jnp.float32) ** steps_of(splits[19], (D, 6), ((0, 32),), -0.2, 0.2)), 3.626755369818841e-15, 5.802808591710146e-14),
        "ema_tables": scatter_about(splits[20], (2, D, V), D ** -0.5, 0.1875, ((1, 32),), jnp.float32),
        "ema_attention": draw_ema_attention(jax.random.fold_in(splits[25], 71), 0),
        "ema_feed_in": scatter_about(splits[22], (D, 2 * FF), D ** -0.5, 0.1875, ((0, 32),), jnp.float32),
        "ema_feed_out": scatter_about(splits[23], (FF, D), FF ** -0.5, 0.09375, ((0, 32),), jnp.float32),
        "ema_norms": draw_ema_norms(jax.random.fold_in(splits[25], 71), 0),
    }


@jax.custom_vjp
def low(v):
    return lax.optimization_barrier(v.astype(jnp.bfloat16)).astype(jnp.float32)

@jax.custom_vjp
def low_back(v):
    return v

def low_keep(v):
    return (low(v), None)

def low_pass(kept, grad):
    return (grad,)

def back_keep(v):
    return (v, None)

def back_low(kept, grad):
    return (low(grad),)
low.defvjp(low_keep, low_pass)
low_back.defvjp(back_keep, back_low)
beta_one = 0.9
beta_two = 0.999
adam_eps = 1e-08
weight_decay = 0.01
learn_rate = 0.02
norm_rate = 0.2
ema_decay = 0.7
norm_eps = 1e-05
highest = lax.Precision.HIGHEST

def matmul(left, right):
    return jnp.dot(left, right, precision=highest, preferred_element_type=jnp.float32)

def layer_norm(values, gain, shift):
    centre = values - lax.optimization_barrier(jnp.mean(values, axis=-1, keepdims=True))
    spread = lax.optimization_barrier(jnp.mean(centre * centre, axis=-1, keepdims=True))
    return centre * lax.rsqrt(spread + norm_eps) * gain + shift

def rope_tables(positions):
    half = HEAD_DIM // 2
    inverse = 10000.0 ** (-jnp.arange(half).astype(jnp.float32) / half)
    angles = positions.astype(jnp.float32)[:, None] * inverse[None, :]
    angles = jnp.concatenate([angles, angles], axis=-1)[:, None, :]
    return (jnp.cos(angles), jnp.sin(angles))

def rotate(values, cosines, sines):
    half = values.shape[-1] // 2
    turned = jnp.concatenate([-values[..., half:], values[..., :half]], axis=-1)
    return values * cosines + turned * sines

def window_loss(params, window_ids, rows, labels, live, cosines, sines):
    tables, attention, feed_in, feed_out, norms = params
    factor = 1.0 / math.sqrt(HEAD_DIM)
    embedded = jnp.take(tables[0], window_ids, axis=1).T
    normed_one = layer_norm(embedded, norms[:, 0], norms[:, 1])
    projected = low_back(matmul(low(normed_one), attention[:, :3 * D]))
    queries = low(rotate(projected[:, :D].reshape(SEQ_LEN, HEADS, HEAD_DIM), cosines, sines))
    key_heads = low(rotate(projected[:, D:2 * D].reshape(SEQ_LEN, HEADS, HEAD_DIM), cosines, sines))
    value_heads = low(projected[:, 2 * D:].reshape(SEQ_LEN, HEADS, HEAD_DIM))
    scores = low_back(jnp.einsum('qhd,khd->hqk', queries, key_heads, precision=highest) * factor)
    chances = jax.nn.softmax(scores, axis=-1)
    mixture = jnp.einsum('hqk,khd->qhd', low(chances), value_heads, precision=highest)
    mixture = low(low_back(mixture)).reshape(SEQ_LEN, D)
    after_attn = embedded + low_back(matmul(mixture, attention[:, 3 * D:]))
    normed_two = layer_norm(after_attn, norms[:, 2], norms[:, 3])
    gate_up = low_back(matmul(low(normed_two), feed_in))
    hidden = low(jax.nn.silu(gate_up[:, :FF]) * gate_up[:, FF:])
    after_feed = after_attn + low_back(matmul(hidden, feed_out))
    selected = after_feed[rows]
    normed_final = layer_norm(selected, norms[:, 4], norms[:, 5])
    logits = low_back(matmul(low(normed_final), tables[1]))
    log_total = jax.nn.logsumexp(logits, axis=-1)
    picked = jnp.take_along_axis(logits, labels[:, None], axis=-1)[:, 0]
    return jnp.sum(live * (log_total - picked))

def reference(token_ids, mask_rows, mask_labels, mask_counts, step_count, vocab_tables, attention, feed_in, feed_out, norm_params, first_tables, first_attention, first_feed_in, first_feed_out, first_norms, second_tables, second_attention, second_feed_in, second_feed_out, second_norms, ema_tables, ema_attention, ema_feed_in, ema_feed_out, ema_norms):
    master = (vocab_tables, attention, feed_in, feed_out, norm_params)
    firsts = (first_tables, first_attention, first_feed_in, first_feed_out, first_norms)
    seconds = (second_tables, second_attention, second_feed_in, second_feed_out, second_norms)
    averages = (ema_tables, ema_attention, ema_feed_in, ema_feed_out, ema_norms)
    group_rates = (learn_rate, learn_rate, learn_rate, learn_rate, norm_rate)
    slot = jnp.arange(SLOTS).astype(jnp.int32)
    bound = jnp.repeat(mask_counts, CAP, axis=1)
    live = (slot[None, :] % CAP < bound).astype(jnp.float32)
    rows = (slot // CAP * S_DEV)[None, :] + mask_rows.astype(jnp.int32)
    count = jnp.sum(mask_counts).astype(jnp.float32)
    cosines, sines = rope_tables(jnp.arange(SEQ_LEN).astype(jnp.int32))

    def full_loss(params):
        rounded = tuple((low(item) for item in params))

        def accumulate(carry, data):
            window_ids, window_rows, labels, window_live = data
            term = jax.checkpoint(window_loss)(rounded, window_ids, window_rows, labels, window_live, cosines, sines)
            return (carry + term, None)
        summed, unused = lax.scan(accumulate, jnp.zeros((), jnp.float32), (token_ids, rows, mask_labels, live))
        return summed / count
    masked_loss, pull = jax.vjp(full_loss, master)
    grads = pull(jnp.ones((), jnp.float32))[0]
    squares = jnp.zeros((), jnp.float32)
    for grad in grads:
        squares = squares + jnp.sum(grad * grad)
    total_norm = jnp.sqrt(squares)
    limit = 1.0 / math.sqrt(SLOTS * WINDOWS)
    clip = jnp.minimum(1.0, limit / (total_norm + 1e-06))
    steps = step_count[0].astype(jnp.float32)
    fix_one = 1.0 - beta_one ** steps
    fix_two = 1.0 - beta_two ** steps
    weights_new, firsts_new, seconds_new, averages_new = ([], [], [], [])
    for weight, grad, first, second, average, step_rate in zip(master, grads, firsts, seconds, averages, group_rates):
        scaled = grad * clip
        first_next = beta_one * first + (1.0 - beta_one) * scaled
        second_next = beta_two * second + (1.0 - beta_two) * scaled * scaled
        update = first_next / fix_one / (jnp.sqrt(second_next / fix_two) + adam_eps) + weight_decay * weight
        weight_next = weight - step_rate * update
        weights_new.append(weight_next)
        firsts_new.append(first_next)
        seconds_new.append(second_next)
        averages_new.append(ema_decay * average + (1.0 - ema_decay) * weight_next)
    return (masked_loss, total_norm, weights_new[0], weights_new[1], weights_new[2], weights_new[3], weights_new[4], firsts_new[0], firsts_new[1], firsts_new[2], firsts_new[3], firsts_new[4], seconds_new[0], seconds_new[1], seconds_new[2], seconds_new[3], seconds_new[4], averages_new[0], averages_new[1], averages_new[2], averages_new[3], averages_new[4])
```

```python
import functools
import jax, jax.numpy as jnp
from jax import lax
from jax.experimental import pallas as pl
from jax.experimental.pallas import tpu as pltpu
HEAD_DIM=64
PAIR=128
MB=1<<20

def dims(a,b): return (((a,),(b,)),((),()))

def low_half(rows):
    lane = lax.broadcasted_iota(jnp.int32,(rows,PAIR),1)
    return lane % HEAD_DIM < HEAD_DIM//2

def turn(x, cosines, sines):
    low = low_half(x.shape[0])
    up = pltpu.roll(x, PAIR-HEAD_DIM//2, 1)
    down = pltpu.roll(x, HEAD_DIM//2, 1)
    return x*cosines + jnp.where(low,-up,down)*sines

def turn_back(g, cosines, sines):
    low = low_half(g.shape[0])
    up = pltpu.roll(g, PAIR-HEAD_DIM//2, 1)
    down = pltpu.roll(g, HEAD_DIM//2, 1)
    return g*cosines + jnp.where(low,up,-down)*sines

def head_mask(head):
    lane = lax.broadcasted_iota(jnp.int32,(1,PAIR),1)
    return (lane//HEAD_DIM==head).astype(jnp.float32).astype(jnp.bfloat16)

def forward_kernel(win_ref, q_ref, kv_ref, mix_ref, total_ref):
    queries = q_ref[...]
    keys = kv_ref[:, :PAIR]
    values = kv_ref[:, PAIR:]
    parts=[]
    for head in range(2):
        scores = lax.dot_general(keys, queries*head_mask(head), dims(1,1), preferred_element_type=jnp.float32)
        top = jnp.max(scores, axis=0, keepdims=True)
        chances = jnp.exp(scores-top)
        total = jnp.sum(chances, axis=0, keepdims=True)
        weights = (chances*(1.0/total)).astype(jnp.bfloat16)
        mixed = lax.dot_general(values, weights, dims(0,0), preferred_element_type=jnp.float32)
        parts.append(mixed[head*HEAD_DIM:(head+1)*HEAD_DIM])
        total_ref[0,0,head:head+1,:] = top+jnp.log(total)
    mix_ref[...] = jnp.concatenate(parts,axis=0).T.astype(jnp.bfloat16)

def attend_forward(win, queries, key_values, span, length):
    tokens,width = queries.shape
    pairs = width//PAIR
    blocks = tokens//span
    return pl.pallas_call(
        forward_kernel,
        grid_spec=pltpu.PrefetchScalarGridSpec(
            num_scalar_prefetch=1, grid=(pairs,blocks),
            in_specs=[pl.BlockSpec((span,PAIR),lambda p,b,w:(b,p)),
                      pl.BlockSpec((length,2*PAIR),lambda p,b,w:(w[b],p))],
            out_specs=[pl.BlockSpec((span,PAIR),lambda p,b,w:(b,p)),
                       pl.BlockSpec((1,1,8,span),lambda p,b,w:(p,b,0,0))]),
        out_shape=[jax.ShapeDtypeStruct((tokens,width),jnp.bfloat16),
                   jax.ShapeDtypeStruct((pairs,blocks,8,span),jnp.float32)],
        compiler_params=pltpu.CompilerParams(vmem_limit_bytes=56*MB),
        cost_estimate=pl.CostEstimate(flops=4*tokens*length*width,bytes_accessed=16*MB,transcendentals=tokens*length*width//HEAD_DIM),
        name="attend_forward",
    )(win,queries,key_values)

def backward_kernel(win_ref, q_ref, kv_ref, grad_ref, total_ref, cosq_ref, sinq_ref, cosk_ref, sink_ref, gq_ref, gkv_ref, acc_ref):
    block = pl.program_id(1)
    length = kv_ref.shape[0]
    @pl.when(block==0)
    def _():
        acc_ref[...] = jnp.zeros_like(acc_ref)
    queries = q_ref[...]
    keys = kv_ref[:, :PAIR]
    values = kv_ref[:, PAIR:]
    grads = grad_ref[...]
    start = pl.multiple_of(win_ref[block]*length, length)
    parts=[]
    grad_keys = None
    for head in range(2):
        mask = head_mask(head)
        queries_h = queries*mask
        grads_h = grads*mask
        scores = lax.dot_general(keys, queries_h, dims(1,1), preferred_element_type=jnp.float32)
        chances = jnp.exp(scores-total_ref[0,0,head:head+1,:])
        grad_chances = lax.dot_general(values, grads_h, dims(1,1), preferred_element_type=jnp.float32)
        both = chances*grad_chances
        inner = jnp.sum(both,axis=0,keepdims=True)
        grad_scores = (both-chances*inner).astype(jnp.bfloat16)
        grad_values_h = lax.dot_general(chances.astype(jnp.bfloat16), grads_h, dims(1,0), preferred_element_type=jnp.float32)
        grad_keys_h = lax.dot_general(grad_scores, queries_h, dims(1,0), preferred_element_type=jnp.float32)
        acc_ref[pl.ds(start,length),:PAIR] += grad_keys_h
        acc_ref[pl.ds(start,length),PAIR:] += grad_values_h
        grad_q = lax.dot_general(keys, grad_scores, dims(0,0), preferred_element_type=jnp.float32)
        parts.append(grad_q[head*HEAD_DIM:(head+1)*HEAD_DIM])
    grad_q = jnp.concatenate(parts,axis=0).T * (HEAD_DIM**-0.5)
    gq_ref[...] = turn_back(grad_q,cosq_ref[...],sinq_ref[...]).astype(jnp.bfloat16)
    @pl.when(block==pl.num_programs(1)-1)
    def _():
        for w in range(acc_ref.shape[0]//length):
            rows = pl.ds(w*length,length)
            gkv_ref[rows,:PAIR] = turn_back(acc_ref[rows,:PAIR],cosk_ref[...],sink_ref[...]).astype(jnp.bfloat16)
            gkv_ref[rows,PAIR:] = acc_ref[rows,PAIR:].astype(jnp.bfloat16)

def attend_backward(win, queries, key_values, grads, totals, rope_q, rope_k, span, length):
    tokens,width = queries.shape
    pairs = width//PAIR
    blocks = tokens//span
    all_rows = key_values.shape[0]
    return pl.pallas_call(
        backward_kernel,
        grid_spec=pltpu.PrefetchScalarGridSpec(
            num_scalar_prefetch=1, grid=(pairs,blocks),
            in_specs=[pl.BlockSpec((span,PAIR),lambda p,b,w:(b,p)),
                      pl.BlockSpec((length,2*PAIR),lambda p,b,w:(w[b],p)),
                      pl.BlockSpec((span,PAIR),lambda p,b,w:(b,p)),
                      pl.BlockSpec((1,1,8,span),lambda p,b,w:(p,b,0,0)),
                      pl.BlockSpec((span,PAIR),lambda p,b,w:(b,0)),
                      pl.BlockSpec((span,PAIR),lambda p,b,w:(b,0)),
                      pl.BlockSpec((length,PAIR),lambda p,b,w:(0,0)),
                      pl.BlockSpec((length,PAIR),lambda p,b,w:(0,0))],
            out_specs=[pl.BlockSpec((span,PAIR),lambda p,b,w:(b,p)),
                       pl.BlockSpec((all_rows,2*PAIR),lambda p,b,w:(0,p))],
            scratch_shapes=[pltpu.VMEM((all_rows,2*PAIR),jnp.float32)]),
        out_shape=[jax.ShapeDtypeStruct((tokens,width),jnp.bfloat16),
                   jax.ShapeDtypeStruct((all_rows,2*width),jnp.bfloat16)],
        compiler_params=pltpu.CompilerParams(vmem_limit_bytes=60*MB),
        cost_estimate=pl.CostEstimate(flops=10*tokens*length*width,bytes_accessed=32*MB,transcendentals=tokens*length*width//HEAD_DIM),
        name="attend_backward",
    )(win,queries,key_values,grads,totals,*rope_q,*rope_k)


from jax.sharding import PartitionSpec as P

AXES = ("dp", "seq")
beta_one = 0.9
beta_two = 0.999
adam_eps = 1e-08
weight_decay = 0.01
learn_rate = 0.02
norm_rate = 0.2
ema_decay = 0.7
norm_eps = 1e-05


def project_kernel(roped, x_ref, w_ref, cos_ref, sin_ref, out_ref):
    product = jnp.dot(x_ref[...], w_ref[...], preferred_element_type=jnp.float32)
    for part in range(product.shape[1] // PAIR):
        piece = product[:, part * PAIR : (part + 1) * PAIR]
        if roped == "all":
            piece = turn(piece, cos_ref[...], sin_ref[...]).astype(jnp.bfloat16)
            piece = piece * jnp.bfloat16(HEAD_DIM**-0.5)
        elif part % 2 == 0:
            piece = turn(piece, cos_ref[...], sin_ref[...])
        out_ref[:, part * PAIR : (part + 1) * PAIR] = piece.astype(jnp.bfloat16)


def project(x, weights, first_column, columns, rope, tile, roped):
    tokens, width = x.shape
    wide = 512
    repeat = rope[0].shape[0] // tile
    return pl.pallas_call(
        functools.partial(project_kernel, roped),
        grid=(columns // wide, tokens // tile),
        in_specs=[
            pl.BlockSpec((tile, width), lambda n, m: (m, 0)),
            pl.BlockSpec((width, wide), lambda n, m: (0, n + first_column // wide)),
            pl.BlockSpec((tile, PAIR), lambda n, m: (lax.rem(m, repeat), 0)),
            pl.BlockSpec((tile, PAIR), lambda n, m: (lax.rem(m, repeat), 0)),
        ],
        out_specs=pl.BlockSpec((tile, wide), lambda n, m: (m, n)),
        out_shape=jax.ShapeDtypeStruct((tokens, columns), jnp.bfloat16),
        compiler_params=pltpu.CompilerParams(vmem_limit_bytes=40 * MB),
        cost_estimate=pl.CostEstimate(
            flops=2 * tokens * width * columns,
            bytes_accessed=2 * (tokens * width + width * columns + tokens * columns),
            transcendentals=0,
        ),
        name="project",
    )(x, weights, *rope)


def rope_tables(positions):
    half = HEAD_DIM // 2
    inverse = 10000.0 ** (-jnp.arange(half).astype(jnp.float32) / half)
    angles = positions.astype(jnp.float32)[:, None] * inverse[None, :]
    copies = PAIR // half
    return (jnp.tile(jnp.cos(angles), (1, copies)), jnp.tile(jnp.sin(angles), (1, copies)))


def norm_forward(values, gain, shift):
    centre = values - jnp.mean(values, axis=-1, keepdims=True)
    spread = jnp.mean(centre * centre, axis=-1, keepdims=True)
    scale = lax.rsqrt(spread + norm_eps)
    unit = centre * scale
    return (unit * gain + shift).astype(jnp.bfloat16), unit, scale


def norm_backward(grad, unit, scale, gain):
    grad_gain = jnp.sum(grad * unit, axis=0)
    grad_shift = jnp.sum(grad, axis=0)
    scaled = grad * gain
    inner = jnp.mean(scaled * unit, axis=-1, keepdims=True)
    outer = jnp.mean(scaled, axis=-1, keepdims=True)
    return scale * (scaled - outer - unit * inner), grad_gain, grad_shift


def product(left, right, left_dim=1, right_dim=0, precision=None):
    return lax.dot_general(
        left, right, dims(left_dim, right_dim), precision=precision,
        preferred_element_type=jnp.float32,
    )


def pair_columns(weights):
    rows, columns = weights.shape
    width = columns // 2
    return weights.reshape(rows, 2, width // PAIR, PAIR).transpose(0, 2, 1, 3).reshape(rows, columns)


def unpair_columns(weights):
    rows, columns = weights.shape
    width = columns // 2
    return weights.reshape(rows, width // PAIR, 2, PAIR).transpose(0, 2, 1, 3).reshape(rows, columns)


def scatter_sum(grads):
    shards, groups = lax.axis_size("seq"), lax.axis_size("dp")
    total, columns = grads.shape
    rows = total // (shards * groups)
    blocks = grads.reshape(groups, shards, rows, columns).transpose(1, 0, 2, 3)
    part = lax.psum_scatter(blocks.reshape(total, columns), "seq", scatter_dimension=0, tiled=True)
    return lax.psum_scatter(part, "dp", scatter_dimension=0, tiled=True)


def on_device(
    token_ids,
    mask_rows,
    mask_labels,
    mask_counts,
    step_count,
    vocab_tables,
    attention,
    feed_in,
    feed_out,
    norm_params,
    first_tables,
    first_attention,
    first_feed_in,
    first_feed_out,
    first_norms,
    second_tables,
    second_attention,
    second_feed_in,
    second_feed_out,
    second_norms,
    ema_tables,
    ema_attention,
    ema_feed_in,
    ema_feed_out,
    ema_norms,
):
    master = (vocab_tables, attention, feed_in, feed_out, norm_params)
    firsts = (first_tables, first_attention, first_feed_in, first_feed_out, first_norms)
    seconds = (second_tables, second_attention, second_feed_in, second_feed_out, second_norms)
    averages = (ema_tables, ema_attention, ema_feed_in, ema_feed_out, ema_norms)
    group_rates = (learn_rate, learn_rate, learn_rate, learn_rate, norm_rate)
    low = jnp.bfloat16

    shards = lax.axis_size("seq")
    devices = shards * lax.axis_size("dp")
    windows, span = token_ids.shape
    slots = mask_rows.shape[1]
    vocab = vocab_tables.shape[2]
    padded = vocab + -vocab % PAIR
    rows, columns = attention.shape
    width = columns // 4
    hidden_width = feed_in.shape[1] // 2
    folds = feed_out.shape[0] // rows
    length = span * shards
    spot = lax.axis_index("seq")

    tables_sent = jnp.pad(vocab_tables, ((0, 0), (0, 0), (0, padded - vocab)))
    early_sent = jnp.concatenate(
        [
            attention[:, :width],
            pair_columns(attention[:, width : 3 * width]),
            attention[:, 3 * width :],
            tables_sent[0],
        ],
        axis=1,
    ).astype(low)
    in_sent = feed_in.reshape(rows, 2, hidden_width // folds, folds).transpose(0, 1, 3, 2)
    late_sent = jnp.concatenate(
        [
            in_sent.reshape(rows, 2 * hidden_width),
            feed_out.reshape(rows, folds * width),
            tables_sent[1],
        ],
        axis=1,
    ).astype(low)
    early = lax.all_gather(early_sent, AXES, axis=0, tiled=True)
    late = lax.all_gather(late_sent, AXES, axis=0, tiled=True)
    table_w = early[:, columns:]
    out_w = early[:, 3 * width : columns]
    feed_w = late[:, : 2 * hidden_width]
    head_w = late[:, 2 * hidden_width + folds * width :]

    small = jnp.concatenate(
        [
            token_ids.reshape(-1).astype(jnp.float32),
            mask_rows.reshape(-1).astype(jnp.float32),
            mask_labels.reshape(-1).astype(jnp.float32),
            mask_counts.reshape(-1).astype(jnp.float32),
            norm_params.astype(low).astype(jnp.float32).reshape(-1),
        ]
    )
    small = jnp.pad(small, (0, -small.shape[0] % PAIR)).reshape(1, -1)
    small_all = lax.all_gather(small, AXES, axis=0, tiled=True)
    cuts = [windows * span, windows * slots, windows * slots, windows]
    marks = [sum(cuts[:i]) for i in range(len(cuts) + 1)]
    gains = small_all[:, marks[4] : marks[4] + rows * 6].reshape(devices * rows, 6)
    count = jnp.sum(small_all[:, marks[3] : marks[4]])
    group = lax.dynamic_slice_in_dim(small_all, lax.axis_index("dp") * shards, shards, axis=0)

    def in_order(first, last):
        piece = group[:, first:last].reshape(shards, windows, -1)
        return piece.transpose(1, 0, 2).reshape(windows * shards, -1)

    ids = in_order(marks[0], marks[1]).astype(jnp.int32)
    block = spot * windows + jnp.arange(windows, dtype=jnp.int32)

    def mine(first, last):
        return lax.dynamic_slice_in_dim(in_order(first, last), spot * windows, windows, axis=0)

    own_rows = mine(marks[1], marks[2]).astype(jnp.int32)
    own_labels = mine(marks[2], marks[3]).astype(jnp.int32).reshape(-1)
    own_counts = mine(marks[3], marks[4])
    live = (jnp.arange(slots, dtype=jnp.float32)[None, :] < own_counts).astype(jnp.float32)
    live = live.reshape(-1)

    base = jnp.minimum(spot * windows // shards, windows - 2)
    wins = block // shards - base
    offset = (spot * windows - base * shards) * span
    ids_two = lax.dynamic_slice_in_dim(ids, base * shards, 2 * shards, axis=0).reshape(-1)
    positions = ((block % shards)[:, None] * span + jnp.arange(span, dtype=jnp.int32)).reshape(-1)
    rope_q = rope_tables(positions)
    rope_k = rope_tables(jnp.arange(length, dtype=jnp.int32))
    tokens = windows * span

    def own(values):
        return lax.dynamic_slice_in_dim(values, offset, tokens, axis=0)

    onehot = (ids_two[:, None] == jnp.arange(padded, dtype=jnp.int32)[None, :]).astype(low)
    onehot = lax.optimization_barrier(onehot)
    embedded_two = product(onehot, table_w, 1, 1)
    normed_one, unit_one, scale_one = norm_forward(embedded_two, gains[:, 0], gains[:, 1])
    normed_own = own(normed_one)
    queries = project(normed_own, early, 0, width, rope_q, span, "all")
    key_values = project(normed_one, early, width, 2 * width, rope_k, 512 if length % 512 == 0 else span, "half")
    mixture, totals = attend_forward(wins, queries, key_values, span, length)
    after_attn = own(embedded_two) + product(mixture, out_w)

    normed_two, unit_two, scale_two = norm_forward(after_attn, gains[:, 2], gains[:, 3])
    gate_up = product(normed_two, feed_w)
    gate, up = gate_up[:, :hidden_width], gate_up[:, hidden_width:]
    sigmoid = jax.nn.sigmoid(gate)
    hidden = (gate * sigmoid * up).astype(low)
    after_feed = after_attn
    for fold in range(folds):
        down = late[:, 2 * hidden_width + fold * width : 2 * hidden_width + (fold + 1) * width]
        after_feed = after_feed + product(hidden[:, fold * width : (fold + 1) * width], down)

    pick = (own_rows[:, :, None] == jnp.arange(span, dtype=jnp.int32)).astype(jnp.float32)
    selected = jnp.einsum(
        "wsp,wpd->wsd", pick, after_feed.reshape(windows, span, width),
        precision=lax.Precision.HIGHEST, preferred_element_type=jnp.float32,
    ).reshape(windows * slots, width)
    normed_final, unit_final, scale_final = norm_forward(selected, gains[:, 4], gains[:, 5])
    column = jnp.arange(padded, dtype=jnp.int32)[None, :]
    logits = jnp.where(column < vocab, product(normed_final, head_w), -jnp.inf)
    log_total = jax.nn.logsumexp(logits, axis=-1)
    wanted = own_labels[:, None] == column
    picked = jnp.sum(jnp.where(wanted, logits, 0.0), axis=-1)
    loss_part = jnp.sum(live * (log_total - picked))

    grad_logits = (
        (jnp.exp(logits - log_total[:, None]) - wanted.astype(jnp.float32)) * (live / count)[:, None]
    ).astype(low)
    grad_head = product(normed_final, grad_logits, 0, 0)
    grad_selected, grad_gain_final, grad_shift_final = norm_backward(
        product(grad_logits, head_w, 1, 1), unit_final, scale_final, gains[:, 4]
    )
    grad_after_feed = jnp.einsum(
        "wsp,wsd->wpd", pick, grad_selected.reshape(windows, slots, width),
        precision=lax.Precision.HIGHEST, preferred_element_type=jnp.float32,
    ).reshape(tokens, width)
    rounded_feed = grad_after_feed.astype(low)
    grad_down = []
    for fold in range(folds):
        grad_down.append(product(hidden[:, fold * width : (fold + 1) * width], rounded_feed, 0, 0))
    down_grads = jnp.concatenate([item.astype(low) for item in grad_down + [grad_head]], axis=1)
    rounded_feed, down_grads = lax.optimization_barrier((rounded_feed, down_grads))
    down_own = scatter_sum(down_grads)
    grad_hidden = []
    for fold in range(folds):
        down = late[:, 2 * hidden_width + fold * width : 2 * hidden_width + (fold + 1) * width]
        grad_hidden.append(product(rounded_feed, down, 1, 1))
    grad_hidden = jnp.concatenate(grad_hidden, axis=1)
    grad_gate = grad_hidden * up * (sigmoid * (1.0 + gate * (1.0 - sigmoid)))
    grad_up = grad_hidden * (gate * sigmoid)
    grad_gate_up = jnp.concatenate([grad_gate, grad_up], axis=1).astype(low)
    in_grads = product(normed_two, grad_gate_up, 0, 0).astype(low)
    grad_gate_up, in_grads = lax.optimization_barrier((grad_gate_up, in_grads))
    in_own = scatter_sum(in_grads)

    grad_inner, grad_gain_two, grad_shift_two = norm_backward(
        product(grad_gate_up, feed_w, 1, 1), unit_two, scale_two, gains[:, 2]
    )
    grad_after_attn = grad_after_feed + grad_inner
    rounded_attn = grad_after_attn.astype(low)
    grad_output = product(mixture, rounded_attn, 0, 0)
    grad_mixture = product(rounded_attn, out_w, 1, 1).astype(low)
    grad_queries, grad_pairs = attend_backward(
        wins, queries, key_values, grad_mixture, totals, rope_q, rope_k, span, length
    )
    grad_query_w = product(normed_own, grad_queries, 0, 0)
    grad_pair_w = product(normed_one, grad_pairs, 0, 0)
    grad_normed = product(grad_pairs, early[:, width : 3 * width], 1, 1)
    grad_normed = lax.dynamic_update_slice_in_dim(
        grad_normed, own(grad_normed) + product(grad_queries, early[:, :width], 1, 1), offset, axis=0
    )
    grad_embedded, grad_gain_one, grad_shift_one = norm_backward(
        grad_normed, unit_one, scale_one, gains[:, 0]
    )
    grad_embedded = lax.dynamic_update_slice_in_dim(
        grad_embedded, own(grad_embedded) + grad_after_attn, offset, axis=0
    )
    grad_embed = product(grad_embedded.astype(low), onehot, 0, 0)
    grad_norms = jnp.stack(
        [
            grad_gain_one,
            grad_shift_one,
            grad_gain_two,
            grad_shift_two,
            grad_gain_final,
            grad_shift_final,
        ],
        axis=1,
    )
    norms_own = lax.psum_scatter(grad_norms, AXES, scatter_dimension=0, tiled=True)
    early_grads = jnp.concatenate(
        [item.astype(low) for item in (grad_query_w, grad_pair_w, grad_output, grad_embed)], axis=1
    )
    early_own = scatter_sum(early_grads).astype(jnp.float32)
    down_own = down_own.astype(jnp.float32)
    in_own = in_own.astype(jnp.float32).reshape(rows, 2, folds, hidden_width // folds)
    grads = (
        jnp.stack(
            [
                early_own[:, columns : columns + vocab],
                down_own[:, folds * width : folds * width + vocab],
            ],
            axis=0,
        ),
        jnp.concatenate(
            [
                early_own[:, :width],
                unpair_columns(early_own[:, width : 3 * width]),
                early_own[:, 3 * width : columns],
            ],
            axis=1,
        ),
        in_own.transpose(0, 1, 3, 2).reshape(rows, 2 * hidden_width),
        down_own[:, : folds * width].reshape(rows * folds, width),
        norms_own,
    )
    squares = jnp.zeros((), jnp.float32)
    for grad in grads:
        squares = squares + jnp.sum(grad * grad)
    squares_all, loss_all = lax.psum((squares, loss_part), AXES)
    masked_loss = loss_all / count
    total_norm = jnp.sqrt(squares_all)
    limit = (slots * shards * windows * lax.axis_size("dp")) ** (-0.5)
    clip = jnp.minimum(1.0, limit / (total_norm + 1e-06))
    steps = step_count[0].astype(jnp.float32)
    fix_one = 1.0 - beta_one**steps
    fix_two = 1.0 - beta_two**steps
    weights_new, firsts_new, seconds_new, averages_new = ([], [], [], [])
    for weight, grad, first, second, average, step_rate in zip(
        master, grads, firsts, seconds, averages, group_rates
    ):
        scaled = grad * clip
        first_next = beta_one * first + (1.0 - beta_one) * scaled
        second_next = beta_two * second + (1.0 - beta_two) * scaled * scaled
        update = (
            first_next / fix_one / (jnp.sqrt(second_next / fix_two) + adam_eps)
            + weight_decay * weight
        )
        weight_next = weight - step_rate * update
        weights_new.append(weight_next)
        firsts_new.append(first_next)
        seconds_new.append(second_next)
        averages_new.append(ema_decay * average + (1.0 - ema_decay) * weight_next)
    return (masked_loss, total_norm, *weights_new, *firsts_new, *seconds_new, *averages_new)


def solution(mesh):
    split = P(AXES, None)
    tables = P(None, AXES, None)
    weights = (tables, split, split, split, split)
    return jax.shard_map(
        on_device,
        mesh=mesh,
        in_specs=(P("dp", "seq"),) * 4 + (P(),) + weights * 4,
        out_specs=(P(), P()) + weights * 4,
        check_vma=False,
    )
```

```python
import functools
import jax, jax.numpy as jnp
from jax import lax
from jax.experimental import pallas as pl
from jax.experimental.pallas import tpu as pltpu
HEAD_DIM=64
PAIR=128
MB=1<<20
MESH = pl.DeviceIdType.MESH

def dims(a,b): return (((a,),(b,)),((),()))

def low_half(rows):
    lane = lax.broadcasted_iota(jnp.int32,(rows,PAIR),1)
    return lane % HEAD_DIM < HEAD_DIM//2

def turn(x, cosines, sines):
    low = low_half(x.shape[0])
    up = pltpu.roll(x, PAIR-HEAD_DIM//2, 1)
    down = pltpu.roll(x, HEAD_DIM//2, 1)
    return x*cosines + jnp.where(low,-up,down)*sines

def turn_back(g, cosines, sines):
    low = low_half(g.shape[0])
    up = pltpu.roll(g, PAIR-HEAD_DIM//2, 1)
    down = pltpu.roll(g, HEAD_DIM//2, 1)
    return g*cosines + jnp.where(low,up,-down)*sines

def head_mask(head):
    lane = lax.broadcasted_iota(jnp.int32,(1,PAIR),1)
    return (lane//HEAD_DIM==head).astype(jnp.float32).astype(jnp.bfloat16)

def forward_kernel(win_ref, q_ref, kv_ref, mix_ref, total_ref):
    queries = q_ref[...]
    keys = kv_ref[:, :PAIR]
    values = kv_ref[:, PAIR:]
    parts=[]
    for head in range(2):
        scores = lax.dot_general(keys, queries*head_mask(head), dims(1,1), preferred_element_type=jnp.float32)
        top = jnp.max(scores, axis=0, keepdims=True)
        chances = jnp.exp(scores-top)
        total = jnp.sum(chances, axis=0, keepdims=True)
        weights = (chances*(1.0/total)).astype(jnp.bfloat16)
        mixed = lax.dot_general(values, weights, dims(0,0), preferred_element_type=jnp.float32)
        parts.append(mixed[head*HEAD_DIM:(head+1)*HEAD_DIM])
        total_ref[0,0,head:head+1,:] = top+jnp.log(total)
    mix_ref[...] = jnp.concatenate(parts,axis=0).T.astype(jnp.bfloat16)

def attend_forward(win, queries, key_values, span, length):
    tokens,width = queries.shape
    pairs = width//PAIR
    blocks = tokens//span
    return pl.pallas_call(
        forward_kernel,
        grid_spec=pltpu.PrefetchScalarGridSpec(
            num_scalar_prefetch=1, grid=(pairs,blocks),
            in_specs=[pl.BlockSpec((span,PAIR),lambda p,b,w:(b,p)),
                      pl.BlockSpec((length,2*PAIR),lambda p,b,w:(w[b],p))],
            out_specs=[pl.BlockSpec((span,PAIR),lambda p,b,w:(b,p)),
                       pl.BlockSpec((1,1,8,span),lambda p,b,w:(p,b,0,0))]),
        out_shape=[jax.ShapeDtypeStruct((tokens,width),jnp.bfloat16),
                   jax.ShapeDtypeStruct((pairs,blocks,8,span),jnp.float32)],
        compiler_params=pltpu.CompilerParams(vmem_limit_bytes=56*MB),
        cost_estimate=pl.CostEstimate(flops=4*tokens*length*width,bytes_accessed=16*MB,transcendentals=tokens*length*width//HEAD_DIM),
        name="attend_forward",
    )(win,queries,key_values)

def backward_kernel(win_ref, q_ref, kv_ref, grad_ref, total_ref, cosq_ref, sinq_ref, cosk_ref, sink_ref, gq_ref, gkv_ref, acc_ref):
    block = pl.program_id(1)
    length = kv_ref.shape[0]
    @pl.when(block==0)
    def _():
        acc_ref[...] = jnp.zeros_like(acc_ref)
    queries = q_ref[...]
    keys = kv_ref[:, :PAIR]
    values = kv_ref[:, PAIR:]
    grads = grad_ref[...]
    start = pl.multiple_of(win_ref[block]*length, length)
    parts=[]
    grad_keys = None
    for head in range(2):
        mask = head_mask(head)
        queries_h = queries*mask
        grads_h = grads*mask
        scores = lax.dot_general(keys, queries_h, dims(1,1), preferred_element_type=jnp.float32)
        chances = jnp.exp(scores-total_ref[0,0,head:head+1,:])
        grad_chances = lax.dot_general(values, grads_h, dims(1,1), preferred_element_type=jnp.float32)
        both = chances*grad_chances
        inner = jnp.sum(both,axis=0,keepdims=True)
        grad_scores = (both-chances*inner).astype(jnp.bfloat16)
        grad_values_h = lax.dot_general(chances.astype(jnp.bfloat16), grads_h, dims(1,0), preferred_element_type=jnp.float32)
        grad_keys_h = lax.dot_general(grad_scores, queries_h, dims(1,0), preferred_element_type=jnp.float32)
        acc_ref[pl.ds(start,length),:PAIR] += grad_keys_h
        acc_ref[pl.ds(start,length),PAIR:] += grad_values_h
        grad_q = lax.dot_general(keys, grad_scores, dims(0,0), preferred_element_type=jnp.float32)
        parts.append(grad_q[head*HEAD_DIM:(head+1)*HEAD_DIM])
    grad_q = jnp.concatenate(parts,axis=0).T * (HEAD_DIM**-0.5)
    gq_ref[...] = turn_back(grad_q,cosq_ref[...],sinq_ref[...]).astype(jnp.bfloat16)
    @pl.when(block==pl.num_programs(1)-1)
    def _():
        for w in range(acc_ref.shape[0]//length):
            rows = pl.ds(w*length,length)
            gkv_ref[rows,:PAIR] = turn_back(acc_ref[rows,:PAIR],cosk_ref[...],sink_ref[...]).astype(jnp.bfloat16)
            gkv_ref[rows,PAIR:] = acc_ref[rows,PAIR:].astype(jnp.bfloat16)

def attend_backward(win, queries, key_values, grads, totals, rope_q, rope_k, span, length):
    tokens,width = queries.shape
    pairs = width//PAIR
    blocks = tokens//span
    all_rows = key_values.shape[0]
    return pl.pallas_call(
        backward_kernel,
        grid_spec=pltpu.PrefetchScalarGridSpec(
            num_scalar_prefetch=1, grid=(pairs,blocks),
            in_specs=[pl.BlockSpec((span,PAIR),lambda p,b,w:(b,p)),
                      pl.BlockSpec((length,2*PAIR),lambda p,b,w:(w[b],p)),
                      pl.BlockSpec((span,PAIR),lambda p,b,w:(b,p)),
                      pl.BlockSpec((1,1,8,span),lambda p,b,w:(p,b,0,0)),
                      pl.BlockSpec((span,PAIR),lambda p,b,w:(b,0)),
                      pl.BlockSpec((span,PAIR),lambda p,b,w:(b,0)),
                      pl.BlockSpec((length,PAIR),lambda p,b,w:(0,0)),
                      pl.BlockSpec((length,PAIR),lambda p,b,w:(0,0))],
            out_specs=[pl.BlockSpec((span,PAIR),lambda p,b,w:(b,p)),
                       pl.BlockSpec((all_rows,2*PAIR),lambda p,b,w:(0,p))],
            scratch_shapes=[pltpu.VMEM((all_rows,2*PAIR),jnp.float32)]),
        out_shape=[jax.ShapeDtypeStruct((tokens,width),jnp.bfloat16),
                   jax.ShapeDtypeStruct((all_rows,2*width),jnp.bfloat16)],
        compiler_params=pltpu.CompilerParams(vmem_limit_bytes=60*MB),
        cost_estimate=pl.CostEstimate(flops=10*tokens*length*width,bytes_accessed=32*MB,transcendentals=tokens*length*width//HEAD_DIM),
        name="attend_backward",
    )(win,queries,key_values,grads,totals,*rope_q,*rope_k)


def cost(flops, moved):
    return pl.CostEstimate(flops=flops, bytes_accessed=moved, transcendentals=0)


def gate_kernel(x_ref, gate_w_ref, up_w_ref, gate_ref, up_ref, hidden_ref):
    gate = jnp.dot(x_ref[...], gate_w_ref[...], preferred_element_type=jnp.float32)
    up = jnp.dot(x_ref[...], up_w_ref[...], preferred_element_type=jnp.float32)
    gate_ref[...] = gate
    up_ref[...] = up
    hidden_ref[...] = (gate * jax.nn.sigmoid(gate) * up).astype(jnp.bfloat16)


def gate_forward(x, weights, hidden_width, wide=512, tile=None):
    tokens, width = x.shape
    tile = tile or tokens
    shift = hidden_width // wide
    spot = lambda n, m: (m, n)
    return pl.pallas_call(
        gate_kernel,
        grid=(hidden_width // wide, tokens // tile),
        in_specs=[
            pl.BlockSpec((tile, width), lambda n, m: (m, 0)),
            pl.BlockSpec((width, wide), lambda n, m: (0, n)),
            pl.BlockSpec((width, wide), lambda n, m: (0, n + shift)),
        ],
        out_specs=[pl.BlockSpec((tile, wide), spot)] * 3,
        out_shape=[
            jax.ShapeDtypeStruct((tokens, hidden_width), jnp.float32),
            jax.ShapeDtypeStruct((tokens, hidden_width), jnp.float32),
            jax.ShapeDtypeStruct((tokens, hidden_width), jnp.bfloat16),
        ],
        compiler_params=pltpu.CompilerParams(vmem_limit_bytes=48 * MB),
        cost_estimate=cost(4 * tokens * width * hidden_width, 10 * tokens * hidden_width + 4 * width * hidden_width),
        name="gate_forward",
    )(x, weights, weights)


def down_kernel(hidden_ref, w_ref, base_ref, out_ref):
    part = jnp.dot(hidden_ref[...], w_ref[...], preferred_element_type=jnp.float32)

    @pl.when(pl.program_id(1) == 0)
    def _():
        out_ref[...] = base_ref[...] + part

    @pl.when(pl.program_id(1) > 0)
    def _():
        out_ref[...] += part


def down_forward(hidden, weights, base, first, tile=None):
    tokens, width = base.shape
    tile = tile or tokens
    folds = hidden.shape[1] // width
    shift = first // width
    return pl.pallas_call(
        down_kernel,
        grid=(tokens // tile, folds),
        in_specs=[
            pl.BlockSpec((tile, width), lambda m, f: (m, f)),
            pl.BlockSpec((width, width), lambda m, f: (0, f + shift)),
            pl.BlockSpec((tile, width), lambda m, f: (m, 0)),
        ],
        out_specs=pl.BlockSpec((tile, width), lambda m, f: (m, 0)),
        out_shape=jax.ShapeDtypeStruct((tokens, width), jnp.float32),
        compiler_params=pltpu.CompilerParams(vmem_limit_bytes=48 * MB),
        cost_estimate=cost(2 * tokens * width * folds * width, 12 * tokens * width + 2 * folds * width * width),
        name="down_forward",
    )(hidden, weights, base)


def gate_back_kernel(grad_ref, w_ref, gate_ref, up_ref, grad_gate_ref, grad_up_ref):
    grad_hidden = lax.dot_general(grad_ref[...], w_ref[...], dims(1, 1), preferred_element_type=jnp.float32)
    gate = gate_ref[...]
    sigmoid = jax.nn.sigmoid(gate)
    grad_up_ref[...] = (grad_hidden * (gate * sigmoid)).astype(jnp.bfloat16)
    grad_gate_ref[...] = (
        grad_hidden * up_ref[...] * (sigmoid * (1.0 + gate * (1.0 - sigmoid)))
    ).astype(jnp.bfloat16)


def gate_backward(grad, weights, gate, up, first, wide=512, tile=None):
    tokens, width = grad.shape
    tile = tile or tokens
    hidden_width = gate.shape[1]
    per = width // wide
    shift = first // width
    spot = lambda n, m: (m, n)
    return pl.pallas_call(
        gate_back_kernel,
        grid=(hidden_width // wide, tokens // tile),
        in_specs=[
            pl.BlockSpec((tile, width), lambda n, m: (m, 0)),
            pl.BlockSpec((wide, width), lambda n, m: (lax.rem(n, per), n // per + shift)),
            pl.BlockSpec((tile, wide), spot),
            pl.BlockSpec((tile, wide), spot),
        ],
        out_specs=[pl.BlockSpec((tile, wide), spot)] * 2,
        out_shape=[jax.ShapeDtypeStruct((tokens, hidden_width), jnp.bfloat16)] * 2,
        compiler_params=pltpu.CompilerParams(vmem_limit_bytes=48 * MB),
        cost_estimate=cost(2 * tokens * width * hidden_width, 12 * tokens * hidden_width + 2 * width * hidden_width),
        name="gate_backward",
    )(grad, weights, gate, up)


def swap_rows(out, value, order):
    outer, inner = order
    rows = value.shape[0] // (outer * inner)
    for i in range(outer):
        for j in range(inner):
            spot, source = (j * outer + i) * rows, (i * inner + j) * rows
            out[spot : spot + rows, :] = value[source : source + rows, :]


def weight_kernel(sides, order, left_ref, *refs):
    out_ref, turned = refs[-2], refs[-1]

    @pl.when(pl.program_id(0) == 0)
    def _():
        swap_rows(turned, left_ref[...].T, order)

    per = pl.num_programs(0) // sides
    for side in range(sides):
        @pl.when(pl.program_id(0) // per == side)
        def _():
            out_ref[...] = jnp.dot(
                turned[...], refs[side][...], preferred_element_type=jnp.float32
            ).astype(jnp.bfloat16)


def weight_grad(left, rights, order, wide=1024, total=None, filled=None, first=0):
    tokens, width = left.shape
    sides, columns = len(rights), rights[0].shape[1]
    per = columns // wide
    return pl.pallas_call(
        functools.partial(weight_kernel, sides, order),
        grid=(sides * per,),
        in_specs=[pl.BlockSpec((tokens, width), lambda n: (0, 0))]
        + [
            pl.BlockSpec((tokens, wide), lambda n, s=s: (0, jnp.clip(n - s * per, 0, per - 1)))
            for s in range(sides)
        ]
        + [pl.BlockSpec(memory_space=pl.ANY)] * (filled is not None),
        out_specs=pl.BlockSpec(
            (pl.Element(width), pl.Element(wide)),
            lambda n: (0, pl.multiple_of(first + n * wide, PAIR)),
        ),
        out_shape=jax.ShapeDtypeStruct((width, total or sides * columns), jnp.bfloat16),
        input_output_aliases={} if filled is None else {1 + sides: 0},
        scratch_shapes=[pltpu.VMEM((width, tokens), jnp.bfloat16)],
        compiler_params=pltpu.CompilerParams(vmem_limit_bytes=56 * MB),
        cost_estimate=cost(2 * tokens * width * sides * columns, 4 * (tokens + width) * sides * columns),
        name="weight_grad",
    )(left, *rights, *([] if filled is None else [filled]))


def down_grad_kernel(order, hidden_ref, grad_ref, filled_ref, out_ref):
    value = lax.dot_general(
        hidden_ref[...], grad_ref[...], dims(0, 0), preferred_element_type=jnp.float32
    )
    swap_rows(out_ref, value.astype(jnp.bfloat16), order)


def down_grad(hidden, grad, filled, first, order):
    tokens, width = grad.shape
    folds = hidden.shape[1] // width
    return pl.pallas_call(
        functools.partial(down_grad_kernel, order),
        grid=(folds,),
        in_specs=[
            pl.BlockSpec((tokens, width), lambda f: (0, f)),
            pl.BlockSpec((tokens, width), lambda f: (0, 0)),
            pl.BlockSpec(memory_space=pl.ANY),
        ],
        out_specs=pl.BlockSpec(
            (pl.Element(width), pl.Element(width)), lambda f: (0, pl.multiple_of(first + f * width, PAIR))
        ),
        out_shape=jax.ShapeDtypeStruct(filled.shape, jnp.bfloat16),
        input_output_aliases={2: 0},
        compiler_params=pltpu.CompilerParams(vmem_limit_bytes=48 * MB),
        cost_estimate=cost(2 * tokens * width * folds * width, 4 * tokens * folds * width),
        name="down_grad",
    )(hidden, grad, filled)


def input_kernel(sides, first_ref, *refs):
    grads, weights, out_ref = refs[:sides], refs[sides:2 * sides], refs[2 * sides]
    part = None
    for grad_ref, w_ref in zip(grads, weights):
        term = lax.dot_general(grad_ref[...], w_ref[...], dims(1, 1), preferred_element_type=jnp.float32)
        part = term if part is None else part + term

    @pl.when(pl.program_id(1) == 0)
    def _():
        out_ref[...] = part

    @pl.when(pl.program_id(1) > 0)
    def _():
        out_ref[...] += part


def input_grad(grads, weights, firsts, wide=1024, tile=None):
    tokens, columns = grads[0].shape
    width = weights.shape[0]
    tile = tile or tokens
    sides = len(grads)
    return pl.pallas_call(
        lambda *refs: input_kernel(sides, None, *refs),
        grid=(tokens // tile, columns // wide),
        in_specs=[pl.BlockSpec((tile, wide), lambda m, k: (m, k))] * sides
        + [
            pl.BlockSpec((width, wide), lambda m, k, first=first: (0, k + first // wide))
            for first in firsts
        ],
        out_specs=pl.BlockSpec((tile, width), lambda m, k: (m, 0)),
        out_shape=jax.ShapeDtypeStruct((tokens, width), jnp.float32),
        compiler_params=pltpu.CompilerParams(vmem_limit_bytes=48 * MB),
        cost_estimate=cost(2 * sides * tokens * width * columns, 2 * sides * (tokens + width) * columns),
        name="input_grad",
    )(*grads, *([weights] * sides))


def grid_sizes():
    cores = 2
    across = lax.axis_size("seq") // cores
    return lax.axis_size("dp") // across, across, across, cores


def column_chunks(columns, count):
    lanes = columns // PAIR
    widths = [(lanes // count + (i < lanes % count)) * PAIR for i in range(count)]
    starts = [sum(widths[:i]) for i in range(count)]
    return [pl.ds(start, wide) for start, wide in zip(starts, widths)]


class Place:
    def __init__(self, sizes):
        self.sizes = dict(zip("zyxc", sizes))
        dp, seq = lax.axis_index("dp"), lax.axis_index("seq")
        self.at = {
            "z": dp // sizes[1],
            "y": lax.rem(dp, sizes[1]),
            "x": seq // sizes[3],
            "c": lax.rem(seq, sizes[3]),
        }

    def other(self, axis, step):
        return lax.rem(self.at[axis] + step, self.sizes[axis])

    def device(self, axis, step):
        at = dict(self.at)
        at[axis] = self.other(axis, step)
        return (at["z"] * self.sizes["y"] + at["y"], at["x"] * self.sizes["c"] + at["c"])

    def steps(self, axis):
        return range(1, self.sizes[axis])

    def greet(self):
        barrier = pltpu.get_barrier_semaphore()
        peers = 0
        for axis in "cxyz":
            for step in self.steps(axis):
                pl.semaphore_signal(barrier, inc=1, device_id=self.device(axis, step), device_id_type=MESH)
                peers += 1
        pl.semaphore_wait(barrier, peers)


def scatter_kernel(sizes, chunks, g_ref, out_ref, own, one, two, three, four, load_sem, send_sem, recv_sem):
    n_z, n_y, n_x, n_c = sizes
    place = Place(sizes)
    at = place.at
    f32 = jnp.float32
    started = []

    def send(src, dst, chunk, slot, axis, step):
        copy = pltpu.make_async_remote_copy(
            src_ref=src, dst_ref=dst, send_sem=send_sem.at[chunk, slot], recv_sem=recv_sem.at[chunk, slot],
            device_id=place.device(axis, step), device_id_type=MESH)
        copy.start()
        started.append(copy)
        return copy

    place.greet()
    loads, cores = [], []
    for chunk, cols in enumerate(chunks):
        load = pltpu.make_async_copy(g_ref.at[:, :, :, at["c"], :, cols], own.at[:, :, :, :, cols], load_sem.at[chunk])
        load.start()
        loads.append(load)
        cores.append(send(g_ref.at[:, :, :, place.other("c", 1), :, cols], one.at[:, :, :, :, cols], chunk, 0, "c", 1))

    waits = {}

    def first(chunk, cols):
        loads[chunk].wait()
        cores[chunk].wait_recv()

        def add(i, carry):
            z, rest = i // (n_y * n_x), lax.rem(i, n_y * n_x)
            y, x = rest // n_x, lax.rem(rest, n_x)
            total = own[z, y, x, :, cols].astype(f32) + one[z, y, x, :, cols].astype(f32)
            one[z, y, x, :, cols] = total.astype(jnp.bfloat16)
            return carry

        lax.fori_loop(0, n_z * n_y * n_x, add, 0)
        axis = "xy"[chunk % 2]
        waits[chunk, 1] = []
        for step in place.steps(axis):
            spot = place.other(axis, step)
            src = one.at[:, :, spot, :, cols] if axis == "x" else one.at[:, spot, :, :, cols]
            waits[chunk, 1].append(send(src, two.at[step - 1, :, :, :, cols], chunk, step, axis, step))

    def second(chunk, cols):
        for copy in waits[chunk, 1]:
            copy.wait_recv()
        axis = "xy"[chunk % 2]
        kept = n_y if axis == "x" else n_x

        def add(i, carry):
            z, k = i // kept, lax.rem(i, kept)
            mine = one[z, k, at["x"], :, cols] if axis == "x" else one[z, at["y"], k, :, cols]
            total = mine.astype(f32)
            for step in place.steps(axis):
                total = total + two[step - 1, z, k, :, cols].astype(f32)
            two[0, z, k, :, cols] = total.astype(jnp.bfloat16)
            return carry

        lax.fori_loop(0, n_z * kept, add, 0)
        axis = "yx"[chunk % 2]
        waits[chunk, 2] = []
        for step in place.steps(axis):
            src = two.at[0, :, place.other(axis, step), :, cols]
            slot = max(n_x, n_y) - 1 + step
            waits[chunk, 2].append(send(src, three.at[step - 1, :, :, cols], chunk, slot, axis, step))

    def third(chunk, cols):
        for copy in waits[chunk, 2]:
            copy.wait_recv()
        axis = "yx"[chunk % 2]

        def add(z, carry):
            total = two[0, z, at[axis], :, cols].astype(f32)
            for step in place.steps(axis):
                total = total + three[step - 1, z, :, cols].astype(f32)
            three[0, z, :, cols] = total.astype(jnp.bfloat16)
            return carry

        lax.fori_loop(0, n_z, add, 0)
        waits[chunk, 3] = []
        for step in place.steps("z"):
            src = three.at[0, place.other("z", step), :, cols]
            slot = 2 * (max(n_x, n_y) - 1) + step
            waits[chunk, 3].append(send(src, four.at[step - 1, :, cols], chunk, slot, "z", step))

    def fourth(chunk, cols):
        for copy in waits[chunk, 3]:
            copy.wait_recv()
        total = three[0, at["z"], :, cols].astype(f32)
        for step in place.steps("z"):
            total = total + four[step - 1, :, cols].astype(f32)
        out_ref[:, cols] = total

    pairs = (len(chunks) + 1) // 2
    for tick in range(pairs + 3):
        for late, stage in enumerate((first, second, third, fourth)):
            for chunk in (2 * (tick - late), 2 * (tick - late) + 1):
                if 0 <= tick - late and chunk < len(chunks):
                    stage(chunk, chunks[chunk])
    for copy in started:
        copy.wait_send()


def scatter_sum_direct(grads, collective_id, count=8):
    sizes = grid_sizes()
    n_z, n_y, n_x, n_c = sizes
    total, columns = grads.shape
    rows = total // (n_z * n_y * n_x * n_c)
    most = max(n_x, n_y)
    slots = 1 + 2 * (most - 1) + n_z - 1
    low = jnp.bfloat16
    chunks = column_chunks(columns, count)
    return pl.pallas_call(
        functools.partial(scatter_kernel, sizes, chunks),
        in_specs=[pl.BlockSpec(memory_space=pl.ANY)],
        out_specs=pl.BlockSpec(memory_space=pltpu.VMEM),
        out_shape=jax.ShapeDtypeStruct((rows, columns), jnp.float32),
        scratch_shapes=[
            pltpu.VMEM((n_z, n_y, n_x, rows, columns), low),
            pltpu.VMEM((n_z, n_y, n_x, rows, columns), low),
            pltpu.VMEM((most - 1, n_z, most, rows, columns), low),
            pltpu.VMEM((most - 1, n_z, rows, columns), low),
            pltpu.VMEM((n_z - 1, rows, columns), low),
            pltpu.SemaphoreType.DMA((count,)),
            pltpu.SemaphoreType.DMA((count, slots)),
            pltpu.SemaphoreType.DMA((count, slots)),
        ],
        compiler_params=pltpu.CompilerParams(
            collective_id=collective_id, has_side_effects=True, vmem_limit_bytes=48 * MB),
        cost_estimate=pl.CostEstimate(flops=2 * total * columns, bytes_accessed=2 * total * columns, transcendentals=0),
        name="scatter_sum",
    )(grads.reshape(n_z, n_y, n_x, n_c, rows, columns))


def total_kernel(sizes, x_ref, out_ref, z_slots, y_slots, x_slots, c_slots, send_sem, recv_sem):
    place = Place(sizes)
    slots = {"z": z_slots, "y": y_slots, "x": x_slots, "c": c_slots}
    place.greet()
    total = x_ref[...]
    started = []
    for turn_at, axis in enumerate("cxyz"):
        held, me = slots[axis], place.at[axis]
        held[me] = total
        arriving = []
        for step in place.steps(axis):
            copy = pltpu.make_async_remote_copy(
                src_ref=held.at[me], dst_ref=held.at[me],
                send_sem=send_sem.at[turn_at, step], recv_sem=recv_sem.at[turn_at, step],
                device_id=place.device(axis, step), device_id_type=MESH)
            copy.start()
            arriving.append(copy)
        for copy in arriving:
            copy.wait_recv()
        started += arriving
        total = held[0]
        for spot in range(1, place.sizes[axis]):
            total = total + held[spot]
    out_ref[...] = total
    for copy in started:
        copy.wait_send()


def total_over_all(values, collective_id):
    sizes = grid_sizes()
    row = lax.broadcasted_iota(jnp.int32, (8, PAIR), 0)
    tile = jnp.zeros((8, PAIR), jnp.float32)
    for i, value in enumerate(values):
        tile = jnp.where(row == i, value, tile)
    total = pl.pallas_call(
        functools.partial(total_kernel, sizes),
        in_specs=[pl.BlockSpec(memory_space=pltpu.VMEM)],
        out_specs=pl.BlockSpec(memory_space=pltpu.VMEM),
        out_shape=jax.ShapeDtypeStruct(tile.shape, jnp.float32),
        scratch_shapes=[pltpu.VMEM((size, 8, PAIR), jnp.float32) for size in sizes]
        + [pltpu.SemaphoreType.DMA((4, max(sizes)))] * 2,
        compiler_params=pltpu.CompilerParams(collective_id=collective_id, has_side_effects=True),
        name="total_over_all",
    )(tile)
    return [total[i, 0] for i in range(len(values))]


from jax.sharding import PartitionSpec as P

AXES = ("dp", "seq")
beta_one = 0.9
beta_two = 0.999
adam_eps = 1e-08
weight_decay = 0.01
learn_rate = 0.02
norm_rate = 0.2
ema_decay = 0.7
norm_eps = 1e-05


def project_kernel(roped, x_ref, w_ref, cos_ref, sin_ref, out_ref):
    product = jnp.dot(x_ref[...], w_ref[...], preferred_element_type=jnp.float32)
    for part in range(product.shape[1] // PAIR):
        piece = product[:, part * PAIR : (part + 1) * PAIR]
        if roped == "all":
            piece = turn(piece, cos_ref[...], sin_ref[...]).astype(jnp.bfloat16)
            piece = piece * jnp.bfloat16(HEAD_DIM**-0.5)
        elif part % 2 == 0:
            piece = turn(piece, cos_ref[...], sin_ref[...])
        out_ref[:, part * PAIR : (part + 1) * PAIR] = piece.astype(jnp.bfloat16)


def project(x, weights, first_column, columns, rope, tile, roped):
    tokens, width = x.shape
    wide = 512
    repeat = rope[0].shape[0] // tile
    return pl.pallas_call(
        functools.partial(project_kernel, roped),
        grid=(tokens // tile, columns // wide),
        in_specs=[
            pl.BlockSpec((tile, width), lambda m, n: (m, 0)),
            pl.BlockSpec((width, wide), lambda m, n: (0, n + first_column // wide)),
            pl.BlockSpec((tile, PAIR), lambda m, n: (lax.rem(m, repeat), 0)),
            pl.BlockSpec((tile, PAIR), lambda m, n: (lax.rem(m, repeat), 0)),
        ],
        out_specs=pl.BlockSpec((tile, wide), lambda m, n: (m, n)),
        out_shape=jax.ShapeDtypeStruct((tokens, columns), jnp.bfloat16),
        compiler_params=pltpu.CompilerParams(vmem_limit_bytes=40 * MB),
        cost_estimate=pl.CostEstimate(
            flops=2 * tokens * width * columns,
            bytes_accessed=2 * (tokens * width + width * columns + tokens * columns),
            transcendentals=0,
        ),
        name="project",
    )(x, weights, *rope)


def rope_tables(positions):
    half = HEAD_DIM // 2
    inverse = 10000.0 ** (-jnp.arange(half).astype(jnp.float32) / half)
    angles = positions.astype(jnp.float32)[:, None] * inverse[None, :]
    copies = PAIR // half
    return (jnp.tile(jnp.cos(angles), (1, copies)), jnp.tile(jnp.sin(angles), (1, copies)))


def norm_forward(values, gain, shift):
    centre = values - jnp.mean(values, axis=-1, keepdims=True)
    spread = jnp.mean(centre * centre, axis=-1, keepdims=True)
    scale = lax.rsqrt(spread + norm_eps)
    unit = centre * scale
    return (unit * gain + shift).astype(jnp.bfloat16), unit, scale


def norm_backward(grad, unit, scale, gain):
    grad_gain = jnp.sum(grad * unit, axis=0)
    grad_shift = jnp.sum(grad, axis=0)
    scaled = grad * gain
    inner = jnp.mean(scaled * unit, axis=-1, keepdims=True)
    outer = jnp.mean(scaled, axis=-1, keepdims=True)
    return scale * (scaled - outer - unit * inner), grad_gain, grad_shift


def product(left, right, left_dim=1, right_dim=0, precision=None):
    return lax.dot_general(
        left, right, dims(left_dim, right_dim), precision=precision,
        preferred_element_type=jnp.float32,
    )


def pair_columns(weights):
    rows, columns = weights.shape
    width = columns // 2
    return weights.reshape(rows, 2, width // PAIR, PAIR).transpose(0, 2, 1, 3).reshape(rows, columns)


def unpair_columns(weights):
    rows, columns = weights.shape
    width = columns // 2
    return weights.reshape(rows, width // PAIR, 2, PAIR).transpose(0, 2, 1, 3).reshape(rows, columns)


def scatter_sum(grads):
    part = lax.psum_scatter(grads, "seq", scatter_dimension=0, tiled=True)
    return lax.psum_scatter(part, "dp", scatter_dimension=0, tiled=True)


def on_device(
    token_ids,
    mask_rows,
    mask_labels,
    mask_counts,
    step_count,
    vocab_tables,
    attention,
    feed_in,
    feed_out,
    norm_params,
    first_tables,
    first_attention,
    first_feed_in,
    first_feed_out,
    first_norms,
    second_tables,
    second_attention,
    second_feed_in,
    second_feed_out,
    second_norms,
    ema_tables,
    ema_attention,
    ema_feed_in,
    ema_feed_out,
    ema_norms,
):
    master = (vocab_tables, attention, feed_in, feed_out, norm_params)
    firsts = (first_tables, first_attention, first_feed_in, first_feed_out, first_norms)
    seconds = (second_tables, second_attention, second_feed_in, second_feed_out, second_norms)
    averages = (ema_tables, ema_attention, ema_feed_in, ema_feed_out, ema_norms)
    group_rates = (learn_rate, learn_rate, learn_rate, learn_rate, norm_rate)
    low = jnp.bfloat16

    shards = lax.axis_size("seq")
    devices = shards * lax.axis_size("dp")
    windows, span = token_ids.shape
    slots = mask_rows.shape[1]
    vocab = vocab_tables.shape[2]
    padded = vocab + -vocab % PAIR
    rows, columns = attention.shape
    width = columns // 4
    hidden_width = feed_in.shape[1] // 2
    folds = feed_out.shape[0] // rows
    length = span * shards
    spot = lax.axis_index("seq")

    tables_sent = jnp.pad(vocab_tables, ((0, 0), (0, 0), (0, padded - vocab)))
    early_sent = jnp.concatenate(
        [
            attention[:, :width],
            pair_columns(attention[:, width : 3 * width]),
            attention[:, 3 * width :],
            tables_sent[0],
        ],
        axis=1,
    ).astype(low)
    in_sent = feed_in.reshape(rows, 2, hidden_width // folds, folds).transpose(0, 1, 3, 2)
    late_sent = jnp.concatenate(
        [
            in_sent.reshape(rows, 2 * hidden_width),
            feed_out.reshape(rows, folds * width),
            tables_sent[1],
        ],
        axis=1,
    ).astype(low)
    early = lax.all_gather(early_sent, AXES, axis=0, tiled=True)
    late = lax.all_gather(late_sent, AXES, axis=0, tiled=True)
    table_w = early[:, columns:]
    out_w = early[:, 3 * width : columns]
    head_w = late[:, 2 * hidden_width + folds * width :]

    small = jnp.concatenate(
        [
            token_ids.reshape(-1).astype(jnp.float32),
            mask_rows.reshape(-1).astype(jnp.float32),
            mask_labels.reshape(-1).astype(jnp.float32),
            mask_counts.reshape(-1).astype(jnp.float32),
            norm_params.astype(low).astype(jnp.float32).reshape(-1),
        ]
    )
    small = jnp.pad(small, (0, -small.shape[0] % PAIR)).reshape(1, -1)
    small_all = lax.all_gather(small, AXES, axis=0, tiled=True)
    cuts = [windows * span, windows * slots, windows * slots, windows]
    marks = [sum(cuts[:i]) for i in range(len(cuts) + 1)]
    gains = small_all[:, marks[4] : marks[4] + rows * 6].reshape(devices * rows, 6)
    count = jnp.sum(small_all[:, marks[3] : marks[4]])
    group = lax.dynamic_slice_in_dim(small_all, lax.axis_index("dp") * shards, shards, axis=0)

    def in_order(first, last):
        piece = group[:, first:last].reshape(shards, windows, -1)
        return piece.transpose(1, 0, 2).reshape(windows * shards, -1)

    ids = in_order(marks[0], marks[1]).astype(jnp.int32)
    block = spot * windows + jnp.arange(windows, dtype=jnp.int32)

    def mine(first, last):
        return lax.dynamic_slice_in_dim(in_order(first, last), spot * windows, windows, axis=0)

    own_rows = mine(marks[1], marks[2]).astype(jnp.int32)
    own_labels = mine(marks[2], marks[3]).astype(jnp.int32).reshape(-1)
    own_counts = mine(marks[3], marks[4])
    live = (jnp.arange(slots, dtype=jnp.float32)[None, :] < own_counts).astype(jnp.float32)
    live = live.reshape(-1)

    base = jnp.minimum(spot * windows // shards, windows - 2)
    wins = block // shards - base
    offset = (spot * windows - base * shards) * span
    ids_two = lax.dynamic_slice_in_dim(ids, base * shards, 2 * shards, axis=0).reshape(-1)
    positions = ((block % shards)[:, None] * span + jnp.arange(span, dtype=jnp.int32)).reshape(-1)
    rope_q = rope_tables(positions)
    rope_k = rope_tables(jnp.arange(length, dtype=jnp.int32))
    tokens = windows * span

    def own(values):
        return lax.dynamic_slice_in_dim(values, offset, tokens, axis=0)

    onehot = (ids_two[:, None] == jnp.arange(padded, dtype=jnp.int32)[None, :]).astype(low)
    onehot = lax.optimization_barrier(onehot)
    embedded_two = product(onehot, table_w, 1, 1)
    normed_one, unit_one, scale_one = norm_forward(embedded_two, gains[:, 0], gains[:, 1])
    normed_own = own(normed_one)
    queries = project(normed_own, early, 0, width, rope_q, tokens, "all")
    key_values = project(normed_one, early, width, 2 * width, rope_k, length, "half")
    mixture, totals = attend_forward(wins, queries, key_values, span, length)
    after_attn = own(embedded_two) + product(mixture, out_w)

    normed_two, unit_two, scale_two = norm_forward(after_attn, gains[:, 2], gains[:, 3])
    gate, up, hidden = gate_forward(normed_two, late, hidden_width)
    after_feed = down_forward(hidden, late, after_attn, 2 * hidden_width)

    pick = (own_rows[:, :, None] == jnp.arange(span, dtype=jnp.int32)).astype(jnp.float32)
    selected = jnp.einsum(
        "wsp,wpd->wsd", pick, after_feed.reshape(windows, span, width),
        precision=lax.Precision.HIGHEST, preferred_element_type=jnp.float32,
    ).reshape(windows * slots, width)
    normed_final, unit_final, scale_final = norm_forward(selected, gains[:, 4], gains[:, 5])
    column = jnp.arange(padded, dtype=jnp.int32)[None, :]
    logits = jnp.where(column < vocab, product(normed_final, head_w), -jnp.inf)
    log_total = jax.nn.logsumexp(logits, axis=-1)
    wanted = own_labels[:, None] == column
    picked = jnp.sum(jnp.where(wanted, logits, 0.0), axis=-1)
    loss_part = jnp.sum(live * (log_total - picked))

    grad_logits = (
        (jnp.exp(logits - log_total[:, None]) - wanted.astype(jnp.float32)) * (live / count)[:, None]
    ).astype(low)
    grad_selected, grad_gain_final, grad_shift_final = norm_backward(
        product(grad_logits, head_w, 1, 1), unit_final, scale_final, gains[:, 4]
    )
    grad_after_feed = jnp.einsum(
        "wsp,wsd->wpd", pick, grad_selected.reshape(windows, slots, width),
        precision=lax.Precision.HIGHEST, preferred_element_type=jnp.float32,
    ).reshape(tokens, width)
    rounded_feed = grad_after_feed.astype(low)
    order = (lax.axis_size("dp"), shards)
    spare = ((0, -grad_logits.shape[0] % PAIR), (0, 0))
    head_wide = max(PAIR * i for i in range(1, 5) if padded % (PAIR * i) == 0)
    everything = padded + folds * width + 2 * hidden_width
    late_grads = weight_grad(
        jnp.pad(normed_final, spare), (jnp.pad(grad_logits, spare),), order, head_wide, everything
    )
    late_grads = down_grad(hidden, rounded_feed, late_grads, padded, order)
    grad_gate, grad_up = gate_backward(rounded_feed, late, gate, up, 2 * hidden_width)
    late_grads = weight_grad(
        normed_two, (grad_gate, grad_up), order, width, everything, late_grads, padded + folds * width
    )
    grad_gate, grad_up, late_grads = lax.optimization_barrier((grad_gate, grad_up, late_grads))
    late_own = scatter_sum(late_grads)

    grad_inner, grad_gain_two, grad_shift_two = norm_backward(
        input_grad((grad_gate, grad_up), late, (0, hidden_width)), unit_two, scale_two, gains[:, 2]
    )
    grad_after_attn = grad_after_feed + grad_inner
    rounded_attn = grad_after_attn.astype(low)
    grad_output = product(mixture, rounded_attn, 0, 0)
    grad_mixture = product(rounded_attn, out_w, 1, 1).astype(low)
    grad_queries, grad_pairs = attend_backward(
        wins, queries, key_values, grad_mixture, totals, rope_q, rope_k, span, length
    )
    grad_query_w = product(normed_own, grad_queries, 0, 0)
    grad_pair_w = product(normed_one, grad_pairs, 0, 0)
    grad_normed = product(grad_pairs, early[:, width : 3 * width], 1, 1)
    grad_normed = lax.dynamic_update_slice_in_dim(
        grad_normed, own(grad_normed) + product(grad_queries, early[:, :width], 1, 1), offset, axis=0
    )
    grad_embedded, grad_gain_one, grad_shift_one = norm_backward(
        grad_normed, unit_one, scale_one, gains[:, 0]
    )
    grad_embedded = lax.dynamic_update_slice_in_dim(
        grad_embedded, own(grad_embedded) + grad_after_attn, offset, axis=0
    )
    grad_embed = product(grad_embedded.astype(low), onehot, 0, 0)
    grad_norms = jnp.stack(
        [
            grad_gain_one,
            grad_shift_one,
            grad_gain_two,
            grad_shift_two,
            grad_gain_final,
            grad_shift_final,
        ],
        axis=1,
    )
    grad_norms = jnp.pad(grad_norms, ((0, 0), (0, PAIR - grad_norms.shape[1])))
    early_grads = jnp.concatenate(
        [
            item.astype(low)
            for item in (grad_query_w, grad_pair_w, grad_output, grad_embed, grad_norms)
        ],
        axis=1,
    )
    early_own = scatter_sum_direct(early_grads, 1, 16)
    late_own = late_own.astype(jnp.float32)
    in_own = late_own[:, padded + folds * width :].reshape(rows, 2, folds, hidden_width // folds)
    grads = (
        jnp.stack(
            [
                early_own[:, columns : columns + vocab],
                late_own[:, :vocab],
            ],
            axis=0,
        ),
        jnp.concatenate(
            [
                early_own[:, :width],
                unpair_columns(early_own[:, width : 3 * width]),
                early_own[:, 3 * width : columns],
            ],
            axis=1,
        ),
        in_own.transpose(0, 1, 3, 2).reshape(rows, 2 * hidden_width),
        late_own[:, padded : padded + folds * width].reshape(rows * folds, width),
        early_own[:, columns + padded : columns + padded + 6],
    )
    grads = lax.optimization_barrier(grads)
    squares = jnp.zeros((), jnp.float32)
    for grad in grads:
        squares = squares + jnp.sum(grad * grad)
    squares_all, loss_all = total_over_all((squares, loss_part), 2)
    masked_loss = loss_all / count
    total_norm = jnp.sqrt(squares_all)
    limit = (slots * shards * windows * lax.axis_size("dp")) ** (-0.5)
    clip = jnp.minimum(1.0, limit / (total_norm + 1e-06))
    steps = step_count[0].astype(jnp.float32)
    fix_one = 1.0 - beta_one**steps
    fix_two = 1.0 - beta_two**steps
    weights_new, firsts_new, seconds_new, averages_new = ([], [], [], [])
    for weight, grad, first, second, average, step_rate in zip(
        master, grads, firsts, seconds, averages, group_rates
    ):
        scaled = grad * clip
        first_next = beta_one * first + (1.0 - beta_one) * scaled
        second_next = beta_two * second + (1.0 - beta_two) * scaled * scaled
        update = (
            first_next / fix_one / (jnp.sqrt(second_next / fix_two) + adam_eps)
            + weight_decay * weight
        )
        weight_next = weight - step_rate * update
        weights_new.append(weight_next)
        firsts_new.append(first_next)
        seconds_new.append(second_next)
        averages_new.append(ema_decay * average + (1.0 - ema_decay) * weight_next)
    return (masked_loss, total_norm, *weights_new, *firsts_new, *seconds_new, *averages_new)


def solution(mesh):
    split = P(AXES, None)
    tables = P(None, AXES, None)
    weights = (tables, split, split, split, split)
    return jax.shard_map(
        on_device,
        mesh=mesh,
        in_specs=(P("dp", "seq"),) * 4 + (P(),) + weights * 4,
        out_specs=(P(), P()) + weights * 4,
        check_vma=False,
    )
```

```python
import functools
import jax, jax.numpy as jnp
from jax import lax
from jax.experimental import pallas as pl
from jax.experimental.pallas import tpu as pltpu
HEAD_DIM=64
PAIR=128
MB=1<<20
MESH = pl.DeviceIdType.MESH

def dims(a,b): return (((a,),(b,)),((),()))

def low_half(rows):
    lane = lax.broadcasted_iota(jnp.int32,(rows,PAIR),1)
    return lane % HEAD_DIM < HEAD_DIM//2

def turn(x, cosines, sines):
    low = low_half(x.shape[0])
    up = pltpu.roll(x, PAIR-HEAD_DIM//2, 1)
    down = pltpu.roll(x, HEAD_DIM//2, 1)
    return x*cosines + jnp.where(low,-up,down)*sines

def turn_back(g, cosines, sines):
    low = low_half(g.shape[0])
    up = pltpu.roll(g, PAIR-HEAD_DIM//2, 1)
    down = pltpu.roll(g, HEAD_DIM//2, 1)
    return g*cosines + jnp.where(low,up,-down)*sines

def head_mask(head):
    lane = lax.broadcasted_iota(jnp.int32,(1,PAIR),1)
    return (lane//HEAD_DIM==head).astype(jnp.float32).astype(jnp.bfloat16)

def forward_kernel(win_ref, q_ref, kv_ref, mix_ref, total_ref):
    queries = q_ref[...]
    keys = kv_ref[:, :PAIR]
    values = kv_ref[:, PAIR:]
    parts=[]
    for head in range(2):
        scores = lax.dot_general(keys, queries*head_mask(head), dims(1,1), preferred_element_type=jnp.float32)
        top = jnp.max(scores, axis=0, keepdims=True)
        chances = jnp.exp(scores-top)
        total = jnp.sum(chances, axis=0, keepdims=True)
        weights = (chances*(1.0/total)).astype(jnp.bfloat16)
        mixed = lax.dot_general(values, weights, dims(0,0), preferred_element_type=jnp.float32)
        parts.append(mixed[head*HEAD_DIM:(head+1)*HEAD_DIM])
        total_ref[0,0,head:head+1,:] = top+jnp.log(total)
    mix_ref[...] = jnp.concatenate(parts,axis=0).T.astype(jnp.bfloat16)

def attend_forward(win, queries, key_values, span, length):
    tokens,width = queries.shape
    pairs = width//PAIR
    blocks = tokens//span
    return pl.pallas_call(
        forward_kernel,
        grid_spec=pltpu.PrefetchScalarGridSpec(
            num_scalar_prefetch=1, grid=(pairs,blocks),
            in_specs=[pl.BlockSpec((span,PAIR),lambda p,b,w:(b,p)),
                      pl.BlockSpec((length,2*PAIR),lambda p,b,w:(w[b],p))],
            out_specs=[pl.BlockSpec((span,PAIR),lambda p,b,w:(b,p)),
                       pl.BlockSpec((1,1,8,span),lambda p,b,w:(p,b,0,0))]),
        out_shape=[jax.ShapeDtypeStruct((tokens,width),jnp.bfloat16),
                   jax.ShapeDtypeStruct((pairs,blocks,8,span),jnp.float32)],
        compiler_params=pltpu.CompilerParams(vmem_limit_bytes=56*MB),
        cost_estimate=pl.CostEstimate(flops=4*tokens*length*width,bytes_accessed=16*MB,transcendentals=tokens*length*width//HEAD_DIM),
        name="attend_forward",
    )(win,queries,key_values)

def backward_kernel(win_ref, q_ref, kv_ref, grad_ref, total_ref, cosq_ref, sinq_ref, cosk_ref, sink_ref, gq_ref, gkv_ref, acc_ref):
    block = pl.program_id(1)
    length = kv_ref.shape[0]
    @pl.when(block==0)
    def _():
        acc_ref[...] = jnp.zeros_like(acc_ref)
    queries = q_ref[...]
    keys = kv_ref[:, :PAIR]
    values = kv_ref[:, PAIR:]
    grads = grad_ref[...]
    start = pl.multiple_of(win_ref[block]*length, length)
    parts=[]
    grad_keys = None
    for head in range(2):
        mask = head_mask(head)
        queries_h = queries*mask
        grads_h = grads*mask
        scores = lax.dot_general(keys, queries_h, dims(1,1), preferred_element_type=jnp.float32)
        chances = jnp.exp(scores-total_ref[0,0,head:head+1,:])
        grad_chances = lax.dot_general(values, grads_h, dims(1,1), preferred_element_type=jnp.float32)
        both = chances*grad_chances
        inner = jnp.sum(both,axis=0,keepdims=True)
        grad_scores = (both-chances*inner).astype(jnp.bfloat16)
        grad_values_h = lax.dot_general(chances.astype(jnp.bfloat16), grads_h, dims(1,0), preferred_element_type=jnp.float32)
        grad_keys_h = lax.dot_general(grad_scores, queries_h, dims(1,0), preferred_element_type=jnp.float32)
        acc_ref[pl.ds(start,length),:PAIR] += grad_keys_h
        acc_ref[pl.ds(start,length),PAIR:] += grad_values_h
        grad_q = lax.dot_general(keys, grad_scores, dims(0,0), preferred_element_type=jnp.float32)
        parts.append(grad_q[head*HEAD_DIM:(head+1)*HEAD_DIM])
    grad_q = jnp.concatenate(parts,axis=0).T * (HEAD_DIM**-0.5)
    gq_ref[...] = turn_back(grad_q,cosq_ref[...],sinq_ref[...]).astype(jnp.bfloat16)
    @pl.when(block==pl.num_programs(1)-1)
    def _():
        for w in range(acc_ref.shape[0]//length):
            rows = pl.ds(w*length,length)
            gkv_ref[rows,:PAIR] = turn_back(acc_ref[rows,:PAIR],cosk_ref[...],sink_ref[...]).astype(jnp.bfloat16)
            gkv_ref[rows,PAIR:] = acc_ref[rows,PAIR:].astype(jnp.bfloat16)

def attend_backward(win, queries, key_values, grads, totals, rope_q, rope_k, span, length):
    tokens,width = queries.shape
    pairs = width//PAIR
    blocks = tokens//span
    all_rows = key_values.shape[0]
    return pl.pallas_call(
        backward_kernel,
        grid_spec=pltpu.PrefetchScalarGridSpec(
            num_scalar_prefetch=1, grid=(pairs,blocks),
            in_specs=[pl.BlockSpec((span,PAIR),lambda p,b,w:(b,p)),
                      pl.BlockSpec((length,2*PAIR),lambda p,b,w:(w[b],p)),
                      pl.BlockSpec((span,PAIR),lambda p,b,w:(b,p)),
                      pl.BlockSpec((1,1,8,span),lambda p,b,w:(p,b,0,0)),
                      pl.BlockSpec((span,PAIR),lambda p,b,w:(b,0)),
                      pl.BlockSpec((span,PAIR),lambda p,b,w:(b,0)),
                      pl.BlockSpec((length,PAIR),lambda p,b,w:(0,0)),
                      pl.BlockSpec((length,PAIR),lambda p,b,w:(0,0))],
            out_specs=[pl.BlockSpec((span,PAIR),lambda p,b,w:(b,p)),
                       pl.BlockSpec((all_rows,2*PAIR),lambda p,b,w:(0,p))],
            scratch_shapes=[pltpu.VMEM((all_rows,2*PAIR),jnp.float32)]),
        out_shape=[jax.ShapeDtypeStruct((tokens,width),jnp.bfloat16),
                   jax.ShapeDtypeStruct((all_rows,2*width),jnp.bfloat16)],
        compiler_params=pltpu.CompilerParams(vmem_limit_bytes=60*MB),
        cost_estimate=pl.CostEstimate(flops=10*tokens*length*width,bytes_accessed=32*MB,transcendentals=tokens*length*width//HEAD_DIM),
        name="attend_backward",
    )(win,queries,key_values,grads,totals,*rope_q,*rope_k)


def cost(flops, moved):
    return pl.CostEstimate(flops=flops, bytes_accessed=moved, transcendentals=0)


def gate_kernel(x_ref, gate_w_ref, up_w_ref, gate_ref, up_ref, hidden_ref):
    gate = jnp.dot(x_ref[...], gate_w_ref[...], preferred_element_type=jnp.float32)
    up = jnp.dot(x_ref[...], up_w_ref[...], preferred_element_type=jnp.float32)
    gate_ref[...] = gate
    up_ref[...] = up
    hidden_ref[...] = (gate * jax.nn.sigmoid(gate) * up).astype(jnp.bfloat16)


def gate_forward(x, weights, hidden_width, wide=512, tile=None):
    tokens, width = x.shape
    tile = tile or tokens
    shift = hidden_width // wide
    spot = lambda n, m: (m, n)
    return pl.pallas_call(
        gate_kernel,
        grid=(hidden_width // wide, tokens // tile),
        in_specs=[
            pl.BlockSpec((tile, width), lambda n, m: (m, 0)),
            pl.BlockSpec((width, wide), lambda n, m: (0, n)),
            pl.BlockSpec((width, wide), lambda n, m: (0, n + shift)),
        ],
        out_specs=[pl.BlockSpec((tile, wide), spot)] * 3,
        out_shape=[
            jax.ShapeDtypeStruct((tokens, hidden_width), jnp.float32),
            jax.ShapeDtypeStruct((tokens, hidden_width), jnp.float32),
            jax.ShapeDtypeStruct((tokens, hidden_width), jnp.bfloat16),
        ],
        compiler_params=pltpu.CompilerParams(vmem_limit_bytes=48 * MB),
        cost_estimate=cost(4 * tokens * width * hidden_width, 10 * tokens * hidden_width + 4 * width * hidden_width),
        name="gate_forward",
    )(x, weights, weights)


def down_kernel(hidden_ref, w_ref, base_ref, out_ref):
    part = jnp.dot(hidden_ref[...], w_ref[...], preferred_element_type=jnp.float32)

    @pl.when(pl.program_id(1) == 0)
    def _():
        out_ref[...] = base_ref[...] + part

    @pl.when(pl.program_id(1) > 0)
    def _():
        out_ref[...] += part


def down_forward(hidden, weights, base, first, tile=None):
    tokens, width = base.shape
    tile = tile or tokens
    folds = hidden.shape[1] // width
    shift = first // width
    return pl.pallas_call(
        down_kernel,
        grid=(tokens // tile, folds),
        in_specs=[
            pl.BlockSpec((tile, width), lambda m, f: (m, f)),
            pl.BlockSpec((width, width), lambda m, f: (0, f + shift)),
            pl.BlockSpec((tile, width), lambda m, f: (m, 0)),
        ],
        out_specs=pl.BlockSpec((tile, width), lambda m, f: (m, 0)),
        out_shape=jax.ShapeDtypeStruct((tokens, width), jnp.float32),
        compiler_params=pltpu.CompilerParams(vmem_limit_bytes=48 * MB),
        cost_estimate=cost(2 * tokens * width * folds * width, 12 * tokens * width + 2 * folds * width * width),
        name="down_forward",
    )(hidden, weights, base)


def gate_back_kernel(grad_ref, w_ref, gate_ref, up_ref, grad_gate_ref, grad_up_ref):
    grad_hidden = lax.dot_general(grad_ref[...], w_ref[...], dims(1, 1), preferred_element_type=jnp.float32)
    gate = gate_ref[...]
    sigmoid = jax.nn.sigmoid(gate)
    grad_up_ref[...] = (grad_hidden * (gate * sigmoid)).astype(jnp.bfloat16)
    grad_gate_ref[...] = (
        grad_hidden * up_ref[...] * (sigmoid * (1.0 + gate * (1.0 - sigmoid)))
    ).astype(jnp.bfloat16)


def gate_backward(grad, weights, gate, up, first, wide=512, tile=None):
    tokens, width = grad.shape
    tile = tile or tokens
    hidden_width = gate.shape[1]
    per = width // wide
    shift = first // width
    spot = lambda n, m: (m, n)
    return pl.pallas_call(
        gate_back_kernel,
        grid=(hidden_width // wide, tokens // tile),
        in_specs=[
            pl.BlockSpec((tile, width), lambda n, m: (m, 0)),
            pl.BlockSpec((wide, width), lambda n, m: (lax.rem(n, per), n // per + shift)),
            pl.BlockSpec((tile, wide), spot),
            pl.BlockSpec((tile, wide), spot),
        ],
        out_specs=[pl.BlockSpec((tile, wide), spot)] * 2,
        out_shape=[jax.ShapeDtypeStruct((tokens, hidden_width), jnp.bfloat16)] * 2,
        compiler_params=pltpu.CompilerParams(vmem_limit_bytes=48 * MB),
        cost_estimate=cost(2 * tokens * width * hidden_width, 12 * tokens * hidden_width + 2 * width * hidden_width),
        name="gate_backward",
    )(grad, weights, gate, up)


def swap_rows(out, value, order):
    outer, inner = order
    rows = value.shape[0] // (outer * inner)
    for i in range(outer):
        for j in range(inner):
            spot, source = (j * outer + i) * rows, (i * inner + j) * rows
            out[spot : spot + rows, :] = value[source : source + rows, :]


def weight_kernel(sides, order, left_ref, *refs):
    out_ref, turned = refs[-2], refs[-1]

    @pl.when(pl.program_id(0) == 0)
    def _():
        swap_rows(turned, left_ref[...].T, order)

    per = pl.num_programs(0) // sides
    for side in range(sides):
        @pl.when(pl.program_id(0) // per == side)
        def _():
            out_ref[...] = jnp.dot(
                turned[...], refs[side][...], preferred_element_type=jnp.float32
            ).astype(jnp.bfloat16)


def weight_grad(left, rights, order, wide=1024, total=None, filled=None, first=0):
    tokens, width = left.shape
    sides, columns = len(rights), rights[0].shape[1]
    per = columns // wide
    return pl.pallas_call(
        functools.partial(weight_kernel, sides, order),
        grid=(sides * per,),
        in_specs=[pl.BlockSpec((tokens, width), lambda n: (0, 0))]
        + [
            pl.BlockSpec((tokens, wide), lambda n, s=s: (0, jnp.clip(n - s * per, 0, per - 1)))
            for s in range(sides)
        ]
        + [pl.BlockSpec(memory_space=pl.ANY)] * (filled is not None),
        out_specs=pl.BlockSpec(
            (pl.Element(width), pl.Element(wide)),
            lambda n: (0, pl.multiple_of(first + n * wide, PAIR)),
        ),
        out_shape=jax.ShapeDtypeStruct(
            filled.shape if filled is not None else (width, total or sides * columns), jnp.bfloat16
        ),
        input_output_aliases={} if filled is None else {1 + sides: 0},
        scratch_shapes=[pltpu.VMEM((width, tokens), jnp.bfloat16)],
        compiler_params=pltpu.CompilerParams(vmem_limit_bytes=56 * MB),
        cost_estimate=cost(2 * tokens * width * sides * columns, 4 * (tokens + width) * sides * columns),
        name="weight_grad",
    )(left, *rights, *([] if filled is None else [filled]))


def down_grad_kernel(order, hidden_ref, grad_ref, filled_ref, out_ref):
    value = lax.dot_general(
        hidden_ref[...], grad_ref[...], dims(0, 0), preferred_element_type=jnp.float32
    )
    swap_rows(out_ref, value.astype(jnp.bfloat16), order)


def down_grad(hidden, grad, filled, first, order):
    tokens, width = grad.shape
    folds = hidden.shape[1] // width
    return pl.pallas_call(
        functools.partial(down_grad_kernel, order),
        grid=(folds,),
        in_specs=[
            pl.BlockSpec((tokens, width), lambda f: (0, f)),
            pl.BlockSpec((tokens, width), lambda f: (0, 0)),
            pl.BlockSpec(memory_space=pl.ANY),
        ],
        out_specs=pl.BlockSpec(
            (pl.Element(width), pl.Element(width)), lambda f: (0, pl.multiple_of(first + f * width, PAIR))
        ),
        out_shape=jax.ShapeDtypeStruct(filled.shape, jnp.bfloat16),
        input_output_aliases={2: 0},
        compiler_params=pltpu.CompilerParams(vmem_limit_bytes=48 * MB),
        cost_estimate=cost(2 * tokens * width * folds * width, 4 * tokens * folds * width),
        name="down_grad",
    )(hidden, grad, filled)


def input_kernel(sides, first_ref, *refs):
    grads, weights, out_ref = refs[:sides], refs[sides:2 * sides], refs[2 * sides]
    part = None
    for grad_ref, w_ref in zip(grads, weights):
        term = lax.dot_general(grad_ref[...], w_ref[...], dims(1, 1), preferred_element_type=jnp.float32)
        part = term if part is None else part + term

    @pl.when(pl.program_id(1) == 0)
    def _():
        out_ref[...] = part

    @pl.when(pl.program_id(1) > 0)
    def _():
        out_ref[...] += part


def input_grad(grads, weights, firsts, wide=1024, tile=None):
    tokens, columns = grads[0].shape
    width = weights.shape[0]
    tile = tile or tokens
    sides = len(grads)
    return pl.pallas_call(
        lambda *refs: input_kernel(sides, None, *refs),
        grid=(tokens // tile, columns // wide),
        in_specs=[pl.BlockSpec((tile, wide), lambda m, k: (m, k))] * sides
        + [
            pl.BlockSpec((width, wide), lambda m, k, first=first: (0, k + first // wide))
            for first in firsts
        ],
        out_specs=pl.BlockSpec((tile, width), lambda m, k: (m, 0)),
        out_shape=jax.ShapeDtypeStruct((tokens, width), jnp.float32),
        compiler_params=pltpu.CompilerParams(vmem_limit_bytes=48 * MB),
        cost_estimate=cost(2 * sides * tokens * width * columns, 2 * sides * (tokens + width) * columns),
        name="input_grad",
    )(*grads, *([weights] * sides))


def onehot_block(ids, first, wide):
    columns = lax.broadcasted_iota(jnp.int32, (ids.shape[0], wide), 1) + first
    return (ids == columns).astype(jnp.float32).astype(jnp.bfloat16)


def embed_kernel(ids_ref, table_ref, out_ref, onehot_ref):
    wide = table_ref.shape[1]
    step = pl.program_id(1)
    onehot = onehot_block(ids_ref[...], step * wide, wide)
    onehot_ref[...] = onehot
    part = lax.dot_general(onehot, table_ref[...], dims(1, 1), preferred_element_type=jnp.float32)

    @pl.when(step == 0)
    def _():
        out_ref[...] = part

    @pl.when(step > 0)
    def _():
        out_ref[...] += part


def embed(ids, weights, first, columns, tile):
    tokens, width = ids.shape[0], weights.shape[0]
    wide = max(PAIR * i for i in range(1, 12) if columns % (PAIR * i) == 0)
    return pl.pallas_call(
        embed_kernel,
        grid=(tokens // tile, columns // wide),
        in_specs=[
            pl.BlockSpec((tile, 1), lambda m, k: (m, 0)),
            pl.BlockSpec(
                (pl.Element(width), pl.Element(wide)),
                lambda m, k: (0, pl.multiple_of(first + k * wide, PAIR)),
            ),
        ],
        out_specs=[
            pl.BlockSpec((tile, width), lambda m, k: (m, 0)),
            pl.BlockSpec((tile, wide), lambda m, k: (m, k)),
        ],
        out_shape=[
            jax.ShapeDtypeStruct((tokens, width), jnp.float32),
            jax.ShapeDtypeStruct((tokens, columns), jnp.bfloat16),
        ],
        compiler_params=pltpu.CompilerParams(vmem_limit_bytes=56 * MB),
        cost_estimate=cost(
            2 * tokens * width * columns, 4 * tokens * width + 2 * (width + tokens) * columns
        ),
        name="embed",
    )(ids, weights)


def grid_sizes():
    cores = 2
    across = lax.axis_size("seq") // cores
    return lax.axis_size("dp") // across, across, across, cores


def column_chunks(columns, count):
    lanes = columns // PAIR
    widths = [(lanes // count + (i < lanes % count)) * PAIR for i in range(count)]
    starts = [sum(widths[:i]) for i in range(count)]
    return [pl.ds(start, wide) for start, wide in zip(starts, widths)]


class Place:
    def __init__(self, sizes):
        self.sizes = dict(zip("zyxc", sizes))
        dp, seq = lax.axis_index("dp"), lax.axis_index("seq")
        self.at = {
            "z": dp // sizes[1],
            "y": lax.rem(dp, sizes[1]),
            "x": seq // sizes[3],
            "c": lax.rem(seq, sizes[3]),
        }

    def other(self, axis, step):
        return lax.rem(self.at[axis] + step, self.sizes[axis])

    def device(self, axis, step):
        at = dict(self.at)
        at[axis] = self.other(axis, step)
        return (at["z"] * self.sizes["y"] + at["y"], at["x"] * self.sizes["c"] + at["c"])

    def steps(self, axis):
        return range(1, self.sizes[axis])

    def greet(self):
        barrier = pltpu.get_barrier_semaphore()
        peers = 0
        for axis in "cxyz":
            for step in self.steps(axis):
                pl.semaphore_signal(barrier, inc=1, device_id=self.device(axis, step), device_id_type=MESH)
                peers += 1
        pl.semaphore_wait(barrier, peers)


def scatter_kernel(sizes, chunks, g_ref, out_ref, own, one, two, three, four, load_sem, send_sem, recv_sem):
    n_z, n_y, n_x, n_c = sizes
    place = Place(sizes)
    at = place.at
    f32 = jnp.float32
    started = []

    def send(src, dst, chunk, slot, axis, step):
        copy = pltpu.make_async_remote_copy(
            src_ref=src, dst_ref=dst, send_sem=send_sem.at[chunk, slot], recv_sem=recv_sem.at[chunk, slot],
            device_id=place.device(axis, step), device_id_type=MESH)
        copy.start()
        started.append(copy)
        return copy

    place.greet()
    loads, cores = [], []
    for chunk, cols in enumerate(chunks):
        load = pltpu.make_async_copy(g_ref.at[:, :, :, at["c"], :, cols], own.at[:, :, :, :, cols], load_sem.at[chunk])
        load.start()
        loads.append(load)
        cores.append(send(g_ref.at[:, :, :, place.other("c", 1), :, cols], one.at[:, :, :, :, cols], chunk, 0, "c", 1))

    waits = {}

    def first(chunk, cols):
        loads[chunk].wait()
        cores[chunk].wait_recv()

        def add(i, carry):
            z, rest = i // (n_y * n_x), lax.rem(i, n_y * n_x)
            y, x = rest // n_x, lax.rem(rest, n_x)
            total = own[z, y, x, :, cols].astype(f32) + one[z, y, x, :, cols].astype(f32)
            one[z, y, x, :, cols] = total.astype(jnp.bfloat16)
            return carry

        lax.fori_loop(0, n_z * n_y * n_x, add, 0)
        axis = "xy"[chunk % 2]
        waits[chunk, 1] = []
        for step in place.steps(axis):
            spot = place.other(axis, step)
            src = one.at[:, :, spot, :, cols] if axis == "x" else one.at[:, spot, :, :, cols]
            waits[chunk, 1].append(send(src, two.at[step - 1, :, :, :, cols], chunk, step, axis, step))

    def second(chunk, cols):
        for copy in waits[chunk, 1]:
            copy.wait_recv()
        axis = "xy"[chunk % 2]
        kept = n_y if axis == "x" else n_x

        def add(i, carry):
            z, k = i // kept, lax.rem(i, kept)
            mine = one[z, k, at["x"], :, cols] if axis == "x" else one[z, at["y"], k, :, cols]
            total = mine.astype(f32)
            for step in place.steps(axis):
                total = total + two[step - 1, z, k, :, cols].astype(f32)
            two[0, z, k, :, cols] = total.astype(jnp.bfloat16)
            return carry

        lax.fori_loop(0, n_z * kept, add, 0)
        axis = "yx"[chunk % 2]
        waits[chunk, 2] = []
        for step in place.steps(axis):
            src = two.at[0, :, place.other(axis, step), :, cols]
            slot = max(n_x, n_y) - 1 + step
            waits[chunk, 2].append(send(src, three.at[step - 1, :, :, cols], chunk, slot, axis, step))

    def third(chunk, cols):
        for copy in waits[chunk, 2]:
            copy.wait_recv()
        axis = "yx"[chunk % 2]

        def add(z, carry):
            total = two[0, z, at[axis], :, cols].astype(f32)
            for step in place.steps(axis):
                total = total + three[step - 1, z, :, cols].astype(f32)
            three[0, z, :, cols] = total.astype(jnp.bfloat16)
            return carry

        lax.fori_loop(0, n_z, add, 0)
        waits[chunk, 3] = []
        for step in place.steps("z"):
            src = three.at[0, place.other("z", step), :, cols]
            slot = 2 * (max(n_x, n_y) - 1) + step
            waits[chunk, 3].append(send(src, four.at[step - 1, :, cols], chunk, slot, "z", step))

    def fourth(chunk, cols):
        for copy in waits[chunk, 3]:
            copy.wait_recv()
        total = three[0, at["z"], :, cols].astype(f32)
        for step in place.steps("z"):
            total = total + four[step - 1, :, cols].astype(f32)
        out_ref[:, cols] = total

    pairs = (len(chunks) + 1) // 2
    for tick in range(pairs + 3):
        for late, stage in enumerate((first, second, third, fourth)):
            for chunk in (2 * (tick - late), 2 * (tick - late) + 1):
                if 0 <= tick - late and chunk < len(chunks):
                    stage(chunk, chunks[chunk])
    for copy in started:
        copy.wait_send()


def scatter_sum_direct(grads, collective_id, count=8):
    sizes = grid_sizes()
    n_z, n_y, n_x, n_c = sizes
    total, columns = grads.shape
    rows = total // (n_z * n_y * n_x * n_c)
    most = max(n_x, n_y)
    slots = 1 + 2 * (most - 1) + n_z - 1
    low = jnp.bfloat16
    chunks = column_chunks(columns, count)
    return pl.pallas_call(
        functools.partial(scatter_kernel, sizes, chunks),
        in_specs=[pl.BlockSpec(memory_space=pl.ANY)],
        out_specs=pl.BlockSpec(memory_space=pltpu.VMEM),
        out_shape=jax.ShapeDtypeStruct((rows, columns), jnp.float32),
        scratch_shapes=[
            pltpu.VMEM((n_z, n_y, n_x, rows, columns), low),
            pltpu.VMEM((n_z, n_y, n_x, rows, columns), low),
            pltpu.VMEM((most - 1, n_z, most, rows, columns), low),
            pltpu.VMEM((most - 1, n_z, rows, columns), low),
            pltpu.VMEM((n_z - 1, rows, columns), low),
            pltpu.SemaphoreType.DMA((count,)),
            pltpu.SemaphoreType.DMA((count, slots)),
            pltpu.SemaphoreType.DMA((count, slots)),
        ],
        compiler_params=pltpu.CompilerParams(
            collective_id=collective_id, has_side_effects=True, vmem_limit_bytes=48 * MB),
        cost_estimate=pl.CostEstimate(flops=2 * total * columns, bytes_accessed=2 * total * columns, transcendentals=0),
        name="scatter_sum",
    )(grads.reshape(n_z, n_y, n_x, n_c, rows, columns))


def total_kernel(sizes, x_ref, out_ref, z_slots, y_slots, x_slots, c_slots, send_sem, recv_sem):
    place = Place(sizes)
    slots = {"z": z_slots, "y": y_slots, "x": x_slots, "c": c_slots}
    place.greet()
    total = x_ref[...]
    started = []
    for turn_at, axis in enumerate("cxyz"):
        held, me = slots[axis], place.at[axis]
        held[me] = total
        arriving = []
        for step in place.steps(axis):
            copy = pltpu.make_async_remote_copy(
                src_ref=held.at[me], dst_ref=held.at[me],
                send_sem=send_sem.at[turn_at, step], recv_sem=recv_sem.at[turn_at, step],
                device_id=place.device(axis, step), device_id_type=MESH)
            copy.start()
            arriving.append(copy)
        for copy in arriving:
            copy.wait_recv()
        started += arriving
        total = held[0]
        for spot in range(1, place.sizes[axis]):
            total = total + held[spot]
    out_ref[...] = total
    for copy in started:
        copy.wait_send()


def total_over_all(values, collective_id):
    sizes = grid_sizes()
    row = lax.broadcasted_iota(jnp.int32, (8, PAIR), 0)
    tile = jnp.zeros((8, PAIR), jnp.float32)
    for i, value in enumerate(values):
        tile = jnp.where(row == i, value, tile)
    total = pl.pallas_call(
        functools.partial(total_kernel, sizes),
        in_specs=[pl.BlockSpec(memory_space=pltpu.VMEM)],
        out_specs=pl.BlockSpec(memory_space=pltpu.VMEM),
        out_shape=jax.ShapeDtypeStruct(tile.shape, jnp.float32),
        scratch_shapes=[pltpu.VMEM((size, 8, PAIR), jnp.float32) for size in sizes]
        + [pltpu.SemaphoreType.DMA((4, max(sizes)))] * 2,
        compiler_params=pltpu.CompilerParams(collective_id=collective_id, has_side_effects=True),
        name="total_over_all",
    )(tile)
    return [total[i, 0] for i in range(len(values))]


def gather_kernel(sizes, pieces, *refs):
    load_sem, send_sem, recv_sem = refs[-3:]
    arrays = (len(refs) - 3) // 2
    n_z, n_y, n_x, n_c = sizes
    place = Place(sizes)
    at = place.at
    started = []
    waits = {}
    most = max(n_x, n_y)

    def send(ref, chunk, slot, axis, step):
        copy = pltpu.make_async_remote_copy(
            src_ref=ref, dst_ref=ref, send_sem=send_sem.at[chunk, slot], recv_sem=recv_sem.at[chunk, slot],
            device_id=place.device(axis, step), device_id_type=MESH)
        copy.start()
        started.append(copy)
        return copy

    loads = []
    for chunk, (array, cols) in enumerate(pieces):
        load = pltpu.make_async_copy(
            refs[array].at[:, cols], refs[arrays + array].at[at["z"], at["y"], at["x"], at["c"], :, cols], load_sem.at[chunk])
        load.start()
        loads.append(load)
    place.greet()

    def first(chunk, out_ref, cols):
        loads[chunk].wait()
        ref = out_ref.at[at["z"], at["y"], at["x"], at["c"], :, cols]
        waits[chunk, 0] = [send(ref, chunk, step - 1, "z", step) for step in place.steps("z")]

    def second(chunk, out_ref, cols):
        for copy in waits[chunk, 0]:
            copy.wait_recv()
        axis = "xy"[chunk % 2]
        ref = out_ref.at[:, at["y"], at["x"], at["c"], :, cols]
        waits[chunk, 1] = [send(ref, chunk, n_z - 2 + step, axis, step) for step in place.steps(axis)]

    def third(chunk, out_ref, cols):
        for copy in waits[chunk, 1]:
            copy.wait_recv()
        axis = "yx"[chunk % 2]
        if axis == "y":
            ref = out_ref.at[:, at["y"], :, at["c"], :, cols]
        else:
            ref = out_ref.at[:, :, at["x"], at["c"], :, cols]
        waits[chunk, 2] = [send(ref, chunk, n_z - 2 + most - 1 + step, axis, step) for step in place.steps(axis)]

    def fourth(chunk, out_ref, cols):
        for copy in waits[chunk, 2]:
            copy.wait_recv()
        ref = out_ref.at[:, :, :, at["c"], :, cols]
        waits[chunk, 3] = [send(ref, chunk, n_z - 2 + 2 * (most - 1) + 1, "c", 1)]

    pairs = (len(pieces) + 1) // 2
    for tick in range(pairs + 3):
        for late, stage in enumerate((first, second, third, fourth)):
            for chunk in (2 * (tick - late), 2 * (tick - late) + 1):
                if 0 <= tick - late and chunk < len(pieces):
                    array, cols = pieces[chunk]
                    stage(chunk, refs[arrays + array], cols)
    for chunk in range(len(pieces)):
        for copy in waits[chunk, 3]:
            copy.wait_recv()
    for copy in started:
        copy.wait_send()


def gather_rows(arrays, counts, collective_id):
    sizes = grid_sizes()
    n_z, n_y, n_x, n_c = sizes
    slots = n_z - 1 + 2 * (max(n_x, n_y) - 1) + 1
    pieces = [
        (i, cols)
        for i, (array, count) in enumerate(zip(arrays, counts))
        for cols in column_chunks(array.shape[1], count)
    ]
    outs = pl.pallas_call(
        functools.partial(gather_kernel, sizes, pieces),
        in_specs=[pl.BlockSpec(memory_space=pl.ANY)] * len(arrays),
        out_specs=[pl.BlockSpec(memory_space=pl.ANY)] * len(arrays),
        out_shape=[jax.ShapeDtypeStruct(sizes + array.shape, array.dtype) for array in arrays],
        scratch_shapes=[
            pltpu.SemaphoreType.DMA((len(pieces),)),
            pltpu.SemaphoreType.DMA((len(pieces), slots)),
            pltpu.SemaphoreType.DMA((len(pieces), slots)),
        ],
        compiler_params=pltpu.CompilerParams(collective_id=collective_id, has_side_effects=True),
        name="gather_rows",
    )(*arrays)
    devices = n_z * n_y * n_x * n_c
    return [out.reshape(devices * array.shape[0], -1) for out, array in zip(outs, arrays)]


from jax.sharding import PartitionSpec as P

AXES = ("dp", "seq")
beta_one = 0.9
beta_two = 0.999
adam_eps = 1e-08
weight_decay = 0.01
learn_rate = 0.02
norm_rate = 0.2
ema_decay = 0.7
norm_eps = 1e-05


def project_kernel(roped, x_ref, w_ref, cos_ref, sin_ref, out_ref):
    product = jnp.dot(x_ref[...], w_ref[...], preferred_element_type=jnp.float32)
    for part in range(product.shape[1] // PAIR):
        piece = product[:, part * PAIR : (part + 1) * PAIR]
        if roped == "all":
            piece = turn(piece, cos_ref[...], sin_ref[...]).astype(jnp.bfloat16)
            piece = piece * jnp.bfloat16(HEAD_DIM**-0.5)
        elif part % 2 == 0:
            piece = turn(piece, cos_ref[...], sin_ref[...])
        out_ref[:, part * PAIR : (part + 1) * PAIR] = piece.astype(jnp.bfloat16)


def project(x, weights, first_column, columns, rope, tile, roped):
    tokens, width = x.shape
    wide = 512
    repeat = rope[0].shape[0] // tile
    return pl.pallas_call(
        functools.partial(project_kernel, roped),
        grid=(tokens // tile, columns // wide),
        in_specs=[
            pl.BlockSpec((tile, width), lambda m, n: (m, 0)),
            pl.BlockSpec((width, wide), lambda m, n: (0, n + first_column // wide)),
            pl.BlockSpec((tile, PAIR), lambda m, n: (lax.rem(m, repeat), 0)),
            pl.BlockSpec((tile, PAIR), lambda m, n: (lax.rem(m, repeat), 0)),
        ],
        out_specs=pl.BlockSpec((tile, wide), lambda m, n: (m, n)),
        out_shape=jax.ShapeDtypeStruct((tokens, columns), jnp.bfloat16),
        compiler_params=pltpu.CompilerParams(vmem_limit_bytes=40 * MB),
        cost_estimate=pl.CostEstimate(
            flops=2 * tokens * width * columns,
            bytes_accessed=2 * (tokens * width + width * columns + tokens * columns),
            transcendentals=0,
        ),
        name="project",
    )(x, weights, *rope)


def rope_tables(positions):
    half = HEAD_DIM // 2
    inverse = 10000.0 ** (-jnp.arange(half).astype(jnp.float32) / half)
    angles = positions.astype(jnp.float32)[:, None] * inverse[None, :]
    copies = PAIR // half
    return (jnp.tile(jnp.cos(angles), (1, copies)), jnp.tile(jnp.sin(angles), (1, copies)))


def norm_forward(values, gain, shift):
    centre = values - jnp.mean(values, axis=-1, keepdims=True)
    spread = jnp.mean(centre * centre, axis=-1, keepdims=True)
    scale = lax.rsqrt(spread + norm_eps)
    unit = centre * scale
    return (unit * gain + shift).astype(jnp.bfloat16), unit, scale


def norm_backward(grad, unit, scale, gain):
    grad_gain = jnp.sum(grad * unit, axis=0)
    grad_shift = jnp.sum(grad, axis=0)
    scaled = grad * gain
    inner = jnp.mean(scaled * unit, axis=-1, keepdims=True)
    outer = jnp.mean(scaled, axis=-1, keepdims=True)
    return scale * (scaled - outer - unit * inner), grad_gain, grad_shift


def product(left, right, left_dim=1, right_dim=0, precision=None):
    return lax.dot_general(
        left, right, dims(left_dim, right_dim), precision=precision,
        preferred_element_type=jnp.float32,
    )


def pair_columns(weights):
    rows, columns = weights.shape
    width = columns // 2
    return weights.reshape(rows, 2, width // PAIR, PAIR).transpose(0, 2, 1, 3).reshape(rows, columns)


def unpair_columns(weights):
    rows, columns = weights.shape
    width = columns // 2
    return weights.reshape(rows, width // PAIR, 2, PAIR).transpose(0, 2, 1, 3).reshape(rows, columns)


def scatter_sum(grads):
    part = lax.psum_scatter(grads, "seq", scatter_dimension=0, tiled=True)
    return lax.psum_scatter(part, "dp", scatter_dimension=0, tiled=True)


def on_device(
    token_ids,
    mask_rows,
    mask_labels,
    mask_counts,
    step_count,
    vocab_tables,
    attention,
    feed_in,
    feed_out,
    norm_params,
    first_tables,
    first_attention,
    first_feed_in,
    first_feed_out,
    first_norms,
    second_tables,
    second_attention,
    second_feed_in,
    second_feed_out,
    second_norms,
    ema_tables,
    ema_attention,
    ema_feed_in,
    ema_feed_out,
    ema_norms,
):
    master = (vocab_tables, attention, feed_in, feed_out, norm_params)
    firsts = (first_tables, first_attention, first_feed_in, first_feed_out, first_norms)
    seconds = (second_tables, second_attention, second_feed_in, second_feed_out, second_norms)
    averages = (ema_tables, ema_attention, ema_feed_in, ema_feed_out, ema_norms)
    group_rates = (learn_rate, learn_rate, learn_rate, learn_rate, norm_rate)
    low = jnp.bfloat16

    shards = lax.axis_size("seq")
    devices = shards * lax.axis_size("dp")
    windows, span = token_ids.shape
    slots = mask_rows.shape[1]
    vocab = vocab_tables.shape[2]
    padded = vocab + -vocab % PAIR
    rows, columns = attention.shape
    width = columns // 4
    hidden_width = feed_in.shape[1] // 2
    folds = feed_out.shape[0] // rows
    length = span * shards
    spot = lax.axis_index("seq")

    tables_sent = jnp.pad(vocab_tables, ((0, 0), (0, 0), (0, padded - vocab)))
    early_sent = jnp.concatenate(
        [
            attention[:, :width],
            pair_columns(attention[:, width : 3 * width]),
            attention[:, 3 * width :],
            tables_sent[0],
        ],
        axis=1,
    ).astype(low)
    in_sent = feed_in.reshape(rows, 2, hidden_width // folds, folds).transpose(0, 1, 3, 2)
    late_sent = jnp.concatenate(
        [
            in_sent.reshape(rows, 2 * hidden_width),
            feed_out.reshape(rows, folds * width),
            tables_sent[1],
        ],
        axis=1,
    ).astype(low)

    small = jnp.concatenate(
        [
            token_ids.reshape(-1).astype(jnp.float32),
            mask_rows.reshape(-1).astype(jnp.float32),
            mask_labels.reshape(-1).astype(jnp.float32),
            mask_counts.reshape(-1).astype(jnp.float32),
            norm_params.astype(low).astype(jnp.float32).reshape(-1),
        ]
    )
    small = jnp.pad(small, (0, -small.shape[0] % (8 * PAIR))).reshape(8, -1)
    late = lax.all_gather(late_sent, AXES, axis=0, tiled=True)
    small_all, early = gather_rows((small, early_sent), (1, 15), 3)
    small_all = small_all.reshape(devices, -1)
    out_w = early[:, 3 * width : columns]
    head_w = late[:, 2 * hidden_width + folds * width :]
    cuts = [windows * span, windows * slots, windows * slots, windows]
    marks = [sum(cuts[:i]) for i in range(len(cuts) + 1)]
    gains = small_all[:, marks[4] : marks[4] + rows * 6].reshape(devices * rows, 6)
    count = jnp.sum(small_all[:, marks[3] : marks[4]])
    group = lax.dynamic_slice_in_dim(small_all, lax.axis_index("dp") * shards, shards, axis=0)

    def in_order(first, last):
        piece = group[:, first:last].reshape(shards, windows, -1)
        return piece.transpose(1, 0, 2).reshape(windows * shards, -1)

    ids = in_order(marks[0], marks[1]).astype(jnp.int32)
    block = spot * windows + jnp.arange(windows, dtype=jnp.int32)

    def mine(first, last):
        return lax.dynamic_slice_in_dim(in_order(first, last), spot * windows, windows, axis=0)

    own_rows = mine(marks[1], marks[2]).astype(jnp.int32)
    own_labels = mine(marks[2], marks[3]).astype(jnp.int32).reshape(-1)
    own_counts = mine(marks[3], marks[4])
    live = (jnp.arange(slots, dtype=jnp.float32)[None, :] < own_counts).astype(jnp.float32)
    live = live.reshape(-1)

    base = jnp.minimum(spot * windows // shards, windows - 2)
    wins = block // shards - base
    offset = (spot * windows - base * shards) * span
    ids_two = lax.dynamic_slice_in_dim(ids, base * shards, 2 * shards, axis=0).reshape(-1)
    positions = ((block % shards)[:, None] * span + jnp.arange(span, dtype=jnp.int32)).reshape(-1)
    rope_q = rope_tables(positions)
    rope_k = rope_tables(jnp.arange(length, dtype=jnp.int32))
    tokens = windows * span

    def own(values):
        return lax.dynamic_slice_in_dim(values, offset, tokens, axis=0)

    embedded_two, onehot = embed(ids_two[:, None], early, columns, padded, length)
    normed_one, unit_one, scale_one = norm_forward(embedded_two, gains[:, 0], gains[:, 1])
    normed_own = own(normed_one)
    queries = project(normed_own, early, 0, width, rope_q, tokens, "all")
    key_values = project(normed_one, early, width, 2 * width, rope_k, length, "half")
    mixture, totals = attend_forward(wins, queries, key_values, span, length)
    after_attn = own(embedded_two) + product(mixture, out_w)

    normed_two, unit_two, scale_two = norm_forward(after_attn, gains[:, 2], gains[:, 3])
    gate, up, hidden = gate_forward(normed_two, late, hidden_width)
    after_feed = down_forward(hidden, late, after_attn, 2 * hidden_width)

    pick = (own_rows[:, :, None] == jnp.arange(span, dtype=jnp.int32)).astype(jnp.float32)
    selected = jnp.einsum(
        "wsp,wpd->wsd", pick, after_feed.reshape(windows, span, width),
        precision=lax.Precision.HIGHEST, preferred_element_type=jnp.float32,
    ).reshape(windows * slots, width)
    normed_final, unit_final, scale_final = norm_forward(selected, gains[:, 4], gains[:, 5])
    column = jnp.arange(padded, dtype=jnp.int32)[None, :]
    logits = jnp.where(column < vocab, product(normed_final, head_w), -jnp.inf)
    log_total = jax.nn.logsumexp(logits, axis=-1)
    wanted = own_labels[:, None] == column
    picked = jnp.sum(jnp.where(wanted, logits, 0.0), axis=-1)
    loss_part = jnp.sum(live * (log_total - picked))

    grad_logits = (
        (jnp.exp(logits - log_total[:, None]) - wanted.astype(jnp.float32)) * (live / count)[:, None]
    ).astype(low)
    grad_selected, grad_gain_final, grad_shift_final = norm_backward(
        product(grad_logits, head_w, 1, 1), unit_final, scale_final, gains[:, 4]
    )
    grad_after_feed = jnp.einsum(
        "wsp,wsd->wpd", pick, grad_selected.reshape(windows, slots, width),
        precision=lax.Precision.HIGHEST, preferred_element_type=jnp.float32,
    ).reshape(tokens, width)
    rounded_feed = grad_after_feed.astype(low)
    order = (lax.axis_size("dp"), shards)
    spare = ((0, -grad_logits.shape[0] % PAIR), (0, 0))
    head_wide = max(PAIR * i for i in range(1, 5) if padded % (PAIR * i) == 0)
    everything = padded + folds * width + 2 * hidden_width
    late_grads = weight_grad(
        jnp.pad(normed_final, spare), (jnp.pad(grad_logits, spare),), order, head_wide, everything
    )
    late_grads = down_grad(hidden, rounded_feed, late_grads, padded, order)
    grad_gate, grad_up = gate_backward(rounded_feed, late, gate, up, 2 * hidden_width)
    late_grads = weight_grad(
        normed_two, (grad_gate, grad_up), order, width, everything, late_grads, padded + folds * width
    )
    grad_gate, grad_up, late_grads = lax.optimization_barrier((grad_gate, grad_up, late_grads))
    late_own = scatter_sum(late_grads)

    grad_inner, grad_gain_two, grad_shift_two = norm_backward(
        input_grad((grad_gate, grad_up), late, (0, hidden_width)), unit_two, scale_two, gains[:, 2]
    )
    grad_after_attn = grad_after_feed + grad_inner
    rounded_attn = grad_after_attn.astype(low)
    grad_mixture = product(rounded_attn, out_w, 1, 1).astype(low)
    grad_queries, grad_pairs = attend_backward(
        wins, queries, key_values, grad_mixture, totals, rope_q, rope_k, span, length
    )
    alone = (1, 1)
    early_grads = weight_grad(mixture, (rounded_attn,), alone, width, columns + padded + PAIR, None, 3 * width)
    early_grads = weight_grad(normed_own, (grad_queries,), alone, width, None, early_grads)
    early_grads = weight_grad(normed_one, (grad_pairs,), alone, width, None, early_grads, width)
    grad_normed = product(grad_pairs, early[:, width : 3 * width], 1, 1)
    grad_normed = lax.dynamic_update_slice_in_dim(
        grad_normed, own(grad_normed) + product(grad_queries, early[:, :width], 1, 1), offset, axis=0
    )
    grad_embedded, grad_gain_one, grad_shift_one = norm_backward(
        grad_normed, unit_one, scale_one, gains[:, 0]
    )
    grad_embedded = lax.dynamic_update_slice_in_dim(
        grad_embedded, own(grad_embedded) + grad_after_attn, offset, axis=0
    )
    early_grads = weight_grad(
        grad_embedded.astype(low), (onehot,), alone, head_wide, None, early_grads, columns
    )
    grad_norms = jnp.stack(
        [
            grad_gain_one,
            grad_shift_one,
            grad_gain_two,
            grad_shift_two,
            grad_gain_final,
            grad_shift_final,
        ],
        axis=1,
    )
    grad_norms = jnp.pad(grad_norms, ((0, 0), (0, PAIR - grad_norms.shape[1]))).astype(low)
    early_grads = lax.dynamic_update_slice(early_grads, grad_norms, (0, columns + padded))
    early_own = scatter_sum_direct(early_grads, 1, 16)
    late_own = late_own.astype(jnp.float32)
    in_own = late_own[:, padded + folds * width :].reshape(rows, 2, folds, hidden_width // folds)
    grads = (
        jnp.stack(
            [
                early_own[:, columns : columns + vocab],
                late_own[:, :vocab],
            ],
            axis=0,
        ),
        jnp.concatenate(
            [
                early_own[:, :width],
                unpair_columns(early_own[:, width : 3 * width]),
                early_own[:, 3 * width : columns],
            ],
            axis=1,
        ),
        in_own.transpose(0, 1, 3, 2).reshape(rows, 2 * hidden_width),
        late_own[:, padded : padded + folds * width].reshape(rows * folds, width),
        early_own[:, columns + padded : columns + padded + 6],
    )
    grads = lax.optimization_barrier(grads)
    squares = jnp.zeros((), jnp.float32)
    for grad in grads:
        squares = squares + jnp.sum(grad * grad)
    squares_all, loss_all = total_over_all((squares, loss_part), 2)
    masked_loss = loss_all / count
    total_norm = jnp.sqrt(squares_all)
    limit = (slots * shards * windows * lax.axis_size("dp")) ** (-0.5)
    clip = jnp.minimum(1.0, limit / (total_norm + 1e-06))
    steps = step_count[0].astype(jnp.float32)
    fix_one = 1.0 - beta_one**steps
    fix_two = 1.0 - beta_two**steps
    weights_new, firsts_new, seconds_new, averages_new = ([], [], [], [])
    for weight, grad, first, second, average, step_rate in zip(
        master, grads, firsts, seconds, averages, group_rates
    ):
        scaled = grad * clip
        first_next = beta_one * first + (1.0 - beta_one) * scaled
        second_next = beta_two * second + (1.0 - beta_two) * scaled * scaled
        update = (
            first_next / fix_one / (jnp.sqrt(second_next / fix_two) + adam_eps)
            + weight_decay * weight
        )
        weight_next = weight - step_rate * update
        weights_new.append(weight_next)
        firsts_new.append(first_next)
        seconds_new.append(second_next)
        averages_new.append(ema_decay * average + (1.0 - ema_decay) * weight_next)
    return (masked_loss, total_norm, *weights_new, *firsts_new, *seconds_new, *averages_new)


def solution(mesh):
    split = P(AXES, None)
    tables = P(None, AXES, None)
    weights = (tables, split, split, split, split)
    return jax.shard_map(
        on_device,
        mesh=mesh,
        in_specs=(P("dp", "seq"),) * 4 + (P(),) + weights * 4,
        out_specs=(P(), P()) + weights * 4,
        check_vma=False,
    )
```

```python
import functools
import math
import jax, jax.numpy as jnp
from jax import lax
from jax.experimental import pallas as pl
from jax.experimental.pallas import tpu as pltpu
HEAD_DIM=64
PAIR=128
MB=1<<20
MESH = pl.DeviceIdType.MESH
norm_eps = 1e-05

def dims(a,b): return (((a,),(b,)),((),()))

def low_half(rows):
    lane = lax.broadcasted_iota(jnp.int32,(rows,PAIR),1)
    return lane % HEAD_DIM < HEAD_DIM//2

def turn(x, cosines, sines):
    low = low_half(x.shape[0])
    up = pltpu.roll(x, PAIR-HEAD_DIM//2, 1)
    down = pltpu.roll(x, HEAD_DIM//2, 1)
    return x*cosines + jnp.where(low,-up,down)*sines

def turn_back(g, cosines, sines):
    low = low_half(g.shape[0])
    up = pltpu.roll(g, PAIR-HEAD_DIM//2, 1)
    down = pltpu.roll(g, HEAD_DIM//2, 1)
    return g*cosines + jnp.where(low,up,-down)*sines

def head_mask(head):
    lane = lax.broadcasted_iota(jnp.int32,(1,PAIR),1)
    return (lane//HEAD_DIM==head).astype(jnp.float32).astype(jnp.bfloat16)

def by_head(rows):
    return jnp.concatenate([rows * head_mask(0), rows * head_mask(1)], axis=0)


def own_halves(mixed, span):
    own = [mixed[:HEAD_DIM, :span], mixed[HEAD_DIM:, span:]]
    return jnp.concatenate(own, axis=0).T


def forward_kernel(win_ref, q_ref, kv_ref, mix_ref, total_ref):
    queries = q_ref[...]
    keys = kv_ref[:, :PAIR]
    values = kv_ref[:, PAIR:]
    span = queries.shape[0]
    scores = lax.dot_general(keys, by_head(queries), dims(1, 1), preferred_element_type=jnp.float32)
    top = jnp.max(scores, axis=0, keepdims=True)
    chances = jnp.exp(scores - top)
    total = jnp.sum(chances, axis=0, keepdims=True)
    weights = (chances * (1.0 / total)).astype(jnp.bfloat16)
    mixed = lax.dot_general(values, weights, dims(0, 0), preferred_element_type=jnp.float32)
    mix_ref[...] = own_halves(mixed, span).astype(jnp.bfloat16)
    totals = top + jnp.log(total)
    for head in range(2):
        total_ref[0, 0, head : head + 1, :] = totals[:, head * span : (head + 1) * span]


def attend_forward(win, queries, key_values, span, length):
    tokens,width = queries.shape
    pairs = width//PAIR
    blocks = tokens//span
    return pl.pallas_call(
        forward_kernel,
        grid_spec=pltpu.PrefetchScalarGridSpec(
            num_scalar_prefetch=1, grid=(pairs,blocks),
            in_specs=[pl.BlockSpec((span,PAIR),lambda p,b,w:(b,p)),
                      pl.BlockSpec((length,2*PAIR),lambda p,b,w:(w[b],p))],
            out_specs=[pl.BlockSpec((span,PAIR),lambda p,b,w:(b,p)),
                       pl.BlockSpec((1,1,8,span),lambda p,b,w:(p,b,0,0))]),
        out_shape=[jax.ShapeDtypeStruct((tokens,width),jnp.bfloat16),
                   jax.ShapeDtypeStruct((pairs,blocks,8,span),jnp.float32)],
        compiler_params=pltpu.CompilerParams(vmem_limit_bytes=56*MB),
        cost_estimate=pl.CostEstimate(flops=4*tokens*length*width,bytes_accessed=16*MB,transcendentals=tokens*length*width//HEAD_DIM),
        name="attend_forward",
    )(win,queries,key_values)


def backward_kernel(windows, shards, sizes, chunks, q_ref, kv_ref, grad_ref, total_ref, cosq_ref, sinq_ref, cosk_ref,
                    sink_ref, wire_ref, gq_ref, gkv_ref, own_ref, acc_ref, *scratch):
    block = pl.program_id(1)
    blocks = pl.num_programs(1)
    step = pl.program_id(0) * blocks + block
    length = cosk_ref.shape[0]
    steps = Scatter(sizes, chunks, wire_ref, own_ref, *scratch)

    @pl.when(step == 0)
    def _():
        steps.begin()

    for number in range(steps.ticks):
        @pl.when(step == 2 * number + 1)
        def _():
            steps.tick(number)

    @pl.when(block == 0)
    def _():
        acc_ref[...] = jnp.zeros_like(acc_ref)

    spot = lax.axis_index("seq") * blocks
    start = pl.multiple_of(((spot + block) // shards - first_window(spot, shards, windows)) * length, length)
    span = pl.ds(start, length)
    queries = q_ref[...]
    keys = kv_ref[span, :PAIR]
    values = kv_ref[span, PAIR:]
    grads = grad_ref[...]
    queries = by_head(queries)
    grads = by_head(grads)
    totals = jnp.concatenate([total_ref[0, 0, head : head + 1, :] for head in range(2)], axis=1)
    scores = lax.dot_general(keys, queries, dims(1, 1), preferred_element_type=jnp.float32)
    chances = jnp.exp(scores - totals)
    acc_ref[span, PAIR:] += jnp.dot(chances.astype(jnp.bfloat16), grads, preferred_element_type=jnp.float32)
    grad_chances = lax.dot_general(values, grads, dims(1, 1), preferred_element_type=jnp.float32)
    both = chances * grad_chances
    inner = jnp.sum(both, axis=0, keepdims=True)
    grad_scores = (both - chances * inner).astype(jnp.bfloat16)
    acc_ref[span, :PAIR] += jnp.dot(grad_scores, queries, preferred_element_type=jnp.float32)
    grad_q = lax.dot_general(keys, grad_scores, dims(0, 0), preferred_element_type=jnp.float32)
    grad_q = own_halves(grad_q, q_ref.shape[0]) * (HEAD_DIM**-0.5)
    gq_ref[...] = turn_back(grad_q, cosq_ref[...], sinq_ref[...]).astype(jnp.bfloat16)

    @pl.when(block == blocks - 1)
    def _():
        for w in range(acc_ref.shape[0] // length):
            rows = pl.ds(w * length, length)
            gkv_ref[rows, :PAIR] = turn_back(acc_ref[rows, :PAIR], cosk_ref[...], sink_ref[...]).astype(jnp.bfloat16)
            gkv_ref[rows, PAIR:] = acc_ref[rows, PAIR:].astype(jnp.bfloat16)

    @pl.when(step == pl.num_programs(0) * blocks - 1)
    def _():
        steps.end()


def first_window(spot, shards, windows):
    window = spot // shards
    return window - window // (windows - 1)


def attend_backward(queries, key_values, grads, totals, rope_q, rope_k, wire, span, length, collective_id):
    tokens, width = queries.shape
    pairs = width // PAIR
    blocks = tokens // span
    all_rows = key_values.shape[0]
    sizes = grid_sizes()
    total, columns = wire.shape
    rows = total // math.prod(sizes)
    count = min(16, 2 * ((pairs * blocks - 2) // 2 - 3))
    block = pl.BlockSpec((span, PAIR), lambda p, b: (b, p))
    rope_block = pl.BlockSpec((span, PAIR), lambda p, b: (b, 0))
    whole = pl.BlockSpec((length, PAIR), lambda p, b: (0, 0), pipeline_mode=pl.Buffered(1))
    return pl.pallas_call(
        functools.partial(backward_kernel, blocks, length // span, sizes, column_chunks(columns, count)),
        grid=(pairs, blocks),
        in_specs=[
            block,
            pl.BlockSpec((all_rows, 2 * PAIR), lambda p, b: (0, p)),
            block,
            pl.BlockSpec((1, 1, 8, span), lambda p, b: (p, b, 0, 0)),
            rope_block, rope_block, whole, whole,
            pl.BlockSpec(memory_space=pl.ANY),
        ],
        out_specs=[
            block,
            pl.BlockSpec((all_rows, 2 * PAIR), lambda p, b: (0, p)),
            pl.BlockSpec((rows, columns), lambda p, b: (0, 0)),
        ],
        scratch_shapes=[pltpu.VMEM((all_rows, 2 * PAIR), jnp.float32)] + scatter_scratch(sizes, rows, columns, count),
        out_shape=[
            jax.ShapeDtypeStruct((tokens, width), jnp.bfloat16),
            jax.ShapeDtypeStruct((all_rows, 2 * width), jnp.bfloat16),
            jax.ShapeDtypeStruct((rows, columns), jnp.float32),
        ],
        compiler_params=pltpu.CompilerParams(
            collective_id=collective_id, has_side_effects=True, vmem_limit_bytes=60 * MB
        ),
        cost_estimate=pl.CostEstimate(
            flops=10 * tokens * length * width, bytes_accessed=48 * MB, transcendentals=tokens * length * width // HEAD_DIM
        ),
        name="attend_backward",
    )(queries, key_values, grads, totals, *rope_q, *rope_k, wire.reshape(*sizes, rows, columns))


def cost(flops, moved):
    return pl.CostEstimate(flops=flops, bytes_accessed=moved, transcendentals=0)


def gate_kernel(x_ref, gate_w_ref, up_w_ref, gate_ref, up_ref, hidden_ref):
    gate = jnp.dot(x_ref[...], gate_w_ref[...], preferred_element_type=jnp.float32)
    up = jnp.dot(x_ref[...], up_w_ref[...], preferred_element_type=jnp.float32)
    gate_ref[...] = gate.astype(jnp.bfloat16)
    up_ref[...] = up.astype(jnp.bfloat16)
    hidden_ref[...] = (gate * jax.nn.sigmoid(gate) * up).astype(jnp.bfloat16)


def gate_forward(x, weights, hidden_width, wide=512, tile=None):
    tokens, width = x.shape
    tile = tile or tokens
    shift = hidden_width // wide
    spot = lambda n, m: (m, n)
    return pl.pallas_call(
        gate_kernel,
        grid=(hidden_width // wide, tokens // tile),
        in_specs=[
            pl.BlockSpec((tile, width), lambda n, m: (m, 0)),
            pl.BlockSpec((width, wide), lambda n, m: (0, n)),
            pl.BlockSpec((width, wide), lambda n, m: (0, n + shift)),
        ],
        out_specs=[pl.BlockSpec((tile, wide), spot)] * 3,
        out_shape=[
            jax.ShapeDtypeStruct((tokens, hidden_width), jnp.bfloat16),
            jax.ShapeDtypeStruct((tokens, hidden_width), jnp.bfloat16),
            jax.ShapeDtypeStruct((tokens, hidden_width), jnp.bfloat16),
        ],
        compiler_params=pltpu.CompilerParams(vmem_limit_bytes=48 * MB),
        cost_estimate=cost(4 * tokens * width * hidden_width, 10 * tokens * hidden_width + 4 * width * hidden_width),
        name="gate_forward",
    )(x, weights, weights)


def down_kernel(hidden_ref, w_ref, base_ref, out_ref):
    part = jnp.dot(hidden_ref[...], w_ref[...], preferred_element_type=jnp.float32)

    @pl.when(pl.program_id(1) == 0)
    def _():
        out_ref[...] = base_ref[...] + part

    @pl.when(pl.program_id(1) > 0)
    def _():
        out_ref[...] += part


def down_forward(hidden, weights, base, first, tile=None):
    tokens, width = base.shape
    tile = tile or tokens
    folds = hidden.shape[1] // width
    shift = first // width
    return pl.pallas_call(
        down_kernel,
        grid=(tokens // tile, folds),
        in_specs=[
            pl.BlockSpec((tile, width), lambda m, f: (m, f)),
            pl.BlockSpec((width, width), lambda m, f: (0, f + shift)),
            pl.BlockSpec((tile, width), lambda m, f: (m, 0)),
        ],
        out_specs=pl.BlockSpec((tile, width), lambda m, f: (m, 0)),
        out_shape=jax.ShapeDtypeStruct((tokens, width), jnp.float32),
        compiler_params=pltpu.CompilerParams(vmem_limit_bytes=48 * MB),
        cost_estimate=cost(2 * tokens * width * folds * width, 12 * tokens * width + 2 * folds * width * width),
        name="down_forward",
    )(hidden, weights, base)


def gate_back_kernel(grad_ref, w_ref, gate_ref, up_ref, grad_gate_ref, grad_up_ref):
    grad_hidden = lax.dot_general(grad_ref[...], w_ref[...], dims(1, 1), preferred_element_type=jnp.float32)
    gate = gate_ref[...].astype(jnp.float32)
    sigmoid = jax.nn.sigmoid(gate)
    grad_up_ref[...] = (grad_hidden * (gate * sigmoid)).astype(jnp.bfloat16)
    grad_gate_ref[...] = (
        grad_hidden * up_ref[...].astype(jnp.float32) * (sigmoid * (1.0 + gate * (1.0 - sigmoid)))
    ).astype(jnp.bfloat16)


def gate_backward(grad, weights, gate, up, first, wide=512, tile=None):
    tokens, width = grad.shape
    tile = tile or tokens
    hidden_width = gate.shape[1]
    per = width // wide
    shift = first // width
    spot = lambda n, m: (m, n)
    return pl.pallas_call(
        gate_back_kernel,
        grid=(hidden_width // wide, tokens // tile),
        in_specs=[
            pl.BlockSpec((tile, width), lambda n, m: (m, 0)),
            pl.BlockSpec((wide, width), lambda n, m: (lax.rem(n, per), n // per + shift)),
            pl.BlockSpec((tile, wide), spot),
            pl.BlockSpec((tile, wide), spot),
        ],
        out_specs=[pl.BlockSpec((tile, wide), spot)] * 2,
        out_shape=[jax.ShapeDtypeStruct((tokens, hidden_width), jnp.bfloat16)] * 2,
        compiler_params=pltpu.CompilerParams(vmem_limit_bytes=48 * MB),
        cost_estimate=cost(2 * tokens * width * hidden_width, 12 * tokens * hidden_width + 2 * width * hidden_width),
        name="gate_backward",
    )(grad, weights, gate, up)


def swap_rows(out, value, order):
    outer, inner = order
    rows = value.shape[0] // (outer * inner)
    for i in range(outer):
        for j in range(inner):
            spot, source = (j * outer + i) * rows, (i * inner + j) * rows
            out[spot : spot + rows, :] = value[source : source + rows, :]


def weight_kernel(sides, order, left_ref, *refs):
    out_ref, turned = refs[-2], refs[-1]

    @pl.when(pl.program_id(0) == 0)
    def _():
        swap_rows(turned, left_ref[...].T, order)

    per = pl.num_programs(0) // sides
    for side in range(sides):
        @pl.when(pl.program_id(0) // per == side)
        def _():
            out_ref[...] = jnp.dot(
                turned[...], refs[side][...], preferred_element_type=jnp.float32
            ).astype(jnp.bfloat16)


def weight_grad(left, rights, order, wide=1024, total=None, filled=None, first=0):
    tokens, width = left.shape
    sides, columns = len(rights), rights[0].shape[1]
    per = columns // wide
    return pl.pallas_call(
        functools.partial(weight_kernel, sides, order),
        grid=(sides * per,),
        in_specs=[pl.BlockSpec((tokens, width), lambda n: (0, 0))]
        + [
            pl.BlockSpec((tokens, wide), lambda n, s=s: (0, jnp.clip(n - s * per, 0, per - 1)))
            for s in range(sides)
        ]
        + [pl.BlockSpec(memory_space=pl.ANY)] * (filled is not None),
        out_specs=pl.BlockSpec(
            (pl.Element(width), pl.Element(wide)),
            lambda n: (0, pl.multiple_of(first + n * wide, PAIR)),
        ),
        out_shape=jax.ShapeDtypeStruct(
            filled.shape if filled is not None else (width, total or sides * columns), jnp.bfloat16
        ),
        input_output_aliases={} if filled is None else {1 + sides: 0},
        scratch_shapes=[pltpu.VMEM((width, tokens), jnp.bfloat16)],
        compiler_params=pltpu.CompilerParams(vmem_limit_bytes=56 * MB),
        cost_estimate=cost(2 * tokens * width * sides * columns, 4 * (tokens + width) * sides * columns),
        name="weight_grad",
    )(left, *rights, *([] if filled is None else [filled]))


def down_grad_kernel(order, hidden_ref, grad_ref, filled_ref, out_ref):
    value = lax.dot_general(
        hidden_ref[...], grad_ref[...], dims(0, 0), preferred_element_type=jnp.float32
    )
    swap_rows(out_ref, value.astype(jnp.bfloat16), order)


def down_grad(hidden, grad, filled, first, order):
    tokens, width = grad.shape
    folds = hidden.shape[1] // width
    return pl.pallas_call(
        functools.partial(down_grad_kernel, order),
        grid=(folds,),
        in_specs=[
            pl.BlockSpec((tokens, width), lambda f: (0, f)),
            pl.BlockSpec((tokens, width), lambda f: (0, 0)),
            pl.BlockSpec(memory_space=pl.ANY),
        ],
        out_specs=pl.BlockSpec(
            (pl.Element(width), pl.Element(width)), lambda f: (0, pl.multiple_of(first + f * width, PAIR))
        ),
        out_shape=jax.ShapeDtypeStruct(filled.shape, jnp.bfloat16),
        input_output_aliases={2: 0},
        compiler_params=pltpu.CompilerParams(vmem_limit_bytes=48 * MB),
        cost_estimate=cost(2 * tokens * width * folds * width, 4 * tokens * folds * width),
        name="down_grad",
    )(hidden, grad, filled)


def input_kernel(sides, first_ref, *refs):
    grads, weights, out_ref = refs[:sides], refs[sides:2 * sides], refs[2 * sides]
    part = None
    for grad_ref, w_ref in zip(grads, weights):
        term = lax.dot_general(grad_ref[...], w_ref[...], dims(1, 1), preferred_element_type=jnp.float32)
        part = term if part is None else part + term

    @pl.when(pl.program_id(1) == 0)
    def _():
        out_ref[...] = part

    @pl.when(pl.program_id(1) > 0)
    def _():
        out_ref[...] += part


def input_grad(grads, weights, firsts, wide=1024, tile=None):
    tokens, columns = grads[0].shape
    width = weights.shape[0]
    tile = tile or tokens
    sides = len(grads)
    return pl.pallas_call(
        lambda *refs: input_kernel(sides, None, *refs),
        grid=(tokens // tile, columns // wide),
        in_specs=[pl.BlockSpec((tile, wide), lambda m, k: (m, k))] * sides
        + [
            pl.BlockSpec((width, wide), lambda m, k, first=first: (0, k + first // wide))
            for first in firsts
        ],
        out_specs=pl.BlockSpec((tile, width), lambda m, k: (m, 0)),
        out_shape=jax.ShapeDtypeStruct((tokens, width), jnp.float32),
        compiler_params=pltpu.CompilerParams(vmem_limit_bytes=48 * MB),
        cost_estimate=cost(2 * sides * tokens * width * columns, 2 * sides * (tokens + width) * columns),
        name="input_grad",
    )(*grads, *([weights] * sides))


def onehot_block(ids, first, wide):
    columns = lax.broadcasted_iota(jnp.int32, (ids.shape[0], wide), 1) + first
    return (ids == columns).astype(jnp.float32).astype(jnp.bfloat16)


def embed_kernel(ids_ref, table_ref, gain_ref, shift_ref, out_ref, onehot_ref, normed_ref, stats_ref):
    wide = table_ref.shape[1]
    step = pl.program_id(1)
    onehot = onehot_block(ids_ref[...], step * wide, wide)
    onehot_ref[...] = onehot
    part = lax.dot_general(onehot, table_ref[...], dims(1, 1), preferred_element_type=jnp.float32)

    @pl.when(step == 0)
    def _():
        out_ref[...] = part

    @pl.when(step > 0)
    def _():
        out_ref[...] += part

    @pl.when(step == pl.num_programs(1) - 1)
    def _():
        values = out_ref[...]
        mean = jnp.mean(values, axis=-1, keepdims=True)
        centre = values - mean
        scale = lax.rsqrt(jnp.mean(centre * centre, axis=-1, keepdims=True) + norm_eps)
        normed_ref[...] = (centre * scale * gain_ref[...] + shift_ref[...]).astype(jnp.bfloat16)
        stats_ref[:, :PAIR] = jnp.broadcast_to(mean, (values.shape[0], PAIR))
        stats_ref[:, PAIR:] = jnp.broadcast_to(scale, (values.shape[0], PAIR))


def embed(ids, weights, first, columns, gain, shift, tile):
    tokens, width = ids.shape[0], weights.shape[0]
    wide = max(PAIR * i for i in range(1, 12) if columns % (PAIR * i) == 0)
    spot = lambda m, k: (m, 0)
    return pl.pallas_call(
        embed_kernel,
        grid=(tokens // tile, columns // wide),
        in_specs=[
            pl.BlockSpec((tile, 1), spot),
            pl.BlockSpec(
                (pl.Element(width), pl.Element(wide)),
                lambda m, k: (0, pl.multiple_of(first + k * wide, PAIR)),
            ),
            pl.BlockSpec((1, width), lambda m, k: (0, 0)),
            pl.BlockSpec((1, width), lambda m, k: (0, 0)),
        ],
        out_specs=[
            pl.BlockSpec((tile, width), spot),
            pl.BlockSpec((tile, wide), lambda m, k: (m, k)),
            pl.BlockSpec((tile, width), spot),
            pl.BlockSpec((tile, 2 * PAIR), spot),
        ],
        out_shape=[
            jax.ShapeDtypeStruct((tokens, width), jnp.float32),
            jax.ShapeDtypeStruct((tokens, columns), jnp.bfloat16),
            jax.ShapeDtypeStruct((tokens, width), jnp.bfloat16),
            jax.ShapeDtypeStruct((tokens, 2 * PAIR), jnp.float32),
        ],
        compiler_params=pltpu.CompilerParams(vmem_limit_bytes=58 * MB),
        cost_estimate=cost(
            2 * tokens * width * columns, 4 * tokens * width + 2 * (width + tokens) * columns
        ),
        name="embed",
    )(ids, weights, gain, shift)


def normed_grad_kernel(spot_ref, pairs_ref, pair_w_ref, queries_ref, query_w_ref, values_ref, stats_ref, later_ref,
                       gain_ref, out_ref, sums_ref):
    place = pl.program_id(0) - spot_ref[0]
    mine = jnp.logical_and(place >= 0, place < spot_ref[1])
    grad = lax.dot_general(pairs_ref[...], pair_w_ref[...], dims(1, 1), preferred_element_type=jnp.float32)
    grad = grad + jnp.where(mine, 1.0, 0.0) * lax.dot_general(
        queries_ref[...], query_w_ref[...], dims(1, 1), preferred_element_type=jnp.float32
    )
    scale = stats_ref[:, PAIR : PAIR + 1]
    unit = (values_ref[...] - stats_ref[:, :1]) * scale
    scaled = grad * gain_ref[...]
    inner = jnp.mean(scaled * unit, axis=-1, keepdims=True)
    outer = jnp.mean(scaled, axis=-1, keepdims=True)
    passed = scale * (scaled - outer - unit * inner)
    out_ref[...] = (passed + jnp.where(mine, 1.0, 0.0) * later_ref[...]).astype(jnp.bfloat16)

    @pl.when(pl.program_id(0) == 0)
    def _():
        sums_ref[...] = jnp.zeros_like(sums_ref)

    sums_ref[0:1, :] += jnp.sum(grad * unit, axis=0, keepdims=True)
    sums_ref[1:2, :] += jnp.sum(grad, axis=0, keepdims=True)


def normed_grad(spot, grad_pairs, grad_queries, weights, values, stats, later, gain, tile):
    tokens, width = values.shape
    blocks = grad_queries.shape[0] // tile
    own = lambda m, s: (jnp.clip(m - s[0], 0, blocks - 1), 0)
    row = lambda m, s: (m, 0)
    return pl.pallas_call(
        normed_grad_kernel,
        grid_spec=pltpu.PrefetchScalarGridSpec(
            num_scalar_prefetch=1,
            grid=(tokens // tile,),
            in_specs=[
                pl.BlockSpec((tile, 2 * width), row),
                pl.BlockSpec((pl.Element(width), pl.Element(2 * width)), lambda m, s: (0, width)),
                pl.BlockSpec((tile, width), own),
                pl.BlockSpec((width, width), lambda m, s: (0, 0)),
                pl.BlockSpec((tile, width), row),
                pl.BlockSpec((tile, 2 * PAIR), row),
                pl.BlockSpec((tile, width), own),
                pl.BlockSpec((1, width), lambda m, s: (0, 0)),
            ],
            out_specs=[
                pl.BlockSpec((tile, width), row),
                pl.BlockSpec((8, width), lambda m, s: (0, 0)),
            ],
        ),
        out_shape=[
            jax.ShapeDtypeStruct((tokens, width), jnp.bfloat16),
            jax.ShapeDtypeStruct((8, width), jnp.float32),
        ],
        compiler_params=pltpu.CompilerParams(vmem_limit_bytes=56 * MB),
        cost_estimate=cost(6 * tokens * width * width, 16 * tokens * width + 6 * width * width),
        name="normed_grad",
    )(spot, grad_pairs, weights, grad_queries, weights, values, stats, later, gain)


def embed_grad_kernel(sizes, chunks, left_ref, onehot_ref, wire_ref, out_ref, own_ref, turned, *scratch):
    step = pl.program_id(0)
    steps = Scatter(sizes, chunks, wire_ref, own_ref, *scratch)

    @pl.when(step == 0)
    def _():
        steps.begin()
        turned[...] = left_ref[...].T

    for number in range(steps.ticks):
        @pl.when(step == number + 1)
        def _():
            steps.tick(number)

    out_ref[...] = jnp.dot(turned[...], onehot_ref[...], preferred_element_type=jnp.float32).astype(jnp.bfloat16)

    @pl.when(step == pl.num_programs(0) - 1)
    def _():
        steps.end()


def embed_grad(left, onehot, wire, total, wide, collective_id):
    tokens, width = left.shape
    columns = onehot.shape[1]
    sizes = grid_sizes()
    rows = wire.shape[0] // math.prod(sizes)
    count = min(12, 2 * (columns // wide - 2 - 3))
    return pl.pallas_call(
        functools.partial(embed_grad_kernel, sizes, column_chunks(wire.shape[1], count)),
        grid=(columns // wide,),
        in_specs=[
            pl.BlockSpec((tokens, width), lambda n: (0, 0), pipeline_mode=pl.Buffered(1)),
            pl.BlockSpec((tokens, wide), lambda n: (0, n)),
            pl.BlockSpec(memory_space=pl.ANY),
        ],
        out_specs=[
            pl.BlockSpec((width, wide), lambda n: (0, n)),
            pl.BlockSpec((rows, wire.shape[1]), lambda n: (0, 0)),
        ],
        out_shape=[
            jax.ShapeDtypeStruct((width, total), jnp.bfloat16),
            jax.ShapeDtypeStruct((rows, wire.shape[1]), jnp.float32),
        ],
        scratch_shapes=[pltpu.VMEM((width, tokens), jnp.bfloat16)]
        + scatter_scratch(sizes, rows, wire.shape[1], count),
        compiler_params=pltpu.CompilerParams(
            collective_id=collective_id, has_side_effects=True, vmem_limit_bytes=58 * MB
        ),
        cost_estimate=cost(2 * tokens * width * columns, 2 * (tokens + width) * columns),
        name="embed_grad",
    )(left, onehot, wire.reshape(*sizes, rows, -1))


def grid_sizes():
    cores = 2
    across = lax.axis_size("seq") // cores
    return lax.axis_size("dp") // across, across, across, cores


def column_chunks(columns, count):
    lanes = columns // PAIR
    widths = [(lanes // count + (i < lanes % count)) * PAIR for i in range(count)]
    starts = [sum(widths[:i]) for i in range(count)]
    return [pl.ds(start, wide) for start, wide in zip(starts, widths)]


class Place:
    def __init__(self, sizes):
        self.sizes = dict(zip("zyxc", sizes))
        dp, seq = lax.axis_index("dp"), lax.axis_index("seq")
        self.at = {
            "z": dp // sizes[1],
            "y": lax.rem(dp, sizes[1]),
            "x": seq // sizes[3],
            "c": lax.rem(seq, sizes[3]),
        }

    def other(self, axis, step):
        return lax.rem(self.at[axis] + step, self.sizes[axis])

    def device(self, axis, step):
        at = dict(self.at)
        at[axis] = self.other(axis, step)
        return (at["z"] * self.sizes["y"] + at["y"], at["x"] * self.sizes["c"] + at["c"])

    def steps(self, axis):
        return range(1, self.sizes[axis])

    def greet(self):
        barrier = pltpu.get_barrier_semaphore()
        peers = 0
        for axis in "cxyz":
            for step in self.steps(axis):
                pl.semaphore_signal(barrier, inc=1, device_id=self.device(axis, step), device_id_type=MESH)
                peers += 1
        pl.semaphore_wait(barrier, peers)


class Scatter:
    def __init__(self, sizes, chunks, g_ref, out_ref, own, one, two, three, four, load_sem, send_sem, recv_sem):
        self.sizes, self.chunks, self.place = sizes, chunks, Place(sizes)
        self.g_ref, self.out_ref = g_ref, out_ref
        self.own, self.one, self.two, self.three, self.four = own, one, two, three, four
        self.load_sem, self.send_sem, self.recv_sem = load_sem, send_sem, recv_sem
        self.most = max(sizes[1:3])
        self.ticks = (len(chunks) + 1) // 2 + 3

    def load(self, chunk):
        at = self.place.at
        cols = self.chunks[chunk]
        return pltpu.make_async_copy(
            self.g_ref.at[:, :, :, at["c"], :, cols], self.own.at[:, :, :, :, cols], self.load_sem.at[chunk]
        )

    def copies(self, chunk, stage):
        place, cols = self.place, self.chunks[chunk]
        out = []

        def add(src, dst, slot, axis, step):
            out.append(pltpu.make_async_remote_copy(
                src_ref=src, dst_ref=dst, send_sem=self.send_sem.at[chunk, slot],
                recv_sem=self.recv_sem.at[chunk, slot], device_id=place.device(axis, step), device_id_type=MESH))

        if stage == 0:
            add(self.g_ref.at[:, :, :, place.other("c", 1), :, cols], self.one.at[:, :, :, :, cols], 0, "c", 1)
        if stage == 1:
            axis = "xy"[chunk % 2]
            for step in place.steps(axis):
                spot = place.other(axis, step)
                src = self.one.at[:, :, spot, :, cols] if axis == "x" else self.one.at[:, spot, :, :, cols]
                add(src, self.two.at[step - 1, :, :, :, cols], step, axis, step)
        if stage == 2:
            axis = "yx"[chunk % 2]
            for step in place.steps(axis):
                src = self.two.at[0, :, place.other(axis, step), :, cols]
                add(src, self.three.at[step - 1, :, :, cols], self.most - 1 + step, axis, step)
        if stage == 3:
            for step in place.steps("z"):
                src = self.three.at[0, place.other("z", step), :, cols]
                add(src, self.four.at[step - 1, :, cols], 2 * (self.most - 1) + step, "z", step)
        return out

    def begin(self):
        self.place.greet()
        for chunk in range(len(self.chunks)):
            self.load(chunk).start()
            for copy in self.copies(chunk, 0):
                copy.start()

    def advance(self, chunk, stage):
        n_z, n_y, n_x, n_c = self.sizes
        place, cols, f32, low = self.place, self.chunks[chunk], jnp.float32, jnp.bfloat16
        at = place.at
        own, one, two, three, four = self.own, self.one, self.two, self.three, self.four
        if stage == 0:
            self.load(chunk).wait()
        for copy in self.copies(chunk, stage):
            copy.wait_recv()
        if stage == 0:

            def add(i, carry):
                z, rest = i // (n_y * n_x), lax.rem(i, n_y * n_x)
                y, x = rest // n_x, lax.rem(rest, n_x)
                total = own[z, y, x, :, cols].astype(f32) + one[z, y, x, :, cols].astype(f32)
                one[z, y, x, :, cols] = total.astype(low)
                return carry

            lax.fori_loop(0, n_z * n_y * n_x, add, 0)
        if stage == 1:
            axis = "xy"[chunk % 2]
            kept = n_y if axis == "x" else n_x

            def add(i, carry):
                z, k = i // kept, lax.rem(i, kept)
                mine = one[z, k, at["x"], :, cols] if axis == "x" else one[z, at["y"], k, :, cols]
                total = mine.astype(f32)
                for step in place.steps(axis):
                    total = total + two[step - 1, z, k, :, cols].astype(f32)
                two[0, z, k, :, cols] = total.astype(low)
                return carry

            lax.fori_loop(0, n_z * kept, add, 0)
        if stage == 2:
            axis = "yx"[chunk % 2]

            def add(z, carry):
                total = two[0, z, at[axis], :, cols].astype(f32)
                for step in place.steps(axis):
                    total = total + three[step - 1, z, :, cols].astype(f32)
                three[0, z, :, cols] = total.astype(low)
                return carry

            lax.fori_loop(0, n_z, add, 0)
        if stage == 3:
            total = three[0, at["z"], :, cols].astype(f32)
            for step in place.steps("z"):
                total = total + four[step - 1, :, cols].astype(f32)
            self.out_ref[:, cols] = total
            return
        for copy in self.copies(chunk, stage + 1):
            copy.start()

    def tick(self, number):
        for stage in range(4):
            for chunk in (2 * (number - stage), 2 * (number - stage) + 1):
                if 0 <= number - stage and chunk < len(self.chunks):
                    self.advance(chunk, stage)

    def end(self):
        for chunk in range(len(self.chunks)):
            for stage in range(4):
                for copy in self.copies(chunk, stage):
                    copy.wait_send()


def scatter_scratch(sizes, rows, columns, count):
    n_z, n_y, n_x, n_c = sizes
    most = max(n_x, n_y)
    slots = 1 + 2 * (most - 1) + n_z - 1
    low = jnp.bfloat16
    return [
        pltpu.VMEM((n_z, n_y, n_x, rows, columns), low),
        pltpu.VMEM((n_z, n_y, n_x, rows, columns), low),
        pltpu.VMEM((most - 1, n_z, most, rows, columns), low),
        pltpu.VMEM((most - 1, n_z, rows, columns), low),
        pltpu.VMEM((n_z - 1, rows, columns), low),
        pltpu.SemaphoreType.DMA((count,)),
        pltpu.SemaphoreType.DMA((count, slots)),
        pltpu.SemaphoreType.DMA((count, slots)),
    ]


def total_steps(place, value, slots, send_sem, recv_sem):
    started = []
    for turn_at, axis in enumerate("cxyz"):
        held, me = slots[axis], place.at[axis]
        held[me] = value
        arriving = []
        for step in place.steps(axis):
            copy = pltpu.make_async_remote_copy(
                src_ref=held.at[me], dst_ref=held.at[me],
                send_sem=send_sem.at[turn_at, step], recv_sem=recv_sem.at[turn_at, step],
                device_id=place.device(axis, step), device_id_type=MESH)
            copy.start()
            arriving.append(copy)
        for copy in arriving:
            copy.wait_recv()
        started += arriving
        value = held[0]
        for spot in range(1, place.sizes[axis]):
            value = value + held[spot]
    return value, started


def scatter_kernel(sizes, chunks, g_ref, tile_ref, out_ref, total_ref, *scratch):
    steps = Scatter(sizes, chunks, g_ref, out_ref, *scratch[:8])
    slots = dict(zip("zyxc", scratch[8:12]))
    steps.begin()
    for number in range(steps.ticks):
        steps.tick(number)
    squares = jnp.zeros((), jnp.float32)
    for cols in chunks:
        squares = squares + jnp.sum(out_ref[:, cols] * out_ref[:, cols])
    row = lax.broadcasted_iota(jnp.int32, (8, PAIR), 0)
    value = tile_ref[...] + jnp.where(row == 0, squares, 0.0)
    value, started = total_steps(steps.place, value, slots, *scratch[12:])
    total_ref[...] = value
    for copy in started:
        copy.wait_send()
    steps.end()


def scatter_and_total(grads, values, collective_id, count=16):
    sizes = grid_sizes()
    total, columns = grads.shape
    rows = total // math.prod(sizes)
    row = lax.broadcasted_iota(jnp.int32, (8, PAIR), 0)
    tile = jnp.zeros((8, PAIR), jnp.float32)
    for i, value in enumerate(values):
        tile = jnp.where(row == i, value, tile)
    sums, totals = pl.pallas_call(
        functools.partial(scatter_kernel, sizes, column_chunks(columns, count)),
        in_specs=[pl.BlockSpec(memory_space=pl.ANY), pl.BlockSpec(memory_space=pltpu.VMEM)],
        out_specs=[pl.BlockSpec(memory_space=pltpu.VMEM)] * 2,
        out_shape=[
            jax.ShapeDtypeStruct((rows, columns), jnp.float32),
            jax.ShapeDtypeStruct(tile.shape, jnp.float32),
        ],
        scratch_shapes=scatter_scratch(sizes, rows, columns, count)
        + [pltpu.VMEM((size, 8, PAIR), jnp.float32) for size in sizes]
        + [pltpu.SemaphoreType.DMA((4, max(sizes)))] * 2,
        compiler_params=pltpu.CompilerParams(
            collective_id=collective_id, has_side_effects=True, vmem_limit_bytes=48 * MB
        ),
        cost_estimate=pl.CostEstimate(flops=2 * total * columns, bytes_accessed=2 * total * columns, transcendentals=0),
        name="scatter_and_total",
    )(grads.reshape(*sizes, rows, columns), tile)
    return sums, [totals[i, 0] for i in range(len(values))]


def gather_kernel(sizes, pieces, *refs):
    load_sem, send_sem, recv_sem = refs[-3:]
    arrays = (len(refs) - 3) // 2
    n_z, n_y, n_x, n_c = sizes
    place = Place(sizes)
    at = place.at
    started = []
    waits = {}
    most = max(n_x, n_y)

    def send(ref, chunk, slot, axis, step):
        copy = pltpu.make_async_remote_copy(
            src_ref=ref, dst_ref=ref, send_sem=send_sem.at[chunk, slot], recv_sem=recv_sem.at[chunk, slot],
            device_id=place.device(axis, step), device_id_type=MESH)
        copy.start()
        started.append(copy)
        return copy

    loads = []
    for chunk, (array, cols) in enumerate(pieces):
        load = pltpu.make_async_copy(
            refs[array].at[:, cols], refs[arrays + array].at[at["z"], at["y"], at["x"], at["c"], :, cols], load_sem.at[chunk])
        load.start()
        loads.append(load)
    place.greet()

    def first(chunk, out_ref, cols):
        loads[chunk].wait()
        ref = out_ref.at[at["z"], at["y"], at["x"], at["c"], :, cols]
        waits[chunk, 0] = [send(ref, chunk, step - 1, "z", step) for step in place.steps("z")]

    def second(chunk, out_ref, cols):
        for copy in waits[chunk, 0]:
            copy.wait_recv()
        axis = "xy"[chunk % 2]
        ref = out_ref.at[:, at["y"], at["x"], at["c"], :, cols]
        waits[chunk, 1] = [send(ref, chunk, n_z - 2 + step, axis, step) for step in place.steps(axis)]

    def third(chunk, out_ref, cols):
        for copy in waits[chunk, 1]:
            copy.wait_recv()
        axis = "yx"[chunk % 2]
        if axis == "y":
            ref = out_ref.at[:, at["y"], :, at["c"], :, cols]
        else:
            ref = out_ref.at[:, :, at["x"], at["c"], :, cols]
        waits[chunk, 2] = [send(ref, chunk, n_z - 2 + most - 1 + step, axis, step) for step in place.steps(axis)]

    def fourth(chunk, out_ref, cols):
        for copy in waits[chunk, 2]:
            copy.wait_recv()
        ref = out_ref.at[:, :, :, at["c"], :, cols]
        waits[chunk, 3] = [send(ref, chunk, n_z - 2 + 2 * (most - 1) + 1, "c", 1)]

    pairs = (len(pieces) + 1) // 2
    for tick in range(pairs + 3):
        for late, stage in enumerate((first, second, third, fourth)):
            for chunk in (2 * (tick - late), 2 * (tick - late) + 1):
                if 0 <= tick - late and chunk < len(pieces):
                    array, cols = pieces[chunk]
                    stage(chunk, refs[arrays + array], cols)
    for chunk in range(len(pieces)):
        for copy in waits[chunk, 3]:
            copy.wait_recv()
    for copy in started:
        copy.wait_send()


def gather_rows(arrays, counts, collective_id):
    sizes = grid_sizes()
    n_z, n_y, n_x, n_c = sizes
    slots = n_z - 1 + 2 * (max(n_x, n_y) - 1) + 1
    pieces = [
        (i, cols)
        for i, (array, count) in enumerate(zip(arrays, counts))
        for cols in column_chunks(array.shape[1], count)
    ]
    outs = pl.pallas_call(
        functools.partial(gather_kernel, sizes, pieces),
        in_specs=[pl.BlockSpec(memory_space=pl.ANY)] * len(arrays),
        out_specs=[pl.BlockSpec(memory_space=pl.ANY)] * len(arrays),
        out_shape=[jax.ShapeDtypeStruct(sizes + array.shape, array.dtype) for array in arrays],
        scratch_shapes=[
            pltpu.SemaphoreType.DMA((len(pieces),)),
            pltpu.SemaphoreType.DMA((len(pieces), slots)),
            pltpu.SemaphoreType.DMA((len(pieces), slots)),
        ],
        compiler_params=pltpu.CompilerParams(collective_id=collective_id, has_side_effects=True),
        name="gather_rows",
    )(*arrays)
    devices = n_z * n_y * n_x * n_c
    return [out.reshape(devices * array.shape[0], -1) for out, array in zip(outs, arrays)]


from jax.sharding import PartitionSpec as P

AXES = ("dp", "seq")
beta_one = 0.9
beta_two = 0.999
adam_eps = 1e-08
weight_decay = 0.01
learn_rate = 0.02
norm_rate = 0.2
ema_decay = 0.7


def project_kernel(roped, x_ref, w_ref, cos_ref, sin_ref, out_ref):
    product = jnp.dot(x_ref[...], w_ref[...], preferred_element_type=jnp.float32)
    for part in range(product.shape[1] // PAIR):
        piece = product[:, part * PAIR : (part + 1) * PAIR]
        if roped == "all":
            piece = turn(piece, cos_ref[...], sin_ref[...]).astype(jnp.bfloat16)
            piece = piece * jnp.bfloat16(HEAD_DIM**-0.5)
        elif part % 2 == 0:
            piece = turn(piece, cos_ref[...], sin_ref[...])
        out_ref[:, part * PAIR : (part + 1) * PAIR] = piece.astype(jnp.bfloat16)


def project(x, weights, first_column, columns, rope, tile, roped):
    tokens, width = x.shape
    wide = 512
    repeat = rope[0].shape[0] // tile
    return pl.pallas_call(
        functools.partial(project_kernel, roped),
        grid=(tokens // tile, columns // wide),
        in_specs=[
            pl.BlockSpec((tile, width), lambda m, n: (m, 0)),
            pl.BlockSpec((width, wide), lambda m, n: (0, n + first_column // wide)),
            pl.BlockSpec((tile, PAIR), lambda m, n: (lax.rem(m, repeat), 0)),
            pl.BlockSpec((tile, PAIR), lambda m, n: (lax.rem(m, repeat), 0)),
        ],
        out_specs=pl.BlockSpec((tile, wide), lambda m, n: (m, n)),
        out_shape=jax.ShapeDtypeStruct((tokens, columns), jnp.bfloat16),
        compiler_params=pltpu.CompilerParams(vmem_limit_bytes=40 * MB),
        cost_estimate=pl.CostEstimate(
            flops=2 * tokens * width * columns,
            bytes_accessed=2 * (tokens * width + width * columns + tokens * columns),
            transcendentals=0,
        ),
        name="project",
    )(x, weights, *rope)


def rope_tables(positions):
    half = HEAD_DIM // 2
    inverse = 10000.0 ** (-jnp.arange(half).astype(jnp.float32) / half)
    angles = positions.astype(jnp.float32)[:, None] * inverse[None, :]
    copies = PAIR // half
    return (jnp.tile(jnp.cos(angles), (1, copies)), jnp.tile(jnp.sin(angles), (1, copies)))


def norm_forward(values, gain, shift):
    centre = values - jnp.mean(values, axis=-1, keepdims=True)
    spread = jnp.mean(centre * centre, axis=-1, keepdims=True)
    scale = lax.rsqrt(spread + norm_eps)
    unit = centre * scale
    return (unit * gain + shift).astype(jnp.bfloat16), unit, scale


def norm_backward(grad, unit, scale, gain):
    grad_gain = jnp.sum(grad * unit, axis=0)
    grad_shift = jnp.sum(grad, axis=0)
    scaled = grad * gain
    inner = jnp.mean(scaled * unit, axis=-1, keepdims=True)
    outer = jnp.mean(scaled, axis=-1, keepdims=True)
    return scale * (scaled - outer - unit * inner), grad_gain, grad_shift


def product(left, right, left_dim=1, right_dim=0, precision=None):
    return lax.dot_general(
        left, right, dims(left_dim, right_dim), precision=precision,
        preferred_element_type=jnp.float32,
    )


def pair_columns(weights):
    rows, columns = weights.shape
    width = columns // 2
    return weights.reshape(rows, 2, width // PAIR, PAIR).transpose(0, 2, 1, 3).reshape(rows, columns)


def unpair_columns(weights):
    rows, columns = weights.shape
    width = columns // 2
    return weights.reshape(rows, width // PAIR, 2, PAIR).transpose(0, 2, 1, 3).reshape(rows, columns)


def most_lanes(columns, most):
    return max(PAIR * i for i in range(1, most + 1) if columns % (PAIR * i) == 0)


def on_device(
    token_ids,
    mask_rows,
    mask_labels,
    mask_counts,
    step_count,
    vocab_tables,
    attention,
    feed_in,
    feed_out,
    norm_params,
    first_tables,
    first_attention,
    first_feed_in,
    first_feed_out,
    first_norms,
    second_tables,
    second_attention,
    second_feed_in,
    second_feed_out,
    second_norms,
    ema_tables,
    ema_attention,
    ema_feed_in,
    ema_feed_out,
    ema_norms,
):
    master = (vocab_tables, attention, feed_in, feed_out, norm_params)
    firsts = (first_tables, first_attention, first_feed_in, first_feed_out, first_norms)
    seconds = (second_tables, second_attention, second_feed_in, second_feed_out, second_norms)
    averages = (ema_tables, ema_attention, ema_feed_in, ema_feed_out, ema_norms)
    group_rates = (learn_rate, learn_rate, learn_rate, learn_rate, norm_rate)
    low = jnp.bfloat16

    shards = lax.axis_size("seq")
    devices = shards * lax.axis_size("dp")
    windows, span = token_ids.shape
    slots = mask_rows.shape[1]
    vocab = vocab_tables.shape[2]
    padded = vocab + -vocab % PAIR
    rows, columns = attention.shape
    width = columns // 4
    hidden_width = feed_in.shape[1] // 2
    folds = feed_out.shape[0] // rows
    length = span * shards
    spot = lax.axis_index("seq")

    tables_sent = jnp.pad(vocab_tables, ((0, 0), (0, 0), (0, padded - vocab)))
    table_sent = tables_sent[0].astype(low)
    attn_sent = jnp.concatenate(
        [
            attention[:, :width],
            pair_columns(attention[:, width : 3 * width]),
            attention[:, 3 * width :],
        ],
        axis=1,
    ).astype(low)
    in_sent = feed_in.reshape(rows, 2, hidden_width // folds, folds).transpose(0, 1, 3, 2)
    late_sent = jnp.concatenate(
        [
            in_sent.reshape(rows, 2 * hidden_width),
            feed_out.reshape(rows, folds * width),
            tables_sent[1],
        ],
        axis=1,
    ).astype(low)

    small = jnp.concatenate(
        [
            token_ids.reshape(-1).astype(jnp.float32),
            mask_rows.reshape(-1).astype(jnp.float32),
            mask_labels.reshape(-1).astype(jnp.float32),
            mask_counts.reshape(-1).astype(jnp.float32),
            norm_params.astype(low).astype(jnp.float32).reshape(-1),
        ]
    )
    small = jnp.pad(small, (0, -small.shape[0] % (8 * PAIR))).reshape(8, -1)
    small_all, table = gather_rows((small, table_sent), (1, 11), 3)
    late_sent, attn_sent, small_all, table = lax.optimization_barrier(
        (late_sent, attn_sent, small_all, table)
    )
    late = lax.all_gather(late_sent, AXES, axis=0, tiled=True)
    (attn,) = gather_rows((attn_sent,), (10,), 5)
    small_all = small_all.reshape(devices, -1)
    out_w = attn[:, 3 * width :]
    head_w = late[:, 2 * hidden_width + folds * width :]
    cuts = [windows * span, windows * slots, windows * slots, windows]
    marks = [sum(cuts[:i]) for i in range(len(cuts) + 1)]
    gains = small_all[:, marks[4] : marks[4] + rows * 6].reshape(devices * rows, 6)
    count = jnp.sum(small_all[:, marks[3] : marks[4]])
    group = lax.dynamic_slice_in_dim(small_all, lax.axis_index("dp") * shards, shards, axis=0)

    def in_order(first, last):
        piece = group[:, first:last].reshape(shards, windows, -1)
        return piece.transpose(1, 0, 2).reshape(windows * shards, -1)

    ids = in_order(marks[0], marks[1]).astype(jnp.int32)
    block = spot * windows + jnp.arange(windows, dtype=jnp.int32)

    def mine(first, last):
        return lax.dynamic_slice_in_dim(in_order(first, last), spot * windows, windows, axis=0)

    own_rows = mine(marks[1], marks[2]).astype(jnp.int32)
    own_labels = mine(marks[2], marks[3]).astype(jnp.int32).reshape(-1)
    own_counts = mine(marks[3], marks[4])
    live = (jnp.arange(slots, dtype=jnp.float32)[None, :] < own_counts).astype(jnp.float32)
    live = live.reshape(-1)

    base = first_window(spot * windows, shards, windows)
    wins = block // shards - base
    offset = (spot * windows - base * shards) * span
    ids_two = lax.dynamic_slice_in_dim(ids, base * shards, 2 * shards, axis=0).reshape(-1)
    positions = ((block % shards)[:, None] * span + jnp.arange(span, dtype=jnp.int32)).reshape(-1)
    rope_q = rope_tables(positions)
    rope_k = rope_tables(jnp.arange(length, dtype=jnp.int32))
    tokens = windows * span

    def own(values):
        return lax.dynamic_slice_in_dim(values, offset, tokens, axis=0)

    embedded_two, onehot, normed_one, stats = embed(
        ids_two[:, None], table, 0, padded, gains[:, 0][None], gains[:, 1][None], length // 2
    )
    normed_own = own(normed_one)
    queries = project(normed_own, attn, 0, width, rope_q, tokens, "all")
    key_values = project(normed_one, attn, width, 2 * width, rope_k, length, "half")
    mixture, totals = attend_forward(wins, queries, key_values, span, length)
    after_attn = own(embedded_two) + product(mixture, out_w)

    normed_two, unit_two, scale_two = norm_forward(after_attn, gains[:, 2], gains[:, 3])
    gate, up, hidden = gate_forward(normed_two, late, hidden_width)
    after_feed = down_forward(hidden, late, after_attn, 2 * hidden_width)

    pick = (own_rows[:, :, None] == jnp.arange(span, dtype=jnp.int32)).astype(jnp.float32)
    selected = jnp.einsum(
        "wsp,wpd->wsd", pick, after_feed.reshape(windows, span, width),
        precision=lax.Precision.HIGHEST, preferred_element_type=jnp.float32,
    ).reshape(windows * slots, width)
    normed_final, unit_final, scale_final = norm_forward(selected, gains[:, 4], gains[:, 5])
    column = jnp.arange(padded, dtype=jnp.int32)[None, :]
    logits = jnp.where(column < vocab, product(normed_final, head_w), -jnp.inf)
    log_total = jax.nn.logsumexp(logits, axis=-1)
    wanted = own_labels[:, None] == column
    picked = jnp.sum(jnp.where(wanted, logits, 0.0), axis=-1)
    loss_part = jnp.sum(live * (log_total - picked))

    grad_logits = (
        (jnp.exp(logits - log_total[:, None]) - wanted.astype(jnp.float32)) * (live / count)[:, None]
    ).astype(low)
    grad_selected, grad_gain_final, grad_shift_final = norm_backward(
        product(grad_logits, head_w, 1, 1), unit_final, scale_final, gains[:, 4]
    )
    grad_after_feed = jnp.einsum(
        "wsp,wsd->wpd", pick, grad_selected.reshape(windows, slots, width),
        precision=lax.Precision.HIGHEST, preferred_element_type=jnp.float32,
    ).reshape(tokens, width)
    rounded_feed = grad_after_feed.astype(low)
    order = (lax.axis_size("dp"), shards)
    spare = ((0, -grad_logits.shape[0] % PAIR), (0, 0))
    late_grads = weight_grad(
        jnp.pad(normed_final, spare), (jnp.pad(grad_logits, spare),), order, most_lanes(padded, 11),
        padded + folds * width,
    )
    late_grads = down_grad(hidden, rounded_feed, late_grads, padded, order)
    rounded_feed, late_grads = lax.optimization_barrier((rounded_feed, late_grads))
    late_part = lax.psum_scatter(late_grads, "seq", scatter_dimension=0, tiled=True)
    grad_gate, grad_up = gate_backward(rounded_feed, late, gate, up, 2 * hidden_width)
    alone = (1, 1)
    in_grads = weight_grad(normed_two, (grad_gate, grad_up), alone)

    grad_inner, grad_gain_two, grad_shift_two = norm_backward(
        input_grad((grad_gate, grad_up), late, (0, hidden_width)), unit_two, scale_two, gains[:, 2]
    )
    grad_after_attn = grad_after_feed + grad_inner
    rounded_attn = grad_after_attn.astype(low)
    grad_mixture = product(rounded_attn, out_w, 1, 1).astype(low)
    grad_queries, grad_pairs, in_own = attend_backward(
        queries, key_values, grad_mixture, totals, rope_q, rope_k, in_grads, span, length, 2
    )
    grad_queries, late_part = lax.optimization_barrier((grad_queries, late_part))
    late_own = lax.psum_scatter(late_part, "dp", scatter_dimension=0, tiled=True)
    attn_grads = weight_grad(mixture, (rounded_attn,), alone, width // 2, columns, None, 3 * width)
    attn_grads = weight_grad(normed_own, (grad_queries,), alone, width // 2, None, attn_grads)
    attn_grads = weight_grad(normed_one, (grad_pairs,), alone, width // 2, None, attn_grads, width)
    tiles = jnp.stack([offset // span, jnp.int32(windows)])
    grad_embedded, sums_one = normed_grad(
        tiles, grad_pairs, grad_queries, attn, embedded_two, stats, grad_after_attn, gains[:, 0][None], span
    )
    grad_gain_one, grad_shift_one = sums_one[0], sums_one[1]
    early_grads, attn_own = embed_grad(grad_embedded, onehot, attn_grads, padded + PAIR, most_lanes(padded, 4), 4)
    grad_norms = jnp.stack(
        [
            grad_gain_one,
            grad_shift_one,
            grad_gain_two,
            grad_shift_two,
            grad_gain_final,
            grad_shift_final,
        ],
        axis=1,
    )
    grad_norms = jnp.pad(grad_norms, ((0, 0), (0, PAIR - grad_norms.shape[1]))).astype(low)
    early_grads = lax.dynamic_update_slice(early_grads, grad_norms, (0, padded))
    late_own = late_own.astype(jnp.float32)
    squares = (
        jnp.sum(late_own * late_own) + jnp.sum(in_own * in_own) + jnp.sum(attn_own * attn_own)
    )
    late_final = (
        late_own[:, :vocab],
        in_own.reshape(rows, 2, folds, hidden_width // folds).transpose(0, 1, 3, 2).reshape(rows, 2 * hidden_width),
        late_own[:, padded:].reshape(rows * folds, width),
        jnp.concatenate(
            [
                attn_own[:, :width],
                unpair_columns(attn_own[:, width : 3 * width]),
                attn_own[:, 3 * width :],
            ],
            axis=1,
        ),
    )
    early_grads, (head_own, in_own, down_own, attn_own) = lax.optimization_barrier((early_grads, late_final))
    early_own, (squares_all, loss_all) = scatter_and_total(early_grads, (squares, loss_part), 1)
    grads = (
        jnp.stack([early_own[:, :vocab], head_own], axis=0),
        attn_own,
        in_own,
        down_own,
        early_own[:, padded : padded + 6],
    )
    masked_loss = loss_all / count
    total_norm = jnp.sqrt(squares_all)
    limit = (slots * shards * windows * lax.axis_size("dp")) ** (-0.5)
    clip = jnp.minimum(1.0, limit / (total_norm + 1e-06))
    steps = step_count[0].astype(jnp.float32)
    fix_one = 1.0 - beta_one**steps
    fix_two = 1.0 - beta_two**steps
    weights_new, firsts_new, seconds_new, averages_new = ([], [], [], [])
    for weight, grad, first, second, average, step_rate in zip(
        master, grads, firsts, seconds, averages, group_rates
    ):
        scaled = grad * clip
        first_next = beta_one * first + (1.0 - beta_one) * scaled
        second_next = beta_two * second + (1.0 - beta_two) * scaled * scaled
        update = (
            first_next / fix_one / (jnp.sqrt(second_next / fix_two) + adam_eps)
            + weight_decay * weight
        )
        weight_next = weight - step_rate * update
        weights_new.append(weight_next)
        firsts_new.append(first_next)
        seconds_new.append(second_next)
        averages_new.append(ema_decay * average + (1.0 - ema_decay) * weight_next)
    return (masked_loss, total_norm, *weights_new, *firsts_new, *seconds_new, *averages_new)


def solution(mesh):
    split = P(AXES, None)
    tables = P(None, AXES, None)
    weights = (tables, split, split, split, split)
    return jax.shard_map(
        on_device,
        mesh=mesh,
        in_specs=(P("dp", "seq"),) * 4 + (P(),) + weights * 4,
        out_specs=(P(), P()) + weights * 4,
        check_vma=False,
    )
```

```python
import functools
import math
import jax, jax.numpy as jnp
from jax import lax
from jax.experimental import pallas as pl
from jax.experimental.pallas import tpu as pltpu
HEAD_DIM=64
PAIR=128
MB=1<<20
MESH = pl.DeviceIdType.MESH
norm_eps = 1e-05

def dims(a,b): return (((a,),(b,)),((),()))

def low_half(rows):
    lane = lax.broadcasted_iota(jnp.int32,(rows,PAIR),1)
    return lane % HEAD_DIM < HEAD_DIM//2

def turn(x, cosines, sines):
    low = low_half(x.shape[0])
    up = pltpu.roll(x, PAIR-HEAD_DIM//2, 1)
    down = pltpu.roll(x, HEAD_DIM//2, 1)
    return x*cosines + jnp.where(low,-up,down)*sines

def turn_back(g, cosines, sines):
    low = low_half(g.shape[0])
    up = pltpu.roll(g, PAIR-HEAD_DIM//2, 1)
    down = pltpu.roll(g, HEAD_DIM//2, 1)
    return g*cosines + jnp.where(low,up,-down)*sines

def head_mask(head):
    lane = lax.broadcasted_iota(jnp.int32,(1,PAIR),1)
    return (lane//HEAD_DIM==head).astype(jnp.float32).astype(jnp.bfloat16)

def by_head(rows):
    return jnp.concatenate([rows * head_mask(0), rows * head_mask(1)], axis=0)


def own_halves(mixed, span):
    own = [mixed[:HEAD_DIM, :span], mixed[HEAD_DIM:, span:]]
    return jnp.concatenate(own, axis=0).T


def forward_kernel(win_ref, q_ref, kv_ref, mix_ref, total_ref):
    queries = q_ref[...]
    keys = kv_ref[:, :PAIR]
    values = kv_ref[:, PAIR:]
    span = queries.shape[0]
    scores = lax.dot_general(keys, by_head(queries), dims(1, 1), preferred_element_type=jnp.float32)
    top = jnp.max(scores, axis=0, keepdims=True)
    chances = jnp.exp(scores - top)
    total = jnp.sum(chances, axis=0, keepdims=True)
    weights = (chances * (1.0 / total)).astype(jnp.bfloat16)
    mixed = lax.dot_general(values, weights, dims(0, 0), preferred_element_type=jnp.float32)
    mix_ref[...] = own_halves(mixed, span).astype(jnp.bfloat16)
    totals = top + jnp.log(total)
    for head in range(2):
        total_ref[0, 0, head : head + 1, :] = totals[:, head * span : (head + 1) * span]


def attend_forward(win, queries, key_values, span, length):
    tokens,width = queries.shape
    pairs = width//PAIR
    blocks = tokens//span
    return pl.pallas_call(
        forward_kernel,
        grid_spec=pltpu.PrefetchScalarGridSpec(
            num_scalar_prefetch=1, grid=(pairs,blocks),
            in_specs=[pl.BlockSpec((span,PAIR),lambda p,b,w:(b,p)),
                      pl.BlockSpec((length,2*PAIR),lambda p,b,w:(w[b],p))],
            out_specs=[pl.BlockSpec((span,PAIR),lambda p,b,w:(b,p)),
                       pl.BlockSpec((1,1,8,span),lambda p,b,w:(p,b,0,0))]),
        out_shape=[jax.ShapeDtypeStruct((tokens,width),jnp.bfloat16),
                   jax.ShapeDtypeStruct((pairs,blocks,8,span),jnp.float32)],
        compiler_params=pltpu.CompilerParams(vmem_limit_bytes=56*MB),
        cost_estimate=pl.CostEstimate(flops=4*tokens*length*width,bytes_accessed=16*MB,transcendentals=tokens*length*width//HEAD_DIM),
        name="attend_forward",
    )(win,queries,key_values)


def backward_kernel(windows, shards, sizes, chunks, q_ref, kv_ref, grad_ref, total_ref, cosq_ref, sinq_ref, cosk_ref,
                    sink_ref, wire_ref, gq_ref, gkv_ref, own_ref, acc_ref, *scratch):
    block = pl.program_id(1)
    blocks = pl.num_programs(1)
    step = pl.program_id(0) * blocks + block
    length = cosk_ref.shape[0]
    steps = Scatter(sizes, chunks, wire_ref, own_ref, *scratch)

    @pl.when(step == 0)
    def _():
        steps.begin()

    for number in range(steps.ticks):
        @pl.when(step == 2 * number + 1)
        def _():
            steps.tick(number)

    @pl.when(block == 0)
    def _():
        acc_ref[...] = jnp.zeros_like(acc_ref)

    spot = lax.axis_index("seq") * blocks
    start = pl.multiple_of(((spot + block) // shards - first_window(spot, shards, windows)) * length, length)
    span = pl.ds(start, length)
    queries = q_ref[...]
    keys = kv_ref[span, :PAIR]
    values = kv_ref[span, PAIR:]
    grads = grad_ref[...]
    queries = by_head(queries)
    grads = by_head(grads)
    totals = jnp.concatenate([total_ref[0, 0, head : head + 1, :] for head in range(2)], axis=1)
    scores = lax.dot_general(keys, queries, dims(1, 1), preferred_element_type=jnp.float32)
    chances = jnp.exp(scores - totals)
    acc_ref[span, PAIR:] += jnp.dot(chances.astype(jnp.bfloat16), grads, preferred_element_type=jnp.float32)
    grad_chances = lax.dot_general(values, grads, dims(1, 1), preferred_element_type=jnp.float32)
    both = chances * grad_chances
    inner = jnp.sum(both, axis=0, keepdims=True)
    grad_scores = (both - chances * inner).astype(jnp.bfloat16)
    acc_ref[span, :PAIR] += jnp.dot(grad_scores, queries, preferred_element_type=jnp.float32)
    grad_q = lax.dot_general(keys, grad_scores, dims(0, 0), preferred_element_type=jnp.float32)
    grad_q = own_halves(grad_q, q_ref.shape[0]) * (HEAD_DIM**-0.5)
    gq_ref[...] = turn_back(grad_q, cosq_ref[...], sinq_ref[...]).astype(jnp.bfloat16)

    @pl.when(block == blocks - 1)
    def _():
        for w in range(acc_ref.shape[0] // length):
            rows = pl.ds(w * length, length)
            gkv_ref[rows, :PAIR] = turn_back(acc_ref[rows, :PAIR], cosk_ref[...], sink_ref[...]).astype(jnp.bfloat16)
            gkv_ref[rows, PAIR:] = acc_ref[rows, PAIR:].astype(jnp.bfloat16)

    @pl.when(step == pl.num_programs(0) * blocks - 1)
    def _():
        steps.end()


def first_window(spot, shards, windows):
    window = spot // shards
    return window - window // (windows - 1)


def attend_backward(queries, key_values, grads, totals, rope_q, rope_k, wire, span, length, collective_id):
    tokens, width = queries.shape
    pairs = width // PAIR
    blocks = tokens // span
    all_rows = key_values.shape[0]
    sizes = grid_sizes()
    total, columns = wire.shape
    rows = total // math.prod(sizes)
    count = min(16, 2 * ((pairs * blocks - 2) // 2 - 3))
    block = pl.BlockSpec((span, PAIR), lambda p, b: (b, p))
    rope_block = pl.BlockSpec((span, PAIR), lambda p, b: (b, 0))
    whole = pl.BlockSpec((length, PAIR), lambda p, b: (0, 0), pipeline_mode=pl.Buffered(1))
    return pl.pallas_call(
        functools.partial(backward_kernel, blocks, length // span, sizes, column_chunks(columns, count)),
        grid=(pairs, blocks),
        in_specs=[
            block,
            pl.BlockSpec((all_rows, 2 * PAIR), lambda p, b: (0, p)),
            block,
            pl.BlockSpec((1, 1, 8, span), lambda p, b: (p, b, 0, 0)),
            rope_block, rope_block, whole, whole,
            pl.BlockSpec(memory_space=pl.ANY),
        ],
        out_specs=[
            block,
            pl.BlockSpec((all_rows, 2 * PAIR), lambda p, b: (0, p)),
            pl.BlockSpec((rows, columns), lambda p, b: (0, 0)),
        ],
        scratch_shapes=[pltpu.VMEM((all_rows, 2 * PAIR), jnp.float32)] + scatter_scratch(sizes, rows, columns, count),
        out_shape=[
            jax.ShapeDtypeStruct((tokens, width), jnp.bfloat16),
            jax.ShapeDtypeStruct((all_rows, 2 * width), jnp.bfloat16),
            jax.ShapeDtypeStruct((rows, columns), jnp.float32),
        ],
        compiler_params=pltpu.CompilerParams(
            collective_id=collective_id, has_side_effects=True, vmem_limit_bytes=60 * MB
        ),
        cost_estimate=pl.CostEstimate(
            flops=10 * tokens * length * width, bytes_accessed=48 * MB, transcendentals=tokens * length * width // HEAD_DIM
        ),
        name="attend_backward",
    )(queries, key_values, grads, totals, *rope_q, *rope_k, wire.reshape(*sizes, rows, columns))


def cost(flops, moved):
    return pl.CostEstimate(flops=flops, bytes_accessed=moved, transcendentals=0)


def gate_kernel(x_ref, gate_w_ref, up_w_ref, gate_ref, up_ref, hidden_ref):
    gate = jnp.dot(x_ref[...], gate_w_ref[...], preferred_element_type=jnp.float32)
    up = jnp.dot(x_ref[...], up_w_ref[...], preferred_element_type=jnp.float32)
    gate_ref[...] = gate.astype(jnp.bfloat16)
    up_ref[...] = up.astype(jnp.bfloat16)
    hidden_ref[...] = (gate * jax.nn.sigmoid(gate) * up).astype(jnp.bfloat16)


def gate_forward(x, weights, hidden_width, wide=512, tile=None):
    tokens, width = x.shape
    tile = tile or tokens
    shift = hidden_width // wide
    spot = lambda n, m: (m, n)
    return pl.pallas_call(
        gate_kernel,
        grid=(hidden_width // wide, tokens // tile),
        in_specs=[
            pl.BlockSpec((tile, width), lambda n, m: (m, 0)),
            pl.BlockSpec((width, wide), lambda n, m: (0, n)),
            pl.BlockSpec((width, wide), lambda n, m: (0, n + shift)),
        ],
        out_specs=[pl.BlockSpec((tile, wide), spot)] * 3,
        out_shape=[
            jax.ShapeDtypeStruct((tokens, hidden_width), jnp.bfloat16),
            jax.ShapeDtypeStruct((tokens, hidden_width), jnp.bfloat16),
            jax.ShapeDtypeStruct((tokens, hidden_width), jnp.bfloat16),
        ],
        compiler_params=pltpu.CompilerParams(vmem_limit_bytes=48 * MB),
        cost_estimate=cost(4 * tokens * width * hidden_width, 10 * tokens * hidden_width + 4 * width * hidden_width),
        name="gate_forward",
    )(x, weights, weights)


def down_kernel(hidden_ref, w_ref, base_ref, out_ref):
    part = jnp.dot(hidden_ref[...], w_ref[...], preferred_element_type=jnp.float32)

    @pl.when(pl.program_id(1) == 0)
    def _():
        out_ref[...] = base_ref[...] + part

    @pl.when(pl.program_id(1) > 0)
    def _():
        out_ref[...] += part


def down_forward(hidden, weights, base, first, tile=None):
    tokens, width = base.shape
    tile = tile or tokens
    folds = hidden.shape[1] // width
    shift = first // width
    return pl.pallas_call(
        down_kernel,
        grid=(tokens // tile, folds),
        in_specs=[
            pl.BlockSpec((tile, width), lambda m, f: (m, f)),
            pl.BlockSpec((width, width), lambda m, f: (0, f + shift)),
            pl.BlockSpec((tile, width), lambda m, f: (m, 0)),
        ],
        out_specs=pl.BlockSpec((tile, width), lambda m, f: (m, 0)),
        out_shape=jax.ShapeDtypeStruct((tokens, width), jnp.float32),
        compiler_params=pltpu.CompilerParams(vmem_limit_bytes=48 * MB),
        cost_estimate=cost(2 * tokens * width * folds * width, 12 * tokens * width + 2 * folds * width * width),
        name="down_forward",
    )(hidden, weights, base)


def gate_back_kernel(grad_ref, w_ref, gate_ref, up_ref, grad_gate_ref, grad_up_ref):
    grad_hidden = lax.dot_general(grad_ref[...], w_ref[...], dims(1, 1), preferred_element_type=jnp.float32)
    gate = gate_ref[...].astype(jnp.float32)
    sigmoid = jax.nn.sigmoid(gate)
    grad_up_ref[...] = (grad_hidden * (gate * sigmoid)).astype(jnp.bfloat16)
    grad_gate_ref[...] = (
        grad_hidden * up_ref[...].astype(jnp.float32) * (sigmoid * (1.0 + gate * (1.0 - sigmoid)))
    ).astype(jnp.bfloat16)


def gate_backward(grad, weights, gate, up, first, wide=512, tile=None):
    tokens, width = grad.shape
    tile = tile or tokens
    hidden_width = gate.shape[1]
    per = width // wide
    shift = first // width
    spot = lambda n, m: (m, n)
    return pl.pallas_call(
        gate_back_kernel,
        grid=(hidden_width // wide, tokens // tile),
        in_specs=[
            pl.BlockSpec((tile, width), lambda n, m: (m, 0)),
            pl.BlockSpec((wide, width), lambda n, m: (lax.rem(n, per), n // per + shift)),
            pl.BlockSpec((tile, wide), spot),
            pl.BlockSpec((tile, wide), spot),
        ],
        out_specs=[pl.BlockSpec((tile, wide), spot)] * 2,
        out_shape=[jax.ShapeDtypeStruct((tokens, hidden_width), jnp.bfloat16)] * 2,
        compiler_params=pltpu.CompilerParams(vmem_limit_bytes=48 * MB),
        cost_estimate=cost(2 * tokens * width * hidden_width, 12 * tokens * hidden_width + 2 * width * hidden_width),
        name="gate_backward",
    )(grad, weights, gate, up)


def swap_rows(out, value, order):
    outer, inner = order
    rows = value.shape[0] // (outer * inner)
    for i in range(outer):
        for j in range(inner):
            spot, source = (j * outer + i) * rows, (i * inner + j) * rows
            out[spot : spot + rows, :] = value[source : source + rows, :]


def weight_kernel(sides, order, left_ref, *refs):
    out_ref, turned = refs[-2], refs[-1]

    @pl.when(pl.program_id(0) == 0)
    def _():
        swap_rows(turned, left_ref[...].T, order)

    per = pl.num_programs(0) // sides
    for side in range(sides):
        @pl.when(pl.program_id(0) // per == side)
        def _():
            out_ref[...] = jnp.dot(
                turned[...], refs[side][...], preferred_element_type=jnp.float32
            ).astype(jnp.bfloat16)


def weight_grad(left, rights, order, wide=1024, total=None, filled=None, first=0):
    tokens, width = left.shape
    sides, columns = len(rights), rights[0].shape[1]
    per = columns // wide
    return pl.pallas_call(
        functools.partial(weight_kernel, sides, order),
        grid=(sides * per,),
        in_specs=[pl.BlockSpec((tokens, width), lambda n: (0, 0))]
        + [
            pl.BlockSpec((tokens, wide), lambda n, s=s: (0, jnp.clip(n - s * per, 0, per - 1)))
            for s in range(sides)
        ]
        + [pl.BlockSpec(memory_space=pl.ANY)] * (filled is not None),
        out_specs=pl.BlockSpec(
            (pl.Element(width), pl.Element(wide)),
            lambda n: (0, pl.multiple_of(first + n * wide, PAIR)),
        ),
        out_shape=jax.ShapeDtypeStruct(
            filled.shape if filled is not None else (width, total or sides * columns), jnp.bfloat16
        ),
        input_output_aliases={} if filled is None else {1 + sides: 0},
        scratch_shapes=[pltpu.VMEM((width, tokens), jnp.bfloat16)],
        compiler_params=pltpu.CompilerParams(vmem_limit_bytes=56 * MB),
        cost_estimate=cost(2 * tokens * width * sides * columns, 4 * (tokens + width) * sides * columns),
        name="weight_grad",
    )(left, *rights, *([] if filled is None else [filled]))


def down_grad_kernel(order, hidden_ref, grad_ref, filled_ref, out_ref):
    value = lax.dot_general(
        hidden_ref[...], grad_ref[...], dims(0, 0), preferred_element_type=jnp.float32
    )
    swap_rows(out_ref, value.astype(jnp.bfloat16), order)


def down_grad(hidden, grad, filled, first, order):
    tokens, width = grad.shape
    folds = hidden.shape[1] // width
    return pl.pallas_call(
        functools.partial(down_grad_kernel, order),
        grid=(folds,),
        in_specs=[
            pl.BlockSpec((tokens, width), lambda f: (0, f)),
            pl.BlockSpec((tokens, width), lambda f: (0, 0)),
            pl.BlockSpec(memory_space=pl.ANY),
        ],
        out_specs=pl.BlockSpec(
            (pl.Element(width), pl.Element(width)), lambda f: (0, pl.multiple_of(first + f * width, PAIR))
        ),
        out_shape=jax.ShapeDtypeStruct(filled.shape, jnp.bfloat16),
        input_output_aliases={2: 0},
        compiler_params=pltpu.CompilerParams(vmem_limit_bytes=48 * MB),
        cost_estimate=cost(2 * tokens * width * folds * width, 4 * tokens * folds * width),
        name="down_grad",
    )(hidden, grad, filled)


def input_kernel(sides, first_ref, *refs):
    grads, weights, out_ref = refs[:sides], refs[sides:2 * sides], refs[2 * sides]
    part = None
    for grad_ref, w_ref in zip(grads, weights):
        term = lax.dot_general(grad_ref[...], w_ref[...], dims(1, 1), preferred_element_type=jnp.float32)
        part = term if part is None else part + term

    @pl.when(pl.program_id(1) == 0)
    def _():
        out_ref[...] = part

    @pl.when(pl.program_id(1) > 0)
    def _():
        out_ref[...] += part


def input_grad(grads, weights, firsts, wide=1024, tile=None):
    tokens, columns = grads[0].shape
    width = weights.shape[0]
    tile = tile or tokens
    sides = len(grads)
    return pl.pallas_call(
        lambda *refs: input_kernel(sides, None, *refs),
        grid=(tokens // tile, columns // wide),
        in_specs=[pl.BlockSpec((tile, wide), lambda m, k: (m, k))] * sides
        + [
            pl.BlockSpec((width, wide), lambda m, k, first=first: (0, k + first // wide))
            for first in firsts
        ],
        out_specs=pl.BlockSpec((tile, width), lambda m, k: (m, 0)),
        out_shape=jax.ShapeDtypeStruct((tokens, width), jnp.float32),
        compiler_params=pltpu.CompilerParams(vmem_limit_bytes=48 * MB),
        cost_estimate=cost(2 * sides * tokens * width * columns, 2 * sides * (tokens + width) * columns),
        name="input_grad",
    )(*grads, *([weights] * sides))


def onehot_block(ids, first, wide):
    columns = lax.broadcasted_iota(jnp.int32, (ids.shape[0], wide), 1) + first
    return (ids == columns).astype(jnp.float32).astype(jnp.bfloat16)


def embed_kernel(ids_ref, table_ref, gain_ref, shift_ref, out_ref, onehot_ref, normed_ref, stats_ref):
    wide = table_ref.shape[1]
    step = pl.program_id(1)
    onehot = onehot_block(ids_ref[...], step * wide, wide)
    onehot_ref[...] = onehot
    part = lax.dot_general(onehot, table_ref[...], dims(1, 1), preferred_element_type=jnp.float32)

    @pl.when(step == 0)
    def _():
        out_ref[...] = part

    @pl.when(step > 0)
    def _():
        out_ref[...] += part

    @pl.when(step == pl.num_programs(1) - 1)
    def _():
        values = out_ref[...]
        mean = jnp.mean(values, axis=-1, keepdims=True)
        centre = values - mean
        scale = lax.rsqrt(jnp.mean(centre * centre, axis=-1, keepdims=True) + norm_eps)
        normed_ref[...] = (centre * scale * gain_ref[...] + shift_ref[...]).astype(jnp.bfloat16)
        stats_ref[:, :PAIR] = jnp.broadcast_to(mean, (values.shape[0], PAIR))
        stats_ref[:, PAIR:] = jnp.broadcast_to(scale, (values.shape[0], PAIR))


def embed(ids, weights, first, columns, gain, shift, tile):
    tokens, width = ids.shape[0], weights.shape[0]
    wide = max(PAIR * i for i in range(1, 12) if columns % (PAIR * i) == 0)
    spot = lambda m, k: (m, 0)
    return pl.pallas_call(
        embed_kernel,
        grid=(tokens // tile, columns // wide),
        in_specs=[
            pl.BlockSpec((tile, 1), spot),
            pl.BlockSpec(
                (pl.Element(width), pl.Element(wide)),
                lambda m, k: (0, pl.multiple_of(first + k * wide, PAIR)),
            ),
            pl.BlockSpec((1, width), lambda m, k: (0, 0)),
            pl.BlockSpec((1, width), lambda m, k: (0, 0)),
        ],
        out_specs=[
            pl.BlockSpec((tile, width), spot),
            pl.BlockSpec((tile, wide), lambda m, k: (m, k)),
            pl.BlockSpec((tile, width), spot),
            pl.BlockSpec((tile, 2 * PAIR), spot),
        ],
        out_shape=[
            jax.ShapeDtypeStruct((tokens, width), jnp.float32),
            jax.ShapeDtypeStruct((tokens, columns), jnp.bfloat16),
            jax.ShapeDtypeStruct((tokens, width), jnp.bfloat16),
            jax.ShapeDtypeStruct((tokens, 2 * PAIR), jnp.float32),
        ],
        compiler_params=pltpu.CompilerParams(vmem_limit_bytes=58 * MB),
        cost_estimate=cost(
            2 * tokens * width * columns, 4 * tokens * width + 2 * (width + tokens) * columns
        ),
        name="embed",
    )(ids, weights, gain, shift)


def normed_grad_kernel(spot_ref, pairs_ref, pair_w_ref, queries_ref, query_w_ref, values_ref, stats_ref, later_ref,
                       gain_ref, out_ref, sums_ref):
    place = pl.program_id(0) - spot_ref[0]
    mine = jnp.logical_and(place >= 0, place < spot_ref[1])
    grad = lax.dot_general(pairs_ref[...], pair_w_ref[...], dims(1, 1), preferred_element_type=jnp.float32)
    grad = grad + jnp.where(mine, 1.0, 0.0) * lax.dot_general(
        queries_ref[...], query_w_ref[...], dims(1, 1), preferred_element_type=jnp.float32
    )
    scale = stats_ref[:, PAIR : PAIR + 1]
    unit = (values_ref[...] - stats_ref[:, :1]) * scale
    scaled = grad * gain_ref[...]
    inner = jnp.mean(scaled * unit, axis=-1, keepdims=True)
    outer = jnp.mean(scaled, axis=-1, keepdims=True)
    passed = scale * (scaled - outer - unit * inner)
    out_ref[...] = (passed + jnp.where(mine, 1.0, 0.0) * later_ref[...]).astype(jnp.bfloat16)

    @pl.when(pl.program_id(0) == 0)
    def _():
        sums_ref[...] = jnp.zeros_like(sums_ref)

    sums_ref[0:1, :] += jnp.sum(grad * unit, axis=0, keepdims=True)
    sums_ref[1:2, :] += jnp.sum(grad, axis=0, keepdims=True)


def normed_grad(spot, grad_pairs, grad_queries, weights, values, stats, later, gain, tile):
    tokens, width = values.shape
    blocks = grad_queries.shape[0] // tile
    own = lambda m, s: (jnp.clip(m - s[0], 0, blocks - 1), 0)
    row = lambda m, s: (m, 0)
    return pl.pallas_call(
        normed_grad_kernel,
        grid_spec=pltpu.PrefetchScalarGridSpec(
            num_scalar_prefetch=1,
            grid=(tokens // tile,),
            in_specs=[
                pl.BlockSpec((tile, 2 * width), row),
                pl.BlockSpec((pl.Element(width), pl.Element(2 * width)), lambda m, s: (0, width)),
                pl.BlockSpec((tile, width), own),
                pl.BlockSpec((width, width), lambda m, s: (0, 0)),
                pl.BlockSpec((tile, width), row),
                pl.BlockSpec((tile, 2 * PAIR), row),
                pl.BlockSpec((tile, width), own),
                pl.BlockSpec((1, width), lambda m, s: (0, 0)),
            ],
            out_specs=[
                pl.BlockSpec((tile, width), row),
                pl.BlockSpec((8, width), lambda m, s: (0, 0)),
            ],
        ),
        out_shape=[
            jax.ShapeDtypeStruct((tokens, width), jnp.bfloat16),
            jax.ShapeDtypeStruct((8, width), jnp.float32),
        ],
        compiler_params=pltpu.CompilerParams(vmem_limit_bytes=56 * MB),
        cost_estimate=cost(6 * tokens * width * width, 16 * tokens * width + 6 * width * width),
        name="normed_grad",
    )(spot, grad_pairs, weights, grad_queries, weights, values, stats, later, gain)


def embed_grad_kernel(sizes, attn_chunks, table_chunks, left_ref, onehot_ref, norms_ref, attn_ref, tile_ref,
                      attn_own_ref, table_own_ref, total_ref, turned, grads, *scratch):
    step, last = pl.program_id(0), pl.num_programs(0) - 1
    attn = Scatter(sizes, attn_chunks, attn_ref, attn_own_ref, *scratch[:8])
    table = Scatter(sizes, table_chunks, grads, table_own_ref, None, *scratch[8:14])
    slots = dict(zip("zyxc", scratch[14:18]))
    norm_piece = len(table_chunks) - 1

    @pl.when(step == 0)
    def _():
        attn.begin()
        grads[:, :, :, :, :, table_chunks[norm_piece]] = norms_ref[...]
        table.send(norm_piece, 0)
        turned[...] = left_ref[...].T

    for number in range(attn.ticks):
        @pl.when(step == number + 1)
        def _():
            attn.tick(number)

    block = jnp.dot(turned[...], onehot_ref[...], preferred_element_type=jnp.float32).astype(jnp.bfloat16)
    for number in range(norm_piece):
        @pl.when(step == number)
        def _():
            grads[:, :, :, :, :, table_chunks[number]] = block.reshape(*grads.shape[:5], block.shape[1])
            table.send(number, 0)
            for stage in range(3):
                if number - 2 - 2 * stage >= 0:
                    table.advance(number - 2 - 2 * stage, stage)

    @pl.when(step == last)
    def _():
        done = {number: len([s for s in range(3) if number + 2 + 2 * s < norm_piece]) for number in range(norm_piece)}
        done[norm_piece] = 0
        for stage in range(4):
            for number in range(norm_piece + 1):
                if done[number] <= stage:
                    table.advance(number, stage)
        squares = jnp.zeros((), jnp.float32)
        for cols in attn_chunks:
            squares = squares + jnp.sum(attn_own_ref[:, cols] * attn_own_ref[:, cols])
        for cols in table_chunks:
            squares = squares + jnp.sum(table_own_ref[:, cols] * table_own_ref[:, cols])
        row = lax.broadcasted_iota(jnp.int32, (8, PAIR), 0)
        value = tile_ref[...] + jnp.where(row == 0, squares, 0.0)
        value, started = total_steps(attn.place, value, slots, *scratch[18:])
        total_ref[...] = value
        for copy in started:
            copy.wait_send()
        attn.end()
        table.end()


def embed_grad(left, onehot, norms, attn_grads, values, wide, collective_id):
    tokens, width = left.shape
    columns = onehot.shape[1]
    sizes = grid_sizes()
    rows = width // math.prod(sizes)
    count = min(12, 2 * (columns // wide - 2 - 3))
    table_chunks = [pl.ds(start, wide) for start in range(0, columns, wide)] + [pl.ds(columns, PAIR)]
    row = lax.broadcasted_iota(jnp.int32, (8, PAIR), 0)
    tile = jnp.zeros((8, PAIR), jnp.float32)
    for i, value in enumerate(values):
        tile = jnp.where(row == i, value, tile)
    attn_columns, table_columns = attn_grads.shape[1], columns + PAIR
    attn_own, table_own, totals = pl.pallas_call(
        functools.partial(embed_grad_kernel, sizes, column_chunks(attn_columns, count), table_chunks),
        grid=(columns // wide,),
        in_specs=[
            pl.BlockSpec((tokens, width), lambda n: (0, 0), pipeline_mode=pl.Buffered(1)),
            pl.BlockSpec((tokens, wide), lambda n: (0, n)),
            pl.BlockSpec(memory_space=pltpu.VMEM),
            pl.BlockSpec(memory_space=pl.ANY),
            pl.BlockSpec(memory_space=pltpu.VMEM),
        ],
        out_specs=[pl.BlockSpec(memory_space=pltpu.VMEM)] * 3,
        out_shape=[
            jax.ShapeDtypeStruct((rows, attn_columns), jnp.float32),
            jax.ShapeDtypeStruct((rows, table_columns), jnp.float32),
            jax.ShapeDtypeStruct(tile.shape, jnp.float32),
        ],
        scratch_shapes=[pltpu.VMEM((width, tokens), jnp.bfloat16), pltpu.VMEM((*sizes, rows, table_columns), jnp.bfloat16)]
        + scatter_scratch(sizes, rows, attn_columns, count)
        + [s for i, s in enumerate(scatter_scratch(sizes, rows, table_columns, len(table_chunks))) if i not in (0, 5)]
        + [pltpu.VMEM((size, 8, PAIR), jnp.float32) for size in sizes]
        + [pltpu.SemaphoreType.DMA((4, max(sizes)))] * 2,
        compiler_params=pltpu.CompilerParams(
            collective_id=collective_id, has_side_effects=True, vmem_limit_bytes=60 * MB
        ),
        cost_estimate=cost(2 * tokens * width * columns, 2 * (tokens + width) * columns),
        name="embed_grad",
    )(left, onehot, norms.reshape(*sizes, rows, PAIR), attn_grads.reshape(*sizes, rows, -1), tile)
    return attn_own, table_own, [totals[i, 0] for i in range(len(values))]


def grid_sizes():
    cores = 2
    across = lax.axis_size("seq") // cores
    return lax.axis_size("dp") // across, across, across, cores


def column_chunks(columns, count):
    lanes = columns // PAIR
    widths = [(lanes // count + (i < lanes % count)) * PAIR for i in range(count)]
    starts = [sum(widths[:i]) for i in range(count)]
    return [pl.ds(start, wide) for start, wide in zip(starts, widths)]


class Place:
    def __init__(self, sizes):
        self.sizes = dict(zip("zyxc", sizes))
        dp, seq = lax.axis_index("dp"), lax.axis_index("seq")
        self.at = {
            "z": dp // sizes[1],
            "y": lax.rem(dp, sizes[1]),
            "x": seq // sizes[3],
            "c": lax.rem(seq, sizes[3]),
        }

    def other(self, axis, step):
        return lax.rem(self.at[axis] + step, self.sizes[axis])

    def device(self, axis, step):
        at = dict(self.at)
        at[axis] = self.other(axis, step)
        return (at["z"] * self.sizes["y"] + at["y"], at["x"] * self.sizes["c"] + at["c"])

    def steps(self, axis):
        return range(1, self.sizes[axis])

    def greet(self):
        barrier = pltpu.get_barrier_semaphore()
        peers = 0
        for axis in "cxyz":
            for step in self.steps(axis):
                pl.semaphore_signal(barrier, inc=1, device_id=self.device(axis, step), device_id_type=MESH)
                peers += 1
        pl.semaphore_wait(barrier, peers)


class Scatter:
    def __init__(self, sizes, chunks, g_ref, out_ref, own, one, two, three, four, *sems):
        self.sizes, self.chunks, self.place = sizes, chunks, Place(sizes)
        self.g_ref, self.out_ref = g_ref, out_ref
        self.own, self.one, self.two, self.three, self.four = own, one, two, three, four
        self.load_sem, self.send_sem, self.recv_sem = ([None] * 3 + list(sems))[-3:]
        self.most = max(sizes[1:3])
        self.ticks = (len(chunks) + 1) // 2 + 3

    def load(self, chunk):
        at = self.place.at
        cols = self.chunks[chunk]
        return pltpu.make_async_copy(
            self.g_ref.at[:, :, :, at["c"], :, cols], self.own.at[:, :, :, :, cols], self.load_sem.at[chunk]
        )

    def copies(self, chunk, stage):
        place, cols = self.place, self.chunks[chunk]
        out = []

        def add(src, dst, slot, axis, step):
            out.append(pltpu.make_async_remote_copy(
                src_ref=src, dst_ref=dst, send_sem=self.send_sem.at[chunk, slot],
                recv_sem=self.recv_sem.at[chunk, slot], device_id=place.device(axis, step), device_id_type=MESH))

        if stage == 0:
            add(self.g_ref.at[:, :, :, place.other("c", 1), :, cols], self.one.at[:, :, :, :, cols], 0, "c", 1)
        if stage == 1:
            axis = "xy"[chunk % 2]
            for step in place.steps(axis):
                spot = place.other(axis, step)
                src = self.one.at[:, :, spot, :, cols] if axis == "x" else self.one.at[:, spot, :, :, cols]
                add(src, self.two.at[step - 1, :, :, :, cols], step, axis, step)
        if stage == 2:
            axis = "yx"[chunk % 2]
            for step in place.steps(axis):
                src = self.two.at[0, :, place.other(axis, step), :, cols]
                add(src, self.three.at[step - 1, :, :, cols], self.most - 1 + step, axis, step)
        if stage == 3:
            for step in place.steps("z"):
                src = self.three.at[0, place.other("z", step), :, cols]
                add(src, self.four.at[step - 1, :, cols], 2 * (self.most - 1) + step, "z", step)
        return out

    def begin(self):
        self.place.greet()
        for chunk in range(len(self.chunks)):
            self.load(chunk).start()
            self.send(chunk, 0)

    def send(self, chunk, stage):
        for copy in self.copies(chunk, stage):
            copy.start()

    def advance(self, chunk, stage):
        n_z, n_y, n_x, n_c = self.sizes
        place, cols, f32, low = self.place, self.chunks[chunk], jnp.float32, jnp.bfloat16
        at = place.at
        own, one, two, three, four = self.own, self.one, self.two, self.three, self.four
        if stage == 0 and own is not None:
            self.load(chunk).wait()
        for copy in self.copies(chunk, stage):
            copy.wait_recv()
        if stage == 0:

            def add(i, carry):
                z, rest = i // (n_y * n_x), lax.rem(i, n_y * n_x)
                y, x = rest // n_x, lax.rem(rest, n_x)
                mine = self.g_ref[z, y, x, at["c"], :, cols] if own is None else own[z, y, x, :, cols]
                total = mine.astype(f32) + one[z, y, x, :, cols].astype(f32)
                one[z, y, x, :, cols] = total.astype(low)
                return carry

            lax.fori_loop(0, n_z * n_y * n_x, add, 0)
        if stage == 1:
            axis = "xy"[chunk % 2]
            kept = n_y if axis == "x" else n_x

            def add(i, carry):
                z, k = i // kept, lax.rem(i, kept)
                mine = one[z, k, at["x"], :, cols] if axis == "x" else one[z, at["y"], k, :, cols]
                total = mine.astype(f32)
                for step in place.steps(axis):
                    total = total + two[step - 1, z, k, :, cols].astype(f32)
                two[0, z, k, :, cols] = total.astype(low)
                return carry

            lax.fori_loop(0, n_z * kept, add, 0)
        if stage == 2:
            axis = "yx"[chunk % 2]

            def add(z, carry):
                total = two[0, z, at[axis], :, cols].astype(f32)
                for step in place.steps(axis):
                    total = total + three[step - 1, z, :, cols].astype(f32)
                three[0, z, :, cols] = total.astype(low)
                return carry

            lax.fori_loop(0, n_z, add, 0)
        if stage == 3:
            total = three[0, at["z"], :, cols].astype(f32)
            for step in place.steps("z"):
                total = total + four[step - 1, :, cols].astype(f32)
            self.out_ref[:, cols] = total
            return
        self.send(chunk, stage + 1)

    def tick(self, number):
        for stage in range(4):
            for chunk in (2 * (number - stage), 2 * (number - stage) + 1):
                if 0 <= number - stage and chunk < len(self.chunks):
                    self.advance(chunk, stage)

    def end(self):
        for chunk in range(len(self.chunks)):
            for stage in range(4):
                for copy in self.copies(chunk, stage):
                    copy.wait_send()


def scatter_scratch(sizes, rows, columns, count):
    n_z, n_y, n_x, n_c = sizes
    most = max(n_x, n_y)
    slots = 1 + 2 * (most - 1) + n_z - 1
    low = jnp.bfloat16
    return [
        pltpu.VMEM((n_z, n_y, n_x, rows, columns), low),
        pltpu.VMEM((n_z, n_y, n_x, rows, columns), low),
        pltpu.VMEM((most - 1, n_z, most, rows, columns), low),
        pltpu.VMEM((most - 1, n_z, rows, columns), low),
        pltpu.VMEM((n_z - 1, rows, columns), low),
        pltpu.SemaphoreType.DMA((count,)),
        pltpu.SemaphoreType.DMA((count, slots)),
        pltpu.SemaphoreType.DMA((count, slots)),
    ]


def total_steps(place, value, slots, send_sem, recv_sem):
    started = []
    for turn_at, axis in enumerate("cxyz"):
        held, me = slots[axis], place.at[axis]
        held[me] = value
        arriving = []
        for step in place.steps(axis):
            copy = pltpu.make_async_remote_copy(
                src_ref=held.at[me], dst_ref=held.at[me],
                send_sem=send_sem.at[turn_at, step], recv_sem=recv_sem.at[turn_at, step],
                device_id=place.device(axis, step), device_id_type=MESH)
            copy.start()
            arriving.append(copy)
        for copy in arriving:
            copy.wait_recv()
        started += arriving
        value = held[0]
        for spot in range(1, place.sizes[axis]):
            value = value + held[spot]
    return value, started


def gather_kernel(sizes, pieces, *refs):
    load_sem, send_sem, recv_sem = refs[-3:]
    arrays = (len(refs) - 3) // 2
    n_z, n_y, n_x, n_c = sizes
    place = Place(sizes)
    at = place.at
    started = []
    waits = {}
    most = max(n_x, n_y)

    def send(ref, chunk, slot, axis, step):
        copy = pltpu.make_async_remote_copy(
            src_ref=ref, dst_ref=ref, send_sem=send_sem.at[chunk, slot], recv_sem=recv_sem.at[chunk, slot],
            device_id=place.device(axis, step), device_id_type=MESH)
        copy.start()
        started.append(copy)
        return copy

    loads = []
    for chunk, (array, cols) in enumerate(pieces):
        load = pltpu.make_async_copy(
            refs[array].at[:, cols], refs[arrays + array].at[at["z"], at["y"], at["x"], at["c"], :, cols], load_sem.at[chunk])
        load.start()
        loads.append(load)
    place.greet()

    def first(chunk, out_ref, cols):
        loads[chunk].wait()
        ref = out_ref.at[at["z"], at["y"], at["x"], at["c"], :, cols]
        waits[chunk, 0] = [send(ref, chunk, step - 1, "z", step) for step in place.steps("z")]

    def second(chunk, out_ref, cols):
        for copy in waits[chunk, 0]:
            copy.wait_recv()
        axis = "xy"[chunk % 2]
        ref = out_ref.at[:, at["y"], at["x"], at["c"], :, cols]
        waits[chunk, 1] = [send(ref, chunk, n_z - 2 + step, axis, step) for step in place.steps(axis)]

    def third(chunk, out_ref, cols):
        for copy in waits[chunk, 1]:
            copy.wait_recv()
        axis = "yx"[chunk % 2]
        if axis == "y":
            ref = out_ref.at[:, at["y"], :, at["c"], :, cols]
        else:
            ref = out_ref.at[:, :, at["x"], at["c"], :, cols]
        waits[chunk, 2] = [send(ref, chunk, n_z - 2 + most - 1 + step, axis, step) for step in place.steps(axis)]

    def fourth(chunk, out_ref, cols):
        for copy in waits[chunk, 2]:
            copy.wait_recv()
        ref = out_ref.at[:, :, :, at["c"], :, cols]
        waits[chunk, 3] = [send(ref, chunk, n_z - 2 + 2 * (most - 1) + 1, "c", 1)]

    pairs = (len(pieces) + 1) // 2
    for tick in range(pairs + 3):
        for late, stage in enumerate((first, second, third, fourth)):
            for chunk in (2 * (tick - late), 2 * (tick - late) + 1):
                if 0 <= tick - late and chunk < len(pieces):
                    array, cols = pieces[chunk]
                    stage(chunk, refs[arrays + array], cols)
    for chunk in range(len(pieces)):
        for copy in waits[chunk, 3]:
            copy.wait_recv()
    for copy in started:
        copy.wait_send()


def gather_rows(arrays, counts, collective_id):
    sizes = grid_sizes()
    n_z, n_y, n_x, n_c = sizes
    slots = n_z - 1 + 2 * (max(n_x, n_y) - 1) + 1
    pieces = [
        (i, cols)
        for i, (array, count) in enumerate(zip(arrays, counts))
        for cols in column_chunks(array.shape[1], count)
    ]
    outs = pl.pallas_call(
        functools.partial(gather_kernel, sizes, pieces),
        in_specs=[pl.BlockSpec(memory_space=pl.ANY)] * len(arrays),
        out_specs=[pl.BlockSpec(memory_space=pl.ANY)] * len(arrays),
        out_shape=[jax.ShapeDtypeStruct(sizes + array.shape, array.dtype) for array in arrays],
        scratch_shapes=[
            pltpu.SemaphoreType.DMA((len(pieces),)),
            pltpu.SemaphoreType.DMA((len(pieces), slots)),
            pltpu.SemaphoreType.DMA((len(pieces), slots)),
        ],
        compiler_params=pltpu.CompilerParams(collective_id=collective_id, has_side_effects=True),
        name="gather_rows",
    )(*arrays)
    devices = n_z * n_y * n_x * n_c
    return [out.reshape(devices * array.shape[0], -1) for out, array in zip(outs, arrays)]


from jax.sharding import PartitionSpec as P

AXES = ("dp", "seq")
beta_one = 0.9
beta_two = 0.999
adam_eps = 1e-08
weight_decay = 0.01
learn_rate = 0.02
norm_rate = 0.2
ema_decay = 0.7


def project_kernel(roped, x_ref, w_ref, cos_ref, sin_ref, out_ref):
    product = jnp.dot(x_ref[...], w_ref[...], preferred_element_type=jnp.float32)
    for part in range(product.shape[1] // PAIR):
        piece = product[:, part * PAIR : (part + 1) * PAIR]
        if roped == "all":
            piece = turn(piece, cos_ref[...], sin_ref[...]).astype(jnp.bfloat16)
            piece = piece * jnp.bfloat16(HEAD_DIM**-0.5)
        elif part % 2 == 0:
            piece = turn(piece, cos_ref[...], sin_ref[...])
        out_ref[:, part * PAIR : (part + 1) * PAIR] = piece.astype(jnp.bfloat16)


def project(x, weights, first_column, columns, rope, tile, roped):
    tokens, width = x.shape
    wide = 512
    repeat = rope[0].shape[0] // tile
    return pl.pallas_call(
        functools.partial(project_kernel, roped),
        grid=(tokens // tile, columns // wide),
        in_specs=[
            pl.BlockSpec((tile, width), lambda m, n: (m, 0)),
            pl.BlockSpec((width, wide), lambda m, n: (0, n + first_column // wide)),
            pl.BlockSpec((tile, PAIR), lambda m, n: (lax.rem(m, repeat), 0)),
            pl.BlockSpec((tile, PAIR), lambda m, n: (lax.rem(m, repeat), 0)),
        ],
        out_specs=pl.BlockSpec((tile, wide), lambda m, n: (m, n)),
        out_shape=jax.ShapeDtypeStruct((tokens, columns), jnp.bfloat16),
        compiler_params=pltpu.CompilerParams(vmem_limit_bytes=40 * MB),
        cost_estimate=pl.CostEstimate(
            flops=2 * tokens * width * columns,
            bytes_accessed=2 * (tokens * width + width * columns + tokens * columns),
            transcendentals=0,
        ),
        name="project",
    )(x, weights, *rope)


def rope_tables(positions):
    half = HEAD_DIM // 2
    inverse = 10000.0 ** (-jnp.arange(half).astype(jnp.float32) / half)
    angles = positions.astype(jnp.float32)[:, None] * inverse[None, :]
    copies = PAIR // half
    return (jnp.tile(jnp.cos(angles), (1, copies)), jnp.tile(jnp.sin(angles), (1, copies)))


def norm_forward(values, gain, shift):
    centre = values - jnp.mean(values, axis=-1, keepdims=True)
    spread = jnp.mean(centre * centre, axis=-1, keepdims=True)
    scale = lax.rsqrt(spread + norm_eps)
    unit = centre * scale
    return (unit * gain + shift).astype(jnp.bfloat16), unit, scale


def norm_backward(grad, unit, scale, gain):
    grad_gain = jnp.sum(grad * unit, axis=0)
    grad_shift = jnp.sum(grad, axis=0)
    scaled = grad * gain
    inner = jnp.mean(scaled * unit, axis=-1, keepdims=True)
    outer = jnp.mean(scaled, axis=-1, keepdims=True)
    return scale * (scaled - outer - unit * inner), grad_gain, grad_shift


def product(left, right, left_dim=1, right_dim=0, precision=None):
    return lax.dot_general(
        left, right, dims(left_dim, right_dim), precision=precision,
        preferred_element_type=jnp.float32,
    )


def pair_columns(weights):
    rows, columns = weights.shape
    width = columns // 2
    return weights.reshape(rows, 2, width // PAIR, PAIR).transpose(0, 2, 1, 3).reshape(rows, columns)


def unpair_columns(weights):
    rows, columns = weights.shape
    width = columns // 2
    return weights.reshape(rows, width // PAIR, 2, PAIR).transpose(0, 2, 1, 3).reshape(rows, columns)


def most_lanes(columns, most):
    return max(PAIR * i for i in range(1, most + 1) if columns % (PAIR * i) == 0)


def on_device(
    token_ids,
    mask_rows,
    mask_labels,
    mask_counts,
    step_count,
    vocab_tables,
    attention,
    feed_in,
    feed_out,
    norm_params,
    first_tables,
    first_attention,
    first_feed_in,
    first_feed_out,
    first_norms,
    second_tables,
    second_attention,
    second_feed_in,
    second_feed_out,
    second_norms,
    ema_tables,
    ema_attention,
    ema_feed_in,
    ema_feed_out,
    ema_norms,
):
    master = (vocab_tables, attention, feed_in, feed_out, norm_params)
    firsts = (first_tables, first_attention, first_feed_in, first_feed_out, first_norms)
    seconds = (second_tables, second_attention, second_feed_in, second_feed_out, second_norms)
    averages = (ema_tables, ema_attention, ema_feed_in, ema_feed_out, ema_norms)
    group_rates = (learn_rate, learn_rate, learn_rate, learn_rate, norm_rate)
    low = jnp.bfloat16

    shards = lax.axis_size("seq")
    devices = shards * lax.axis_size("dp")
    windows, span = token_ids.shape
    slots = mask_rows.shape[1]
    vocab = vocab_tables.shape[2]
    padded = vocab + -vocab % PAIR
    rows, columns = attention.shape
    width = columns // 4
    hidden_width = feed_in.shape[1] // 2
    folds = feed_out.shape[0] // rows
    length = span * shards
    spot = lax.axis_index("seq")

    tables_sent = jnp.pad(vocab_tables, ((0, 0), (0, 0), (0, padded - vocab)))
    table_sent = tables_sent[0].astype(low)
    attn_sent = jnp.concatenate(
        [
            attention[:, :width],
            pair_columns(attention[:, width : 3 * width]),
            attention[:, 3 * width :],
        ],
        axis=1,
    ).astype(low)
    in_sent = feed_in.reshape(rows, 2, hidden_width // folds, folds).transpose(0, 1, 3, 2)
    late_sent = jnp.concatenate(
        [
            in_sent.reshape(rows, 2 * hidden_width),
            feed_out.reshape(rows, folds * width),
            tables_sent[1],
        ],
        axis=1,
    ).astype(low)

    small = jnp.concatenate(
        [
            token_ids.reshape(-1).astype(jnp.float32),
            mask_rows.reshape(-1).astype(jnp.float32),
            mask_labels.reshape(-1).astype(jnp.float32),
            mask_counts.reshape(-1).astype(jnp.float32),
            norm_params.astype(low).astype(jnp.float32).reshape(-1),
        ]
    )
    small = jnp.pad(small, (0, -small.shape[0] % (8 * PAIR))).reshape(8, -1)
    small_all, table = gather_rows((small, table_sent), (1, 11), 3)
    late_sent, attn_sent, small_all, table = lax.optimization_barrier(
        (late_sent, attn_sent, small_all, table)
    )
    late = lax.all_gather(late_sent, AXES, axis=0, tiled=True)
    (attn,) = gather_rows((attn_sent,), (10,), 5)
    small_all = small_all.reshape(devices, -1)
    out_w = attn[:, 3 * width :]
    head_w = late[:, 2 * hidden_width + folds * width :]
    cuts = [windows * span, windows * slots, windows * slots, windows]
    marks = [sum(cuts[:i]) for i in range(len(cuts) + 1)]
    gains = small_all[:, marks[4] : marks[4] + rows * 6].reshape(devices * rows, 6)
    count = jnp.sum(small_all[:, marks[3] : marks[4]])
    group = lax.dynamic_slice_in_dim(small_all, lax.axis_index("dp") * shards, shards, axis=0)

    def in_order(first, last):
        piece = group[:, first:last].reshape(shards, windows, -1)
        return piece.transpose(1, 0, 2).reshape(windows * shards, -1)

    ids = in_order(marks[0], marks[1]).astype(jnp.int32)
    block = spot * windows + jnp.arange(windows, dtype=jnp.int32)

    def mine(first, last):
        return lax.dynamic_slice_in_dim(in_order(first, last), spot * windows, windows, axis=0)

    own_rows = mine(marks[1], marks[2]).astype(jnp.int32)
    own_labels = mine(marks[2], marks[3]).astype(jnp.int32).reshape(-1)
    own_counts = mine(marks[3], marks[4])
    live = (jnp.arange(slots, dtype=jnp.float32)[None, :] < own_counts).astype(jnp.float32)
    live = live.reshape(-1)

    base = first_window(spot * windows, shards, windows)
    wins = block // shards - base
    offset = (spot * windows - base * shards) * span
    ids_two = lax.dynamic_slice_in_dim(ids, base * shards, 2 * shards, axis=0).reshape(-1)
    positions = ((block % shards)[:, None] * span + jnp.arange(span, dtype=jnp.int32)).reshape(-1)
    rope_q = rope_tables(positions)
    rope_k = rope_tables(jnp.arange(length, dtype=jnp.int32))
    tokens = windows * span

    def own(values):
        return lax.dynamic_slice_in_dim(values, offset, tokens, axis=0)

    embedded_two, onehot, normed_one, stats = embed(
        ids_two[:, None], table, 0, padded, gains[:, 0][None], gains[:, 1][None], length // 2
    )
    normed_own = own(normed_one)
    queries = project(normed_own, attn, 0, width, rope_q, tokens, "all")
    key_values = project(normed_one, attn, width, 2 * width, rope_k, length, "half")
    mixture, totals = attend_forward(wins, queries, key_values, span, length)
    after_attn = own(embedded_two) + product(mixture, out_w)

    normed_two, unit_two, scale_two = norm_forward(after_attn, gains[:, 2], gains[:, 3])
    gate, up, hidden = gate_forward(normed_two, late, hidden_width)
    after_feed = down_forward(hidden, late, after_attn, 2 * hidden_width)

    pick = (own_rows[:, :, None] == jnp.arange(span, dtype=jnp.int32)).astype(jnp.float32)
    selected = jnp.einsum(
        "wsp,wpd->wsd", pick, after_feed.reshape(windows, span, width),
        precision=lax.Precision.HIGHEST, preferred_element_type=jnp.float32,
    ).reshape(windows * slots, width)
    normed_final, unit_final, scale_final = norm_forward(selected, gains[:, 4], gains[:, 5])
    column = jnp.arange(padded, dtype=jnp.int32)[None, :]
    logits = jnp.where(column < vocab, product(normed_final, head_w), -jnp.inf)
    log_total = jax.nn.logsumexp(logits, axis=-1)
    wanted = own_labels[:, None] == column
    picked = jnp.sum(jnp.where(wanted, logits, 0.0), axis=-1)
    loss_part = jnp.sum(live * (log_total - picked))

    grad_logits = (
        (jnp.exp(logits - log_total[:, None]) - wanted.astype(jnp.float32)) * (live / count)[:, None]
    ).astype(low)
    grad_selected, grad_gain_final, grad_shift_final = norm_backward(
        product(grad_logits, head_w, 1, 1), unit_final, scale_final, gains[:, 4]
    )
    grad_after_feed = jnp.einsum(
        "wsp,wsd->wpd", pick, grad_selected.reshape(windows, slots, width),
        precision=lax.Precision.HIGHEST, preferred_element_type=jnp.float32,
    ).reshape(tokens, width)
    rounded_feed = grad_after_feed.astype(low)
    order = (lax.axis_size("dp"), shards)
    spare = ((0, -grad_logits.shape[0] % PAIR), (0, 0))
    late_grads = weight_grad(
        jnp.pad(normed_final, spare), (jnp.pad(grad_logits, spare),), order, most_lanes(padded, 11),
        padded + folds * width,
    )
    late_grads = down_grad(hidden, rounded_feed, late_grads, padded, order)
    rounded_feed, late_grads = lax.optimization_barrier((rounded_feed, late_grads))
    late_part = lax.psum_scatter(late_grads, "seq", scatter_dimension=0, tiled=True)
    grad_gate, grad_up = gate_backward(rounded_feed, late, gate, up, 2 * hidden_width)
    alone = (1, 1)
    in_grads = weight_grad(normed_two, (grad_gate, grad_up), alone)

    grad_inner, grad_gain_two, grad_shift_two = norm_backward(
        input_grad((grad_gate, grad_up), late, (0, hidden_width)), unit_two, scale_two, gains[:, 2]
    )
    grad_after_attn = grad_after_feed + grad_inner
    rounded_attn = grad_after_attn.astype(low)
    grad_mixture = product(rounded_attn, out_w, 1, 1).astype(low)
    grad_queries, grad_pairs, in_own = attend_backward(
        queries, key_values, grad_mixture, totals, rope_q, rope_k, in_grads, span, length, 2
    )
    grad_queries, late_part = lax.optimization_barrier((grad_queries, late_part))
    late_own = lax.psum_scatter(late_part, "dp", scatter_dimension=0, tiled=True)
    attn_grads = weight_grad(mixture, (rounded_attn,), alone, width // 2, columns, None, 3 * width)
    attn_grads = weight_grad(normed_own, (grad_queries,), alone, width // 2, None, attn_grads)
    attn_grads = weight_grad(normed_one, (grad_pairs,), alone, width // 2, None, attn_grads, width)
    tiles = jnp.stack([offset // span, jnp.int32(windows)])
    grad_embedded, sums_one = normed_grad(
        tiles, grad_pairs, grad_queries, attn, embedded_two, stats, grad_after_attn, gains[:, 0][None], span
    )
    grad_gain_one, grad_shift_one = sums_one[0], sums_one[1]
    grad_norms = jnp.stack(
        [
            grad_gain_one,
            grad_shift_one,
            grad_gain_two,
            grad_shift_two,
            grad_gain_final,
            grad_shift_final,
        ],
        axis=1,
    )
    grad_norms = jnp.pad(grad_norms, ((0, 0), (0, PAIR - grad_norms.shape[1]))).astype(low)
    late_own = late_own.astype(jnp.float32)
    squares = jnp.sum(late_own * late_own) + jnp.sum(in_own * in_own)
    late_final = (
        late_own[:, :vocab],
        in_own.reshape(rows, 2, folds, hidden_width // folds).transpose(0, 1, 3, 2).reshape(rows, 2 * hidden_width),
        late_own[:, padded:].reshape(rows * folds, width),
    )
    grad_embedded, (head_own, in_own, down_own) = lax.optimization_barrier((grad_embedded, late_final))
    attn_own, table_own, (squares_all, loss_all) = embed_grad(
        grad_embedded, onehot, grad_norms, attn_grads, (squares, loss_part), most_lanes(padded, 4), 1
    )
    grads = (
        jnp.stack([table_own[:, :vocab], head_own], axis=0),
        jnp.concatenate(
            [
                attn_own[:, :width],
                unpair_columns(attn_own[:, width : 3 * width]),
                attn_own[:, 3 * width :],
            ],
            axis=1,
        ),
        in_own,
        down_own,
        table_own[:, padded : padded + 6],
    )
    masked_loss = loss_all / count
    total_norm = jnp.sqrt(squares_all)
    limit = (slots * shards * windows * lax.axis_size("dp")) ** (-0.5)
    clip = jnp.minimum(1.0, limit / (total_norm + 1e-06))
    steps = step_count[0].astype(jnp.float32)
    fix_one = 1.0 - beta_one**steps
    fix_two = 1.0 - beta_two**steps
    weights_new, firsts_new, seconds_new, averages_new = ([], [], [], [])
    for weight, grad, first, second, average, step_rate in zip(
        master, grads, firsts, seconds, averages, group_rates
    ):
        scaled = grad * clip
        first_next = beta_one * first + (1.0 - beta_one) * scaled
        second_next = beta_two * second + (1.0 - beta_two) * scaled * scaled
        update = (
            first_next / fix_one / (jnp.sqrt(second_next / fix_two) + adam_eps)
            + weight_decay * weight
        )
        weight_next = weight - step_rate * update
        weights_new.append(weight_next)
        firsts_new.append(first_next)
        seconds_new.append(second_next)
        averages_new.append(ema_decay * average + (1.0 - ema_decay) * weight_next)
    return (masked_loss, total_norm, *weights_new, *firsts_new, *seconds_new, *averages_new)


def solution(mesh):
    split = P(AXES, None)
    tables = P(None, AXES, None)
    weights = (tables, split, split, split, split)
    return jax.shard_map(
        on_device,
        mesh=mesh,
        in_specs=(P("dp", "seq"),) * 4 + (P(),) + weights * 4,
        out_specs=(P(), P()) + weights * 4,
        check_vma=False,
    )
```

```python
import functools
import math
import jax, jax.numpy as jnp
from jax import lax
from jax.experimental import pallas as pl
from jax.experimental.pallas import tpu as pltpu
HEAD_DIM=64
PAIR=128
MB=1<<20
MESH = pl.DeviceIdType.MESH
norm_eps = 1e-05

def dims(a,b): return (((a,),(b,)),((),()))

def low_half(rows):
    lane = lax.broadcasted_iota(jnp.int32,(rows,PAIR),1)
    return lane % HEAD_DIM < HEAD_DIM//2

def turn(x, cosines, sines):
    low = low_half(x.shape[0])
    up = pltpu.roll(x, PAIR-HEAD_DIM//2, 1)
    down = pltpu.roll(x, HEAD_DIM//2, 1)
    return x*cosines + jnp.where(low,-up,down)*sines

def turn_back(g, cosines, sines):
    low = low_half(g.shape[0])
    up = pltpu.roll(g, PAIR-HEAD_DIM//2, 1)
    down = pltpu.roll(g, HEAD_DIM//2, 1)
    return g*cosines + jnp.where(low,up,-down)*sines

def head_mask(head):
    lane = lax.broadcasted_iota(jnp.int32,(1,PAIR),1)
    return (lane//HEAD_DIM==head).astype(jnp.float32).astype(jnp.bfloat16)

def by_head(rows):
    return jnp.concatenate([rows * head_mask(0), rows * head_mask(1)], axis=0)


def own_halves(mixed, span):
    own = [mixed[:HEAD_DIM, :span], mixed[HEAD_DIM:, span:]]
    return jnp.concatenate(own, axis=0).T


def forward_kernel(win_ref, q_ref, kv_ref, mix_ref, total_ref):
    queries = q_ref[...]
    keys = kv_ref[:, :PAIR]
    values = kv_ref[:, PAIR:]
    span = queries.shape[0]
    scores = lax.dot_general(keys, by_head(queries), dims(1, 1), preferred_element_type=jnp.float32)
    top = jnp.max(scores, axis=0, keepdims=True)
    chances = jnp.exp(scores - top)
    total = jnp.sum(chances, axis=0, keepdims=True)
    weights = (chances * (1.0 / total)).astype(jnp.bfloat16)
    mixed = lax.dot_general(values, weights, dims(0, 0), preferred_element_type=jnp.float32)
    mix_ref[...] = own_halves(mixed, span).astype(jnp.bfloat16)
    totals = top + jnp.log(total)
    for head in range(2):
        total_ref[0, 0, head : head + 1, :] = totals[:, head * span : (head + 1) * span]


def attend_forward(win, queries, key_values, span, length):
    tokens,width = queries.shape
    pairs = width//PAIR
    blocks = tokens//span
    return pl.pallas_call(
        forward_kernel,
        grid_spec=pltpu.PrefetchScalarGridSpec(
            num_scalar_prefetch=1, grid=(pairs,blocks),
            in_specs=[pl.BlockSpec((span,PAIR),lambda p,b,w:(b,p)),
                      pl.BlockSpec((length,2*PAIR),lambda p,b,w:(w[b],p))],
            out_specs=[pl.BlockSpec((span,PAIR),lambda p,b,w:(b,p)),
                       pl.BlockSpec((1,1,8,span),lambda p,b,w:(p,b,0,0))]),
        out_shape=[jax.ShapeDtypeStruct((tokens,width),jnp.bfloat16),
                   jax.ShapeDtypeStruct((pairs,blocks,8,span),jnp.float32)],
        compiler_params=pltpu.CompilerParams(vmem_limit_bytes=56*MB),
        cost_estimate=pl.CostEstimate(flops=4*tokens*length*width,bytes_accessed=16*MB,transcendentals=tokens*length*width//HEAD_DIM),
        name="attend_forward",
    )(win,queries,key_values)


def backward_kernel(windows, shards, sizes, chunks, q_ref, kv_ref, grad_ref, total_ref, cosq_ref, sinq_ref, cosk_ref,
                    sink_ref, wire_ref, gq_ref, gkv_ref, own_ref, acc_ref, *scratch):
    block = pl.program_id(1)
    blocks = pl.num_programs(1)
    step = pl.program_id(0) * blocks + block
    length = cosk_ref.shape[0]
    steps = Scatter(sizes, chunks, wire_ref, own_ref, *scratch)

    @pl.when(step == 0)
    def _():
        steps.begin()

    for number in range(steps.ticks):
        @pl.when(step == 2 * number + 1)
        def _():
            steps.tick(number)

    @pl.when(block == 0)
    def _():
        acc_ref[...] = jnp.zeros_like(acc_ref)

    spot = lax.axis_index("seq") * blocks
    start = pl.multiple_of(((spot + block) // shards - first_window(spot, shards, windows)) * length, length)
    span = pl.ds(start, length)
    queries = q_ref[...]
    keys = kv_ref[span, :PAIR]
    values = kv_ref[span, PAIR:]
    grads = grad_ref[...]
    queries = by_head(queries)
    grads = by_head(grads)
    totals = jnp.concatenate([total_ref[0, 0, head : head + 1, :] for head in range(2)], axis=1)
    scores = lax.dot_general(keys, queries, dims(1, 1), preferred_element_type=jnp.float32)
    chances = jnp.exp(scores - totals)
    acc_ref[span, PAIR:] += jnp.dot(chances.astype(jnp.bfloat16), grads, preferred_element_type=jnp.float32)
    grad_chances = lax.dot_general(values, grads, dims(1, 1), preferred_element_type=jnp.float32)
    both = chances * grad_chances
    inner = jnp.sum(both, axis=0, keepdims=True)
    grad_scores = (both - chances * inner).astype(jnp.bfloat16)
    acc_ref[span, :PAIR] += jnp.dot(grad_scores, queries, preferred_element_type=jnp.float32)
    grad_q = lax.dot_general(keys, grad_scores, dims(0, 0), preferred_element_type=jnp.float32)
    grad_q = own_halves(grad_q, q_ref.shape[0]) * (HEAD_DIM**-0.5)
    gq_ref[...] = turn_back(grad_q, cosq_ref[...], sinq_ref[...]).astype(jnp.bfloat16)

    @pl.when(block == blocks - 1)
    def _():
        for w in range(acc_ref.shape[0] // length):
            rows = pl.ds(w * length, length)
            gkv_ref[rows, :PAIR] = turn_back(acc_ref[rows, :PAIR], cosk_ref[...], sink_ref[...]).astype(jnp.bfloat16)
            gkv_ref[rows, PAIR:] = acc_ref[rows, PAIR:].astype(jnp.bfloat16)

    @pl.when(step == pl.num_programs(0) * blocks - 1)
    def _():
        steps.end()


def first_window(spot, shards, windows):
    window = spot // shards
    return window - window // (windows - 1)


def attend_backward(queries, key_values, grads, totals, rope_q, rope_k, wire, span, length, collective_id):
    tokens, width = queries.shape
    pairs = width // PAIR
    blocks = tokens // span
    all_rows = key_values.shape[0]
    sizes = grid_sizes()
    total, columns = wire.shape
    rows = total // math.prod(sizes)
    count = min(16, 2 * ((pairs * blocks - 2) // 2 - 3))
    block = pl.BlockSpec((span, PAIR), lambda p, b: (b, p))
    rope_block = pl.BlockSpec((span, PAIR), lambda p, b: (b, 0))
    whole = pl.BlockSpec((length, PAIR), lambda p, b: (0, 0), pipeline_mode=pl.Buffered(1))
    return pl.pallas_call(
        functools.partial(backward_kernel, blocks, length // span, sizes, column_chunks(columns, count)),
        grid=(pairs, blocks),
        in_specs=[
            block,
            pl.BlockSpec((all_rows, 2 * PAIR), lambda p, b: (0, p)),
            block,
            pl.BlockSpec((1, 1, 8, span), lambda p, b: (p, b, 0, 0)),
            rope_block, rope_block, whole, whole,
            pl.BlockSpec(memory_space=pl.ANY),
        ],
        out_specs=[
            block,
            pl.BlockSpec((all_rows, 2 * PAIR), lambda p, b: (0, p)),
            pl.BlockSpec((rows, columns), lambda p, b: (0, 0)),
        ],
        scratch_shapes=[pltpu.VMEM((all_rows, 2 * PAIR), jnp.float32)] + scatter_scratch(sizes, rows, columns, count),
        out_shape=[
            jax.ShapeDtypeStruct((tokens, width), jnp.bfloat16),
            jax.ShapeDtypeStruct((all_rows, 2 * width), jnp.bfloat16),
            jax.ShapeDtypeStruct((rows, columns), jnp.float32),
        ],
        compiler_params=pltpu.CompilerParams(
            collective_id=collective_id, has_side_effects=True, vmem_limit_bytes=60 * MB
        ),
        cost_estimate=pl.CostEstimate(
            flops=10 * tokens * length * width, bytes_accessed=48 * MB, transcendentals=tokens * length * width // HEAD_DIM
        ),
        name="attend_backward",
    )(queries, key_values, grads, totals, *rope_q, *rope_k, wire.reshape(*sizes, rows, columns))


def cost(flops, moved):
    return pl.CostEstimate(flops=flops, bytes_accessed=moved, transcendentals=0)


def gate_kernel(x_ref, gate_w_ref, up_w_ref, gate_ref, up_ref, hidden_ref):
    gate = jnp.dot(x_ref[...], gate_w_ref[...], preferred_element_type=jnp.float32)
    up = jnp.dot(x_ref[...], up_w_ref[...], preferred_element_type=jnp.float32)
    gate_ref[...] = gate.astype(jnp.bfloat16)
    up_ref[...] = up.astype(jnp.bfloat16)
    hidden_ref[...] = (gate * jax.nn.sigmoid(gate) * up).astype(jnp.bfloat16)


def gate_forward(x, weights, hidden_width, wide=512, tile=None):
    tokens, width = x.shape
    tile = tile or tokens
    shift = hidden_width // wide
    spot = lambda n, m: (m, n)
    return pl.pallas_call(
        gate_kernel,
        grid=(hidden_width // wide, tokens // tile),
        in_specs=[
            pl.BlockSpec((tile, width), lambda n, m: (m, 0)),
            pl.BlockSpec((width, wide), lambda n, m: (0, n)),
            pl.BlockSpec((width, wide), lambda n, m: (0, n + shift)),
        ],
        out_specs=[pl.BlockSpec((tile, wide), spot)] * 3,
        out_shape=[
            jax.ShapeDtypeStruct((tokens, hidden_width), jnp.bfloat16),
            jax.ShapeDtypeStruct((tokens, hidden_width), jnp.bfloat16),
            jax.ShapeDtypeStruct((tokens, hidden_width), jnp.bfloat16),
        ],
        compiler_params=pltpu.CompilerParams(vmem_limit_bytes=48 * MB),
        cost_estimate=cost(4 * tokens * width * hidden_width, 10 * tokens * hidden_width + 4 * width * hidden_width),
        name="gate_forward",
    )(x, weights, weights)


def down_kernel(hidden_ref, w_ref, base_ref, out_ref):
    part = jnp.dot(hidden_ref[...], w_ref[...], preferred_element_type=jnp.float32)

    @pl.when(pl.program_id(1) == 0)
    def _():
        out_ref[...] = base_ref[...] + part

    @pl.when(pl.program_id(1) > 0)
    def _():
        out_ref[...] += part


def down_forward(hidden, weights, base, first, tile=None):
    tokens, width = base.shape
    tile = tile or tokens
    folds = hidden.shape[1] // width
    shift = first // width
    return pl.pallas_call(
        down_kernel,
        grid=(tokens // tile, folds),
        in_specs=[
            pl.BlockSpec((tile, width), lambda m, f: (m, f)),
            pl.BlockSpec((width, width), lambda m, f: (0, f + shift)),
            pl.BlockSpec((tile, width), lambda m, f: (m, 0)),
        ],
        out_specs=pl.BlockSpec((tile, width), lambda m, f: (m, 0)),
        out_shape=jax.ShapeDtypeStruct((tokens, width), jnp.float32),
        compiler_params=pltpu.CompilerParams(vmem_limit_bytes=48 * MB),
        cost_estimate=cost(2 * tokens * width * folds * width, 12 * tokens * width + 2 * folds * width * width),
        name="down_forward",
    )(hidden, weights, base)


def gate_back_kernel(grad_ref, w_ref, gate_ref, up_ref, grad_gate_ref, grad_up_ref):
    grad_hidden = lax.dot_general(grad_ref[...], w_ref[...], dims(1, 1), preferred_element_type=jnp.float32)
    gate = gate_ref[...].astype(jnp.float32)
    sigmoid = jax.nn.sigmoid(gate)
    grad_up_ref[...] = (grad_hidden * (gate * sigmoid)).astype(jnp.bfloat16)
    grad_gate_ref[...] = (
        grad_hidden * up_ref[...].astype(jnp.float32) * (sigmoid * (1.0 + gate * (1.0 - sigmoid)))
    ).astype(jnp.bfloat16)


def gate_backward(grad, weights, gate, up, first, wide=512, tile=None):
    tokens, width = grad.shape
    tile = tile or tokens
    hidden_width = gate.shape[1]
    per = width // wide
    shift = first // width
    spot = lambda n, m: (m, n)
    return pl.pallas_call(
        gate_back_kernel,
        grid=(hidden_width // wide, tokens // tile),
        in_specs=[
            pl.BlockSpec((tile, width), lambda n, m: (m, 0)),
            pl.BlockSpec((wide, width), lambda n, m: (lax.rem(n, per), n // per + shift)),
            pl.BlockSpec((tile, wide), spot),
            pl.BlockSpec((tile, wide), spot),
        ],
        out_specs=[pl.BlockSpec((tile, wide), spot)] * 2,
        out_shape=[jax.ShapeDtypeStruct((tokens, hidden_width), jnp.bfloat16)] * 2,
        compiler_params=pltpu.CompilerParams(vmem_limit_bytes=48 * MB),
        cost_estimate=cost(2 * tokens * width * hidden_width, 12 * tokens * hidden_width + 2 * width * hidden_width),
        name="gate_backward",
    )(grad, weights, gate, up)


def swap_rows(out, value, order):
    outer, inner = order
    rows = value.shape[0] // (outer * inner)
    for i in range(outer):
        for j in range(inner):
            spot, source = (j * outer + i) * rows, (i * inner + j) * rows
            out[spot : spot + rows, :] = value[source : source + rows, :]


def weight_kernel(sides, order, left_ref, *refs):
    out_ref, turned = refs[-2], refs[-1]

    @pl.when(pl.program_id(0) == 0)
    def _():
        swap_rows(turned, left_ref[...].T, order)

    per = pl.num_programs(0) // sides
    for side in range(sides):
        @pl.when(pl.program_id(0) // per == side)
        def _():
            out_ref[...] = jnp.dot(
                turned[...], refs[side][...], preferred_element_type=jnp.float32
            ).astype(jnp.bfloat16)


def weight_grad(left, rights, order, wide=1024, total=None, filled=None, first=0):
    tokens, width = left.shape
    sides, columns = len(rights), rights[0].shape[1]
    per = columns // wide
    return pl.pallas_call(
        functools.partial(weight_kernel, sides, order),
        grid=(sides * per,),
        in_specs=[pl.BlockSpec((tokens, width), lambda n: (0, 0))]
        + [
            pl.BlockSpec((tokens, wide), lambda n, s=s: (0, jnp.clip(n - s * per, 0, per - 1)))
            for s in range(sides)
        ]
        + [pl.BlockSpec(memory_space=pl.ANY)] * (filled is not None),
        out_specs=pl.BlockSpec(
            (pl.Element(width), pl.Element(wide)),
            lambda n: (0, pl.multiple_of(first + n * wide, PAIR)),
        ),
        out_shape=jax.ShapeDtypeStruct(
            filled.shape if filled is not None else (width, total or sides * columns), jnp.bfloat16
        ),
        input_output_aliases={} if filled is None else {1 + sides: 0},
        scratch_shapes=[pltpu.VMEM((width, tokens), jnp.bfloat16)],
        compiler_params=pltpu.CompilerParams(vmem_limit_bytes=56 * MB),
        cost_estimate=cost(2 * tokens * width * sides * columns, 4 * (tokens + width) * sides * columns),
        name="weight_grad",
    )(left, *rights, *([] if filled is None else [filled]))


def down_grad_kernel(order, hidden_ref, grad_ref, filled_ref, out_ref):
    value = lax.dot_general(
        hidden_ref[...], grad_ref[...], dims(0, 0), preferred_element_type=jnp.float32
    )
    swap_rows(out_ref, value.astype(jnp.bfloat16), order)


def down_grad(hidden, grad, filled, first, order):
    tokens, width = grad.shape
    folds = hidden.shape[1] // width
    return pl.pallas_call(
        functools.partial(down_grad_kernel, order),
        grid=(folds,),
        in_specs=[
            pl.BlockSpec((tokens, width), lambda f: (0, f)),
            pl.BlockSpec((tokens, width), lambda f: (0, 0)),
            pl.BlockSpec(memory_space=pl.ANY),
        ],
        out_specs=pl.BlockSpec(
            (pl.Element(width), pl.Element(width)), lambda f: (0, pl.multiple_of(first + f * width, PAIR))
        ),
        out_shape=jax.ShapeDtypeStruct(filled.shape, jnp.bfloat16),
        input_output_aliases={2: 0},
        compiler_params=pltpu.CompilerParams(vmem_limit_bytes=48 * MB),
        cost_estimate=cost(2 * tokens * width * folds * width, 4 * tokens * folds * width),
        name="down_grad",
    )(hidden, grad, filled)


def input_kernel(sides, first_ref, *refs):
    grads, weights, out_ref = refs[:sides], refs[sides:2 * sides], refs[2 * sides]
    part = None
    for grad_ref, w_ref in zip(grads, weights):
        term = lax.dot_general(grad_ref[...], w_ref[...], dims(1, 1), preferred_element_type=jnp.float32)
        part = term if part is None else part + term

    @pl.when(pl.program_id(1) == 0)
    def _():
        out_ref[...] = part

    @pl.when(pl.program_id(1) > 0)
    def _():
        out_ref[...] += part


def input_grad(grads, weights, firsts, wide=1024, tile=None):
    tokens, columns = grads[0].shape
    width = weights.shape[0]
    tile = tile or tokens
    sides = len(grads)
    return pl.pallas_call(
        lambda *refs: input_kernel(sides, None, *refs),
        grid=(tokens // tile, columns // wide),
        in_specs=[pl.BlockSpec((tile, wide), lambda m, k: (m, k))] * sides
        + [
            pl.BlockSpec((width, wide), lambda m, k, first=first: (0, k + first // wide))
            for first in firsts
        ],
        out_specs=pl.BlockSpec((tile, width), lambda m, k: (m, 0)),
        out_shape=jax.ShapeDtypeStruct((tokens, width), jnp.float32),
        compiler_params=pltpu.CompilerParams(vmem_limit_bytes=48 * MB),
        cost_estimate=cost(2 * sides * tokens * width * columns, 2 * sides * (tokens + width) * columns),
        name="input_grad",
    )(*grads, *([weights] * sides))


def onehot_block(ids, first, wide):
    columns = lax.broadcasted_iota(jnp.int32, (ids.shape[0], wide), 1) + first
    return (ids == columns).astype(jnp.float32).astype(jnp.bfloat16)


def embed_kernel(ids_ref, table_ref, gain_ref, shift_ref, out_ref, onehot_ref, normed_ref, stats_ref):
    wide = table_ref.shape[1]
    step = pl.program_id(1)
    onehot = onehot_block(ids_ref[...], step * wide, wide)
    onehot_ref[...] = onehot
    part = lax.dot_general(onehot, table_ref[...], dims(1, 1), preferred_element_type=jnp.float32)

    @pl.when(step == 0)
    def _():
        out_ref[...] = part

    @pl.when(step > 0)
    def _():
        out_ref[...] += part

    @pl.when(step == pl.num_programs(1) - 1)
    def _():
        values = out_ref[...]
        mean = jnp.mean(values, axis=-1, keepdims=True)
        centre = values - mean
        scale = lax.rsqrt(jnp.mean(centre * centre, axis=-1, keepdims=True) + norm_eps)
        normed_ref[...] = (centre * scale * gain_ref[...] + shift_ref[...]).astype(jnp.bfloat16)
        stats_ref[:, :PAIR] = jnp.broadcast_to(mean, (values.shape[0], PAIR))
        stats_ref[:, PAIR:] = jnp.broadcast_to(scale, (values.shape[0], PAIR))


def embed(ids, weights, first, columns, gain, shift, tile):
    tokens, width = ids.shape[0], weights.shape[0]
    wide = max(PAIR * i for i in range(1, 12) if columns % (PAIR * i) == 0)
    spot = lambda m, k: (m, 0)
    return pl.pallas_call(
        embed_kernel,
        grid=(tokens // tile, columns // wide),
        in_specs=[
            pl.BlockSpec((tile, 1), spot),
            pl.BlockSpec(
                (pl.Element(width), pl.Element(wide)),
                lambda m, k: (0, pl.multiple_of(first + k * wide, PAIR)),
            ),
            pl.BlockSpec((1, width), lambda m, k: (0, 0)),
            pl.BlockSpec((1, width), lambda m, k: (0, 0)),
        ],
        out_specs=[
            pl.BlockSpec((tile, width), spot),
            pl.BlockSpec((tile, wide), lambda m, k: (m, k)),
            pl.BlockSpec((tile, width), spot),
            pl.BlockSpec((tile, 2 * PAIR), spot),
        ],
        out_shape=[
            jax.ShapeDtypeStruct((tokens, width), jnp.float32),
            jax.ShapeDtypeStruct((tokens, columns), jnp.bfloat16),
            jax.ShapeDtypeStruct((tokens, width), jnp.bfloat16),
            jax.ShapeDtypeStruct((tokens, 2 * PAIR), jnp.float32),
        ],
        compiler_params=pltpu.CompilerParams(vmem_limit_bytes=58 * MB),
        cost_estimate=cost(
            2 * tokens * width * columns, 4 * tokens * width + 2 * (width + tokens) * columns
        ),
        name="embed",
    )(ids, weights, gain, shift)


def normed_grad_kernel(shards, windows, blocks, sizes, chunks, pairs_ref, low_w_ref, high_w_ref, queries_ref, query_w_ref, values_ref,
                       stats_ref, later_ref, gain_ref, wire_ref, out_ref, sums_ref, own_ref, *scratch):
    step = pl.program_id(0)
    tile = out_ref.shape[0]
    steps = Scatter(sizes, chunks, wire_ref, own_ref, *scratch)

    @pl.when(step == 0)
    def _():
        steps.begin()
        sums_ref[...] = jnp.zeros_like(sums_ref)

    for number in range(steps.ticks):
        @pl.when(step == number + 1)
        def _():
            steps.tick(number)

    spot = lax.axis_index("seq") * blocks
    first = spot - first_window(spot, shards, windows) * shards
    width = out_ref.shape[1]
    spots = lax.broadcasted_iota(jnp.int32, (1, width), 1) * 0 + (step - first)
    mine = jnp.where(spots < 0, 0.0, jnp.where(spots < blocks, 1.0, 0.0))
    place = lax.rem(step + 2 * shards * blocks - first, blocks)
    here = pl.ds(pl.multiple_of(place * tile, tile), tile)
    grad = lax.dot_general(
        pairs_ref[:, :width], low_w_ref[...], dims(1, 1), preferred_element_type=jnp.float32
    )
    grad = grad + lax.dot_general(
        pairs_ref[:, width:], high_w_ref[...], dims(1, 1), preferred_element_type=jnp.float32
    )
    grad = grad + mine * lax.dot_general(
        queries_ref[here, :], query_w_ref[...], dims(1, 1), preferred_element_type=jnp.float32
    )
    scale = stats_ref[:, PAIR : PAIR + 1]
    unit = (values_ref[...] - stats_ref[:, :1]) * scale
    scaled = grad * gain_ref[...]
    inner = jnp.mean(scaled * unit, axis=-1, keepdims=True)
    outer = jnp.mean(scaled, axis=-1, keepdims=True)
    passed = scale * (scaled - outer - unit * inner)
    out_ref[...] = (passed + mine * later_ref[here, :]).astype(jnp.bfloat16)
    sums_ref[0:1, :] += jnp.sum(grad * unit, axis=0, keepdims=True)
    sums_ref[1:2, :] += jnp.sum(grad, axis=0, keepdims=True)

    @pl.when(step == pl.num_programs(0) - 1)
    def _():
        for number in range(steps.ticks):
            if number + 1 > 2 * shards - 1:
                steps.tick(number)
        steps.end()


def normed_grad(grad_pairs, grad_queries, weights, values, stats, later, gain, wire, shards, windows, tile, collective_id):
    tokens, width = values.shape
    blocks = grad_queries.shape[0] // tile
    sizes = grid_sizes()
    rows = wire.shape[0] // math.prod(sizes)
    count = 10
    row = lambda m: (m, 0)
    once = dict(pipeline_mode=pl.Buffered(1))
    whole = pl.BlockSpec(memory_space=pltpu.VMEM)
    return pl.pallas_call(
        functools.partial(
            normed_grad_kernel, shards, windows, blocks, sizes, column_chunks(wire.shape[1], count)
        ),
        grid=(tokens // tile,),
        in_specs=[
            pl.BlockSpec((tile, 2 * width), row),
            pl.BlockSpec((width, width), lambda m: (0, 1), **once),
            pl.BlockSpec((width, width), lambda m: (0, 2), **once),
            whole,
            pl.BlockSpec((width, width), lambda m: (0, 0), **once),
            pl.BlockSpec((tile, width), row),
            pl.BlockSpec((tile, 2 * PAIR), row),
            whole,
            pl.BlockSpec((1, width), lambda m: (0, 0)),
            pl.BlockSpec(memory_space=pl.ANY),
        ],
        out_specs=[
            pl.BlockSpec((tile, width), row),
            pl.BlockSpec((8, width), lambda m: (0, 0)),
            pl.BlockSpec((rows, wire.shape[1]), lambda m: (0, 0)),
        ],
        out_shape=[
            jax.ShapeDtypeStruct((tokens, width), jnp.bfloat16),
            jax.ShapeDtypeStruct((8, width), jnp.float32),
            jax.ShapeDtypeStruct((rows, wire.shape[1]), jnp.float32),
        ],
        scratch_shapes=scatter_scratch(sizes, rows, wire.shape[1], count),
        compiler_params=pltpu.CompilerParams(
            collective_id=collective_id, has_side_effects=True, vmem_limit_bytes=58 * MB
        ),
        cost_estimate=cost(6 * tokens * width * width, 16 * tokens * width + 6 * width * width),
        name="normed_grad",
    )(grad_pairs, weights, weights, grad_queries, weights, values, stats, later, gain, wire.reshape(*sizes, rows, -1))


def embed_grad_kernel(sizes, chunks, left_ref, onehot_ref, norms_ref, tile_ref, table_own_ref, total_ref, turned, grads,
                      *scratch):
    step, last = pl.program_id(0), pl.num_programs(0) - 1
    table = Scatter(sizes, chunks, grads, table_own_ref, None, *scratch[:6])
    slots = dict(zip("zyxc", scratch[6:10]))
    norm_piece = len(chunks) - 1

    @pl.when(step == 0)
    def _():
        table.place.greet()
        grads[:, :, :, :, :, chunks[norm_piece]] = norms_ref[...]
        table.send(norm_piece, 0)
        turned[...] = left_ref[...].T

    block = jnp.dot(turned[...], onehot_ref[...], preferred_element_type=jnp.float32).astype(jnp.bfloat16)
    for number in range(norm_piece):
        @pl.when(step == number)
        def _():
            grads[:, :, :, :, :, chunks[number]] = block.reshape(*grads.shape[:5], block.shape[1])
            table.send(number, 0)
            for stage in range(3):
                if number - 1 - stage >= 0:
                    table.advance(number - 1 - stage, stage)

    @pl.when(step == last)
    def _():
        done = {number: len([s for s in range(3) if number + 1 + s < norm_piece]) for number in range(norm_piece)}
        done[norm_piece] = 0
        for stage in range(4):
            for number in range(norm_piece + 1):
                if done[number] <= stage:
                    table.advance(number, stage)
        squares = jnp.zeros((), jnp.float32)
        for cols in chunks:
            squares = squares + jnp.sum(table_own_ref[:, cols] * table_own_ref[:, cols])
        row = lax.broadcasted_iota(jnp.int32, (8, PAIR), 0)
        value = tile_ref[...] + jnp.where(row == 0, squares, 0.0)
        value, started = total_steps(table.place, value, slots, *scratch[10:])
        total_ref[...] = value
        for copy in started:
            copy.wait_send()
        table.end()


def embed_grad(left, onehot, norms, values, wide, collective_id):
    tokens, width = left.shape
    columns = onehot.shape[1]
    sizes = grid_sizes()
    rows = width // math.prod(sizes)
    chunks = [pl.ds(start, wide) for start in range(0, columns, wide)] + [pl.ds(columns, PAIR)]
    row = lax.broadcasted_iota(jnp.int32, (8, PAIR), 0)
    tile = jnp.zeros((8, PAIR), jnp.float32)
    for i, value in enumerate(values):
        tile = jnp.where(row == i, value, tile)
    total_columns = columns + PAIR
    table_own, totals = pl.pallas_call(
        functools.partial(embed_grad_kernel, sizes, chunks),
        grid=(columns // wide,),
        in_specs=[
            pl.BlockSpec((tokens, width), lambda n: (0, 0), pipeline_mode=pl.Buffered(1)),
            pl.BlockSpec((tokens, wide), lambda n: (0, n)),
            pl.BlockSpec(memory_space=pltpu.VMEM),
            pl.BlockSpec(memory_space=pltpu.VMEM),
        ],
        out_specs=[pl.BlockSpec(memory_space=pltpu.VMEM)] * 2,
        out_shape=[
            jax.ShapeDtypeStruct((rows, total_columns), jnp.float32),
            jax.ShapeDtypeStruct(tile.shape, jnp.float32),
        ],
        scratch_shapes=[pltpu.VMEM((width, tokens), jnp.bfloat16), pltpu.VMEM((*sizes, rows, total_columns), jnp.bfloat16)]
        + [s for i, s in enumerate(scatter_scratch(sizes, rows, total_columns, len(chunks))) if i not in (0, 5)]
        + [pltpu.VMEM((size, 8, PAIR), jnp.float32) for size in sizes]
        + [pltpu.SemaphoreType.DMA((4, max(sizes)))] * 2,
        compiler_params=pltpu.CompilerParams(
            collective_id=collective_id, has_side_effects=True, vmem_limit_bytes=58 * MB
        ),
        cost_estimate=cost(2 * tokens * width * columns, 2 * (tokens + width) * columns),
        name="embed_grad",
    )(left, onehot, norms.reshape(*sizes, rows, PAIR), tile)
    return table_own, [totals[i, 0] for i in range(len(values))]


def grid_sizes():
    cores = 2
    across = lax.axis_size("seq") // cores
    return lax.axis_size("dp") // across, across, across, cores


def column_chunks(columns, count):
    lanes = columns // PAIR
    widths = [(lanes // count + (i < lanes % count)) * PAIR for i in range(count)]
    starts = [sum(widths[:i]) for i in range(count)]
    return [pl.ds(start, wide) for start, wide in zip(starts, widths)]


class Place:
    def __init__(self, sizes):
        self.sizes = dict(zip("zyxc", sizes))
        dp, seq = lax.axis_index("dp"), lax.axis_index("seq")
        self.at = {
            "z": dp // sizes[1],
            "y": lax.rem(dp, sizes[1]),
            "x": seq // sizes[3],
            "c": lax.rem(seq, sizes[3]),
        }

    def other(self, axis, step):
        return lax.rem(self.at[axis] + step, self.sizes[axis])

    def device(self, axis, step):
        at = dict(self.at)
        at[axis] = self.other(axis, step)
        return (at["z"] * self.sizes["y"] + at["y"], at["x"] * self.sizes["c"] + at["c"])

    def steps(self, axis):
        return range(1, self.sizes[axis])

    def greet(self):
        barrier = pltpu.get_barrier_semaphore()
        peers = 0
        for axis in "cxyz":
            for step in self.steps(axis):
                pl.semaphore_signal(barrier, inc=1, device_id=self.device(axis, step), device_id_type=MESH)
                peers += 1
        pl.semaphore_wait(barrier, peers)


class Scatter:
    def __init__(self, sizes, chunks, g_ref, out_ref, own, one, two, three, four, *sems):
        self.sizes, self.chunks, self.place = sizes, chunks, Place(sizes)
        self.g_ref, self.out_ref = g_ref, out_ref
        self.own, self.one, self.two, self.three, self.four = own, one, two, three, four
        self.load_sem, self.send_sem, self.recv_sem = ([None] * 3 + list(sems))[-3:]
        self.most = max(sizes[1:3])
        self.ticks = (len(chunks) + 1) // 2 + 3

    def load(self, chunk):
        at = self.place.at
        cols = self.chunks[chunk]
        return pltpu.make_async_copy(
            self.g_ref.at[:, :, :, at["c"], :, cols], self.own.at[:, :, :, :, cols], self.load_sem.at[chunk]
        )

    def copies(self, chunk, stage):
        place, cols = self.place, self.chunks[chunk]
        out = []

        def add(src, dst, slot, axis, step):
            out.append(pltpu.make_async_remote_copy(
                src_ref=src, dst_ref=dst, send_sem=self.send_sem.at[chunk, slot],
                recv_sem=self.recv_sem.at[chunk, slot], device_id=place.device(axis, step), device_id_type=MESH))

        if stage == 0:
            add(self.g_ref.at[:, :, :, place.other("c", 1), :, cols], self.one.at[:, :, :, :, cols], 0, "c", 1)
        if stage == 1:
            axis = "xy"[chunk % 2]
            for step in place.steps(axis):
                spot = place.other(axis, step)
                src = self.one.at[:, :, spot, :, cols] if axis == "x" else self.one.at[:, spot, :, :, cols]
                add(src, self.two.at[step - 1, :, :, :, cols], step, axis, step)
        if stage == 2:
            axis = "yx"[chunk % 2]
            for step in place.steps(axis):
                src = self.two.at[0, :, place.other(axis, step), :, cols]
                add(src, self.three.at[step - 1, :, :, cols], self.most - 1 + step, axis, step)
        if stage == 3:
            for step in place.steps("z"):
                src = self.three.at[0, place.other("z", step), :, cols]
                add(src, self.four.at[step - 1, :, cols], 2 * (self.most - 1) + step, "z", step)
        return out

    def begin(self):
        self.place.greet()
        for chunk in range(len(self.chunks)):
            self.load(chunk).start()
            self.send(chunk, 0)

    def send(self, chunk, stage):
        for copy in self.copies(chunk, stage):
            copy.start()

    def advance(self, chunk, stage):
        n_z, n_y, n_x, n_c = self.sizes
        place, cols, f32, low = self.place, self.chunks[chunk], jnp.float32, jnp.bfloat16
        at = place.at
        own, one, two, three, four = self.own, self.one, self.two, self.three, self.four
        if stage == 0 and own is not None:
            self.load(chunk).wait()
        for copy in self.copies(chunk, stage):
            copy.wait_recv()
        if stage == 0:

            def add(i, carry):
                z, rest = i // (n_y * n_x), lax.rem(i, n_y * n_x)
                y, x = rest // n_x, lax.rem(rest, n_x)
                mine = self.g_ref[z, y, x, at["c"], :, cols] if own is None else own[z, y, x, :, cols]
                total = mine.astype(f32) + one[z, y, x, :, cols].astype(f32)
                one[z, y, x, :, cols] = total.astype(low)
                return carry

            lax.fori_loop(0, n_z * n_y * n_x, add, 0)
        if stage == 1:
            axis = "xy"[chunk % 2]
            kept = n_y if axis == "x" else n_x

            def add(i, carry):
                z, k = i // kept, lax.rem(i, kept)
                mine = one[z, k, at["x"], :, cols] if axis == "x" else one[z, at["y"], k, :, cols]
                total = mine.astype(f32)
                for step in place.steps(axis):
                    total = total + two[step - 1, z, k, :, cols].astype(f32)
                two[0, z, k, :, cols] = total.astype(low)
                return carry

            lax.fori_loop(0, n_z * kept, add, 0)
        if stage == 2:
            axis = "yx"[chunk % 2]

            def add(z, carry):
                total = two[0, z, at[axis], :, cols].astype(f32)
                for step in place.steps(axis):
                    total = total + three[step - 1, z, :, cols].astype(f32)
                three[0, z, :, cols] = total.astype(low)
                return carry

            lax.fori_loop(0, n_z, add, 0)
        if stage == 3:
            total = three[0, at["z"], :, cols].astype(f32)
            for step in place.steps("z"):
                total = total + four[step - 1, :, cols].astype(f32)
            self.out_ref[:, cols] = total
            return
        self.send(chunk, stage + 1)

    def tick(self, number):
        for stage in range(4):
            for chunk in (2 * (number - stage), 2 * (number - stage) + 1):
                if 0 <= number - stage and chunk < len(self.chunks):
                    self.advance(chunk, stage)

    def end(self):
        for chunk in range(len(self.chunks)):
            for stage in range(4):
                for copy in self.copies(chunk, stage):
                    copy.wait_send()


def scatter_scratch(sizes, rows, columns, count):
    n_z, n_y, n_x, n_c = sizes
    most = max(n_x, n_y)
    slots = 1 + 2 * (most - 1) + n_z - 1
    low = jnp.bfloat16
    return [
        pltpu.VMEM((n_z, n_y, n_x, rows, columns), low),
        pltpu.VMEM((n_z, n_y, n_x, rows, columns), low),
        pltpu.VMEM((most - 1, n_z, most, rows, columns), low),
        pltpu.VMEM((most - 1, n_z, rows, columns), low),
        pltpu.VMEM((n_z - 1, rows, columns), low),
        pltpu.SemaphoreType.DMA((count,)),
        pltpu.SemaphoreType.DMA((count, slots)),
        pltpu.SemaphoreType.DMA((count, slots)),
    ]


def total_steps(place, value, slots, send_sem, recv_sem):
    started = []
    for turn_at, axis in enumerate("cxyz"):
        held, me = slots[axis], place.at[axis]
        held[me] = value
        arriving = []
        for step in place.steps(axis):
            copy = pltpu.make_async_remote_copy(
                src_ref=held.at[me], dst_ref=held.at[me],
                send_sem=send_sem.at[turn_at, step], recv_sem=recv_sem.at[turn_at, step],
                device_id=place.device(axis, step), device_id_type=MESH)
            copy.start()
            arriving.append(copy)
        for copy in arriving:
            copy.wait_recv()
        started += arriving
        value = held[0]
        for spot in range(1, place.sizes[axis]):
            value = value + held[spot]
    return value, started


def gather_kernel(sizes, pieces, *refs):
    load_sem, send_sem, recv_sem = refs[-3:]
    arrays = (len(refs) - 3) // 2
    n_z, n_y, n_x, n_c = sizes
    place = Place(sizes)
    at = place.at
    started = []
    waits = {}
    most = max(n_x, n_y)

    def send(ref, chunk, slot, axis, step):
        copy = pltpu.make_async_remote_copy(
            src_ref=ref, dst_ref=ref, send_sem=send_sem.at[chunk, slot], recv_sem=recv_sem.at[chunk, slot],
            device_id=place.device(axis, step), device_id_type=MESH)
        copy.start()
        started.append(copy)
        return copy

    loads = []
    for chunk, (array, cols) in enumerate(pieces):
        load = pltpu.make_async_copy(
            refs[array].at[:, cols], refs[arrays + array].at[at["z"], at["y"], at["x"], at["c"], :, cols], load_sem.at[chunk])
        load.start()
        loads.append(load)
    place.greet()

    def first(chunk, out_ref, cols):
        loads[chunk].wait()
        ref = out_ref.at[at["z"], at["y"], at["x"], at["c"], :, cols]
        waits[chunk, 0] = [send(ref, chunk, step - 1, "z", step) for step in place.steps("z")]

    def second(chunk, out_ref, cols):
        for copy in waits[chunk, 0]:
            copy.wait_recv()
        axis = "xy"[chunk % 2]
        ref = out_ref.at[:, at["y"], at["x"], at["c"], :, cols]
        waits[chunk, 1] = [send(ref, chunk, n_z - 2 + step, axis, step) for step in place.steps(axis)]

    def third(chunk, out_ref, cols):
        for copy in waits[chunk, 1]:
            copy.wait_recv()
        axis = "yx"[chunk % 2]
        if axis == "y":
            ref = out_ref.at[:, at["y"], :, at["c"], :, cols]
        else:
            ref = out_ref.at[:, :, at["x"], at["c"], :, cols]
        waits[chunk, 2] = [send(ref, chunk, n_z - 2 + most - 1 + step, axis, step) for step in place.steps(axis)]

    def fourth(chunk, out_ref, cols):
        for copy in waits[chunk, 2]:
            copy.wait_recv()
        ref = out_ref.at[:, :, :, at["c"], :, cols]
        waits[chunk, 3] = [send(ref, chunk, n_z - 2 + 2 * (most - 1) + 1, "c", 1)]

    pairs = (len(pieces) + 1) // 2
    for tick in range(pairs + 3):
        for late, stage in enumerate((first, second, third, fourth)):
            for chunk in (2 * (tick - late), 2 * (tick - late) + 1):
                if 0 <= tick - late and chunk < len(pieces):
                    array, cols = pieces[chunk]
                    stage(chunk, refs[arrays + array], cols)
    for chunk in range(len(pieces)):
        for copy in waits[chunk, 3]:
            copy.wait_recv()
    for copy in started:
        copy.wait_send()


def gather_rows(arrays, counts, collective_id):
    sizes = grid_sizes()
    n_z, n_y, n_x, n_c = sizes
    slots = n_z - 1 + 2 * (max(n_x, n_y) - 1) + 1
    pieces = [
        (i, cols)
        for i, (array, count) in enumerate(zip(arrays, counts))
        for cols in column_chunks(array.shape[1], count)
    ]
    outs = pl.pallas_call(
        functools.partial(gather_kernel, sizes, pieces),
        in_specs=[pl.BlockSpec(memory_space=pl.ANY)] * len(arrays),
        out_specs=[pl.BlockSpec(memory_space=pl.ANY)] * len(arrays),
        out_shape=[jax.ShapeDtypeStruct(sizes + array.shape, array.dtype) for array in arrays],
        scratch_shapes=[
            pltpu.SemaphoreType.DMA((len(pieces),)),
            pltpu.SemaphoreType.DMA((len(pieces), slots)),
            pltpu.SemaphoreType.DMA((len(pieces), slots)),
        ],
        compiler_params=pltpu.CompilerParams(collective_id=collective_id, has_side_effects=True),
        name="gather_rows",
    )(*arrays)
    devices = n_z * n_y * n_x * n_c
    return [out.reshape(devices * array.shape[0], -1) for out, array in zip(outs, arrays)]


from jax.sharding import PartitionSpec as P

AXES = ("dp", "seq")
beta_one = 0.9
beta_two = 0.999
adam_eps = 1e-08
weight_decay = 0.01
learn_rate = 0.02
norm_rate = 0.2
ema_decay = 0.7


def project_kernel(roped, x_ref, w_ref, cos_ref, sin_ref, out_ref):
    product = jnp.dot(x_ref[...], w_ref[...], preferred_element_type=jnp.float32)
    for part in range(product.shape[1] // PAIR):
        piece = product[:, part * PAIR : (part + 1) * PAIR]
        if roped == "all":
            piece = turn(piece, cos_ref[...], sin_ref[...]).astype(jnp.bfloat16)
            piece = piece * jnp.bfloat16(HEAD_DIM**-0.5)
        elif part % 2 == 0:
            piece = turn(piece, cos_ref[...], sin_ref[...])
        out_ref[:, part * PAIR : (part + 1) * PAIR] = piece.astype(jnp.bfloat16)


def project(x, weights, first_column, columns, rope, tile, roped):
    tokens, width = x.shape
    wide = 512
    repeat = rope[0].shape[0] // tile
    return pl.pallas_call(
        functools.partial(project_kernel, roped),
        grid=(tokens // tile, columns // wide),
        in_specs=[
            pl.BlockSpec((tile, width), lambda m, n: (m, 0)),
            pl.BlockSpec((width, wide), lambda m, n: (0, n + first_column // wide)),
            pl.BlockSpec((tile, PAIR), lambda m, n: (lax.rem(m, repeat), 0)),
            pl.BlockSpec((tile, PAIR), lambda m, n: (lax.rem(m, repeat), 0)),
        ],
        out_specs=pl.BlockSpec((tile, wide), lambda m, n: (m, n)),
        out_shape=jax.ShapeDtypeStruct((tokens, columns), jnp.bfloat16),
        compiler_params=pltpu.CompilerParams(vmem_limit_bytes=40 * MB),
        cost_estimate=pl.CostEstimate(
            flops=2 * tokens * width * columns,
            bytes_accessed=2 * (tokens * width + width * columns + tokens * columns),
            transcendentals=0,
        ),
        name="project",
    )(x, weights, *rope)


def rope_tables(positions):
    half = HEAD_DIM // 2
    inverse = 10000.0 ** (-jnp.arange(half).astype(jnp.float32) / half)
    angles = positions.astype(jnp.float32)[:, None] * inverse[None, :]
    copies = PAIR // half
    return (jnp.tile(jnp.cos(angles), (1, copies)), jnp.tile(jnp.sin(angles), (1, copies)))


def norm_forward(values, gain, shift):
    centre = values - jnp.mean(values, axis=-1, keepdims=True)
    spread = jnp.mean(centre * centre, axis=-1, keepdims=True)
    scale = lax.rsqrt(spread + norm_eps)
    unit = centre * scale
    return (unit * gain + shift).astype(jnp.bfloat16), unit, scale


def norm_backward(grad, unit, scale, gain):
    grad_gain = jnp.sum(grad * unit, axis=0)
    grad_shift = jnp.sum(grad, axis=0)
    scaled = grad * gain
    inner = jnp.mean(scaled * unit, axis=-1, keepdims=True)
    outer = jnp.mean(scaled, axis=-1, keepdims=True)
    return scale * (scaled - outer - unit * inner), grad_gain, grad_shift


def product(left, right, left_dim=1, right_dim=0, precision=None):
    return lax.dot_general(
        left, right, dims(left_dim, right_dim), precision=precision,
        preferred_element_type=jnp.float32,
    )


def pair_columns(weights):
    rows, columns = weights.shape
    width = columns // 2
    return weights.reshape(rows, 2, width // PAIR, PAIR).transpose(0, 2, 1, 3).reshape(rows, columns)


def unpair_columns(weights):
    rows, columns = weights.shape
    width = columns // 2
    return weights.reshape(rows, width // PAIR, 2, PAIR).transpose(0, 2, 1, 3).reshape(rows, columns)


def most_lanes(columns, most):
    return max(PAIR * i for i in range(1, most + 1) if columns % (PAIR * i) == 0)


def on_device(
    token_ids,
    mask_rows,
    mask_labels,
    mask_counts,
    step_count,
    vocab_tables,
    attention,
    feed_in,
    feed_out,
    norm_params,
    first_tables,
    first_attention,
    first_feed_in,
    first_feed_out,
    first_norms,
    second_tables,
    second_attention,
    second_feed_in,
    second_feed_out,
    second_norms,
    ema_tables,
    ema_attention,
    ema_feed_in,
    ema_feed_out,
    ema_norms,
):
    master = (vocab_tables, attention, feed_in, feed_out, norm_params)
    firsts = (first_tables, first_attention, first_feed_in, first_feed_out, first_norms)
    seconds = (second_tables, second_attention, second_feed_in, second_feed_out, second_norms)
    averages = (ema_tables, ema_attention, ema_feed_in, ema_feed_out, ema_norms)
    group_rates = (learn_rate, learn_rate, learn_rate, learn_rate, norm_rate)
    low = jnp.bfloat16

    shards = lax.axis_size("seq")
    devices = shards * lax.axis_size("dp")
    windows, span = token_ids.shape
    slots = mask_rows.shape[1]
    vocab = vocab_tables.shape[2]
    padded = vocab + -vocab % PAIR
    rows, columns = attention.shape
    width = columns // 4
    hidden_width = feed_in.shape[1] // 2
    folds = feed_out.shape[0] // rows
    length = span * shards
    spot = lax.axis_index("seq")

    tables_sent = jnp.pad(vocab_tables, ((0, 0), (0, 0), (0, padded - vocab)))
    table_sent = tables_sent[0].astype(low)
    attn_sent = jnp.concatenate(
        [
            attention[:, :width],
            pair_columns(attention[:, width : 3 * width]),
            attention[:, 3 * width :],
        ],
        axis=1,
    ).astype(low)
    in_sent = feed_in.reshape(rows, 2, hidden_width // folds, folds).transpose(0, 1, 3, 2)
    late_sent = jnp.concatenate(
        [
            in_sent.reshape(rows, 2 * hidden_width),
            feed_out.reshape(rows, folds * width),
            tables_sent[1],
        ],
        axis=1,
    ).astype(low)

    small = jnp.concatenate(
        [
            token_ids.reshape(-1).astype(jnp.float32),
            mask_rows.reshape(-1).astype(jnp.float32),
            mask_labels.reshape(-1).astype(jnp.float32),
            mask_counts.reshape(-1).astype(jnp.float32),
            norm_params.astype(low).astype(jnp.float32).reshape(-1),
        ]
    )
    small = jnp.pad(small, (0, -small.shape[0] % (8 * PAIR))).reshape(8, -1)
    small_all, table = gather_rows((small, table_sent), (1, 11), 3)
    late_sent, attn_sent, small_all, table = lax.optimization_barrier(
        (late_sent, attn_sent, small_all, table)
    )
    late = lax.all_gather(late_sent, AXES, axis=0, tiled=True)
    (attn,) = gather_rows((attn_sent,), (10,), 5)
    small_all = small_all.reshape(devices, -1)
    out_w = attn[:, 3 * width :]
    head_w = late[:, 2 * hidden_width + folds * width :]
    cuts = [windows * span, windows * slots, windows * slots, windows]
    marks = [sum(cuts[:i]) for i in range(len(cuts) + 1)]
    gains = small_all[:, marks[4] : marks[4] + rows * 6].reshape(devices * rows, 6)
    count = jnp.sum(small_all[:, marks[3] : marks[4]])
    group = lax.dynamic_slice_in_dim(small_all, lax.axis_index("dp") * shards, shards, axis=0)

    def in_order(first, last):
        piece = group[:, first:last].reshape(shards, windows, -1)
        return piece.transpose(1, 0, 2).reshape(windows * shards, -1)

    ids = in_order(marks[0], marks[1]).astype(jnp.int32)
    block = spot * windows + jnp.arange(windows, dtype=jnp.int32)

    def mine(first, last):
        return lax.dynamic_slice_in_dim(in_order(first, last), spot * windows, windows, axis=0)

    own_rows = mine(marks[1], marks[2]).astype(jnp.int32)
    own_labels = mine(marks[2], marks[3]).astype(jnp.int32).reshape(-1)
    own_counts = mine(marks[3], marks[4])
    live = (jnp.arange(slots, dtype=jnp.float32)[None, :] < own_counts).astype(jnp.float32)
    live = live.reshape(-1)

    base = first_window(spot * windows, shards, windows)
    wins = block // shards - base
    offset = (spot * windows - base * shards) * span
    ids_two = lax.dynamic_slice_in_dim(ids, base * shards, 2 * shards, axis=0).reshape(-1)
    positions = ((block % shards)[:, None] * span + jnp.arange(span, dtype=jnp.int32)).reshape(-1)
    rope_q = rope_tables(positions)
    rope_k = rope_tables(jnp.arange(length, dtype=jnp.int32))
    tokens = windows * span

    def own(values):
        return lax.dynamic_slice_in_dim(values, offset, tokens, axis=0)

    embedded_two, onehot, normed_one, stats = embed(
        ids_two[:, None], table, 0, padded, gains[:, 0][None], gains[:, 1][None], length // 2
    )
    normed_own = own(normed_one)
    queries = project(normed_own, attn, 0, width, rope_q, tokens, "all")
    key_values = project(normed_one, attn, width, 2 * width, rope_k, length, "half")
    mixture, totals = attend_forward(wins, queries, key_values, span, length)
    after_attn = own(embedded_two) + product(mixture, out_w)

    normed_two, unit_two, scale_two = norm_forward(after_attn, gains[:, 2], gains[:, 3])
    gate, up, hidden = gate_forward(normed_two, late, hidden_width)
    after_feed = down_forward(hidden, late, after_attn, 2 * hidden_width)

    pick = (own_rows[:, :, None] == jnp.arange(span, dtype=jnp.int32)).astype(jnp.float32)
    selected = jnp.einsum(
        "wsp,wpd->wsd", pick, after_feed.reshape(windows, span, width),
        precision=lax.Precision.HIGHEST, preferred_element_type=jnp.float32,
    ).reshape(windows * slots, width)
    normed_final, unit_final, scale_final = norm_forward(selected, gains[:, 4], gains[:, 5])
    column = jnp.arange(padded, dtype=jnp.int32)[None, :]
    logits = jnp.where(column < vocab, product(normed_final, head_w), -jnp.inf)
    log_total = jax.nn.logsumexp(logits, axis=-1)
    wanted = own_labels[:, None] == column
    picked = jnp.sum(jnp.where(wanted, logits, 0.0), axis=-1)
    loss_part = jnp.sum(live * (log_total - picked))

    grad_logits = (
        (jnp.exp(logits - log_total[:, None]) - wanted.astype(jnp.float32)) * (live / count)[:, None]
    ).astype(low)
    grad_selected, grad_gain_final, grad_shift_final = norm_backward(
        product(grad_logits, head_w, 1, 1), unit_final, scale_final, gains[:, 4]
    )
    grad_after_feed = jnp.einsum(
        "wsp,wsd->wpd", pick, grad_selected.reshape(windows, slots, width),
        precision=lax.Precision.HIGHEST, preferred_element_type=jnp.float32,
    ).reshape(tokens, width)
    rounded_feed = grad_after_feed.astype(low)
    order = (lax.axis_size("dp"), shards)
    spare = ((0, -grad_logits.shape[0] % PAIR), (0, 0))
    late_grads = weight_grad(
        jnp.pad(normed_final, spare), (jnp.pad(grad_logits, spare),), order, most_lanes(padded, 11),
        padded + folds * width,
    )
    late_grads = down_grad(hidden, rounded_feed, late_grads, padded, order)
    rounded_feed, late_grads = lax.optimization_barrier((rounded_feed, late_grads))
    late_part = lax.psum_scatter(late_grads, "seq", scatter_dimension=0, tiled=True)
    grad_gate, grad_up = gate_backward(rounded_feed, late, gate, up, 2 * hidden_width)
    alone = (1, 1)
    in_grads = weight_grad(normed_two, (grad_gate, grad_up), alone)

    grad_inner, grad_gain_two, grad_shift_two = norm_backward(
        input_grad((grad_gate, grad_up), late, (0, hidden_width)), unit_two, scale_two, gains[:, 2]
    )
    grad_after_attn = grad_after_feed + grad_inner
    rounded_attn = grad_after_attn.astype(low)
    grad_mixture = product(rounded_attn, out_w, 1, 1).astype(low)
    grad_queries, grad_pairs, in_own = attend_backward(
        queries, key_values, grad_mixture, totals, rope_q, rope_k, in_grads, span, length, 2
    )
    grad_queries, late_part = lax.optimization_barrier((grad_queries, late_part))
    late_own = lax.psum_scatter(late_part, "dp", scatter_dimension=0, tiled=True)
    attn_grads = weight_grad(mixture, (rounded_attn,), alone, width // 2, columns, None, 3 * width)
    attn_grads = weight_grad(normed_own, (grad_queries,), alone, width // 2, None, attn_grads)
    attn_grads = weight_grad(normed_one, (grad_pairs,), alone, width // 2, None, attn_grads, width)
    grad_embedded, sums_one, attn_own = normed_grad(
        grad_pairs, grad_queries, attn, embedded_two, stats, grad_after_attn, gains[:, 0][None], attn_grads, shards,
        windows, span, 4,
    )
    grad_gain_one, grad_shift_one = sums_one[0], sums_one[1]
    grad_norms = jnp.stack(
        [
            grad_gain_one,
            grad_shift_one,
            grad_gain_two,
            grad_shift_two,
            grad_gain_final,
            grad_shift_final,
        ],
        axis=1,
    )
    grad_norms = jnp.pad(grad_norms, ((0, 0), (0, PAIR - grad_norms.shape[1]))).astype(low)
    late_own = late_own.astype(jnp.float32)
    squares = jnp.sum(late_own * late_own) + jnp.sum(in_own * in_own) + jnp.sum(attn_own * attn_own)
    late_final = (
        late_own[:, :vocab],
        in_own.reshape(rows, 2, folds, hidden_width // folds).transpose(0, 1, 3, 2).reshape(rows, 2 * hidden_width),
        late_own[:, padded:].reshape(rows * folds, width),
        jnp.concatenate(
            [
                attn_own[:, :width],
                unpair_columns(attn_own[:, width : 3 * width]),
                attn_own[:, 3 * width :],
            ],
            axis=1,
        ),
    )
    grad_embedded, (head_own, in_own, down_own, attn_own) = lax.optimization_barrier((grad_embedded, late_final))
    table_own, (squares_all, loss_all) = embed_grad(
        grad_embedded, onehot, grad_norms, (squares, loss_part), most_lanes(padded, 4), 1
    )
    grads = (
        jnp.stack([table_own[:, :vocab], head_own], axis=0),
        attn_own,
        in_own,
        down_own,
        table_own[:, padded : padded + 6],
    )
    masked_loss = loss_all / count
    total_norm = jnp.sqrt(squares_all)
    limit = (slots * shards * windows * lax.axis_size("dp")) ** (-0.5)
    clip = jnp.minimum(1.0, limit / (total_norm + 1e-06))
    steps = step_count[0].astype(jnp.float32)
    fix_one = 1.0 - beta_one**steps
    fix_two = 1.0 - beta_two**steps
    weights_new, firsts_new, seconds_new, averages_new = ([], [], [], [])
    for weight, grad, first, second, average, step_rate in zip(
        master, grads, firsts, seconds, averages, group_rates
    ):
        scaled = grad * clip
        first_next = beta_one * first + (1.0 - beta_one) * scaled
        second_next = beta_two * second + (1.0 - beta_two) * scaled * scaled
        update = (
            first_next / fix_one / (jnp.sqrt(second_next / fix_two) + adam_eps)
            + weight_decay * weight
        )
        weight_next = weight - step_rate * update
        weights_new.append(weight_next)
        firsts_new.append(first_next)
        seconds_new.append(second_next)
        averages_new.append(ema_decay * average + (1.0 - ema_decay) * weight_next)
    return (masked_loss, total_norm, *weights_new, *firsts_new, *seconds_new, *averages_new)


def solution(mesh):
    split = P(AXES, None)
    tables = P(None, AXES, None)
    weights = (tables, split, split, split, split)
    return jax.shard_map(
        on_device,
        mesh=mesh,
        in_specs=(P("dp", "seq"),) * 4 + (P(),) + weights * 4,
        out_specs=(P(), P()) + weights * 4,
        check_vma=False,
    )
```
